256 devices in a mesh: grp: 4 (over x), row: 64 (over y, z, core).
Axes of the slice: x: 4, y: 4, z: 8, core: 2. Of those that a mesh axis runs over, the one named last changes fastest.
Arguments:
- serving: bfloat16 [131072, 128], P('row'), may hold values from -1 to 1
- serving_scale: bfloat16 [1024], P('row'), may hold values from 0.099609375 to 1
- hot_blocks: int32 [4, 128], P('grp', 'row'), may hold values from 0 to 15, as said below
- bag_lengths: int32 [256, 256], P(('grp', 'row')), may hold values from 1 to 16, 1024 in all within a row
- bag_indices: int32 [256, 1024], P(('grp', 'row')), may hold values from 0 to 16383, as said below
- dense_act: bfloat16 [65536, 128], P(('grp', 'row')), may hold values from -6 to 6
- labels: float32 [65536], P(('grp', 'row')), may hold values from 0 to 1
- w_top: bfloat16 [256, 1024], replicated, may hold values from -0.375 to 0.375
- w_out: float32 [1024], replicated, may hold values from -0.012 to 0.012
- master: float32 [4, 32768, 128], P('grp', 'row'), may hold values from -0.3 to 0.3
- accum: float32 [4, 32768], P('grp', 'row'), may hold values from 1e-05 to 0.0001
Outputs:
- new_master: float32 [4, 32768, 128], P('grp', 'row')
- new_accum: float32 [4, 32768], P('grp', 'row')
- new_serving: bfloat16 [131072, 128], P('row')
- new_scale: bfloat16 [1024], P('row')
- top_grad: float32 [256, 1024], replicated
The draws below stay inside these ranges and needn't reach their ends.
Inputs may be any that keep to these rules, and one draw needn't show every extreme that they name: `hot_blocks`: the 2 entries that one group names in one row shard are distinct. `bag_indices`: in each device's line, exactly 8 distinct values lie in each range of 256 consecutive positions that starts at a multiple of 256.
All inputs are finite; a program needn't handle non-finite values. Where the reference program divides by a largest or mean magnitude, that divisor is 1e-20 or more.
Results may differ from the reference program's by a relative error of at most 0.012.
Values may be sent and summed in bfloat16 or wider, within the bound.
No kernel may reach another device: no remote copies, remote signals or barrier semaphores. Data moves between devices by JAX's collectives and lax.ppermute only.
A program may use at most 128 MiB of HBM per device.

```python
import math
import jax
import jax.numpy as jnp
import numpy as np
from jax import lax

D = 128
DENSE_W = 128
FF = 1024
BLOCK = 128
BLK_DEV = 16
HOT_DEV = 2
BAGS_DEV = 256
MOST = 16
NNZ_DEV = 1024
CAP = 8
ROWS = 131072
HOTROWS = 16384
BAGS = 65536
N_GRP = 4
N_ROW = 64
DEVICES = 256


def draw_hot_blocks(key, part):
    keys = jax.random.split(jax.random.fold_in(key, 11), N_GRP * N_ROW)
    picks = jax.vmap(lambda one: jax.random.permutation(one, BLK_DEV)[:HOT_DEV])(keys)
    return picks.reshape(N_GRP, N_ROW * HOT_DEV).astype(jnp.int32)


def draw_bag_indices(key, part):
    span = HOT_DEV * BLOCK
    base = N_ROW * CAP

    def one_device(device_key):
        keys = jax.random.split(device_key, N_ROW + 4)
        picks = jax.vmap(lambda one: jax.random.permutation(one, span)[:CAP])(keys[:N_ROW])
        offsets = (jnp.arange(N_ROW, dtype=jnp.int32) * span)[:, None]
        candidates = (picks.astype(jnp.int32) + offsets).reshape(base)
        candidates = jax.random.permutation(keys[N_ROW], candidates)
        first_pick = jax.random.randint(keys[N_ROW + 1], (NNZ_DEV - base,), 0, base)
        second_pick = jax.random.randint(keys[N_ROW + 2], (NNZ_DEV - base,), 0, base)
        repeats = candidates[jnp.minimum(first_pick, second_pick)]
        return jax.random.permutation(keys[N_ROW + 3], jnp.concatenate([candidates, repeats])).astype(jnp.int32)
    device_keys = jax.random.split(jax.random.fold_in(key, 23), DEVICES)
    return jax.vmap(one_device)(device_keys)


def level_of(rng, extent, cuts, smallest, largest):
    def one(axis_at, shards_of):
        draws = jax.random.uniform(jax.random.fold_in(jax.random.fold_in(rng, 6), axis_at), (shards_of,), jnp.float32, smallest / len(cuts), largest / len(cuts))
        return jnp.repeat(jnp.exp(draws), extent[axis_at] // shards_of).reshape((-1,) + (1,) * (len(extent) - axis_at - 1))

    level = one(*cuts[0])
    for cut in cuts[1:]:
        level = level * one(*cut)
    return level


def split_up(number_of, total, bound, lean):
    portions = [(1 << 20) // math.isqrt(rank ** lean) + 1 for rank in range(2, number_of + 1)]
    surplus, counts = total - bound - (number_of - 1), [1] * (number_of - 1)
    while surplus > 0:
        movable = [i for i in range(number_of - 1) if counts[i] < bound]
        pool, left = sum([portions[i] for i in movable]), surplus
        for i in movable:
            more = min(bound - counts[i], max(1, left * portions[i] // pool), surplus)
            counts[i] = counts[i] + more
            surplus = surplus - more
    return np.array([bound] + counts)


def ragged(key, number_of, total, reach, skew):
    if number_of == 2:
        one = jax.random.randint(key, (), max(1, total - reach), min(reach, total - 1) + 1)
        return jnp.stack([one, total - one])
    tallies = jnp.asarray(split_up(number_of, total, reach, skew), jnp.int32)
    twos = (number_of - 1) // 2
    giver, sink = tallies[1:1 + 2 * twos:2], tallies[2:2 + 2 * twos:2]
    slack = jnp.minimum(giver - 1, reach - sink)
    moved = jax.random.randint(jax.random.fold_in(key, 1), (twos,), 0, 1 << 20) % (slack + 1)
    tallies = tallies.at[1:1 + 2 * twos:2].set(giver - moved).at[2:2 + 2 * twos:2].set(sink + moved)
    return tallies[jax.random.permutation(jax.random.fold_in(key, 2), number_of)]


def centred(rng, extent, spread, most, cuts=(), kind=jnp.bfloat16):
    level = level_of(rng, extent, cuts, -0.22, 0.18) if cuts else 1.0
    result = jax.random.normal(rng, extent, jnp.float32) * spread * level
    return jnp.minimum(jnp.maximum(result, -most), most).astype(kind)


def setup_inputs(seed: int = 0) -> dict:
    key_list = jax.random.split(jax.random.key(seed), 12)
    serving = jnp.clip(jax.random.uniform(key_list[0], (ROWS, D), jnp.float32, -1.0, 1.0) * level_of(key_list[0], (ROWS, D), ((0, 64),), -0.4, 0.0), -1.0, 1.0).astype(jnp.bfloat16)
    serving_scale = jnp.clip(jnp.exp(math.log(1.0) - 2.306499 * jax.random.uniform(key_list[1], (ROWS // BLOCK,), jnp.float32) ** level_of(key_list[1], (ROWS // BLOCK,), ((0, 64),), -0.2, 0.2)), 0.099609375, 1.0).astype(jnp.bfloat16)
    hot_blocks = draw_hot_blocks(jax.random.fold_in(key_list[11], 71), 0)
    bag_lengths = jax.vmap(lambda own: ragged(own, BAGS_DEV, NNZ_DEV, MOST, 1))(jax.random.split(key_list[3], DEVICES)).reshape((DEVICES, BAGS_DEV)).astype(jnp.int32)
    bag_indices = draw_bag_indices(jax.random.fold_in(key_list[11], 71), 0)
    dense_act = centred(key_list[5], (BAGS, DENSE_W), 1.0, 6.0, ((0, 256),))
    labels = jnp.clip(1.0 * jax.random.uniform(key_list[6], (BAGS,), jnp.float32) ** level_of(key_list[6], (BAGS,), ((0, 256),), -0.2, 0.2), 0.0, 1.0)
    w_top = centred(key_list[7], (D + DENSE_W, FF), (D + DENSE_W) ** -0.5, 0.375)
    w_out = centred(key_list[8], (FF,), 0.002, 0.012, (), jnp.float32)
    master = centred(key_list[9], (N_GRP, ROWS // N_GRP, D), 0.05, 0.3, ((0, 4), (1, 64)), jnp.float32)
    accum = jnp.clip(jnp.exp(math.log(0.0001) - 2.3025851 * jax.random.uniform(key_list[10], (N_GRP, ROWS // N_GRP), jnp.float32) ** level_of(key_list[10], (N_GRP, ROWS // N_GRP), ((0, 4), (1, 64)), -0.2, 0.2)), 9.999999747378752e-06, 0.0001)
    return {"serving": serving, "serving_scale": serving_scale, "hot_blocks": hot_blocks, "bag_lengths": bag_lengths, "bag_indices": bag_indices, "dense_act": dense_act, "labels": labels, "w_top": w_top, "w_out": w_out, "master": master, "accum": accum}


lr_step = 0.05

def pool_grad(table, lengths, indices, dense_d, labels_d, w_top, w_out):
    ends = jnp.cumsum(lengths).astype(jnp.int32)
    starts = ends - lengths
    marks = jnp.zeros((indices.shape[0],), jnp.int32).at[starts].add(1)
    bag = (jnp.cumsum(marks) - 1).astype(jnp.int32)
    pooled = jax.ops.segment_sum(table[indices], bag, num_segments=lengths.shape[0])
    joined = jnp.concatenate([pooled.astype(jnp.bfloat16), dense_d], axis=1)
    pre = jnp.dot(joined, w_top, preferred_element_type=jnp.float32)
    sig = jax.nn.sigmoid(pre)
    logit = jnp.dot(pre * sig, w_out, precision=lax.Precision.HIGHEST)
    dlogit = jax.nn.sigmoid(logit) - labels_d
    dpre = (dlogit[:, None] * w_out[None, :] * (sig * (1.0 + pre * (1.0 - sig)))).astype(jnp.bfloat16)
    top = lax.dot_general(joined, dpre, (((0,), (0,)), ((), ())), preferred_element_type=jnp.float32)
    dz = lax.dot_general(dpre, w_top, (((1,), (1,)), ((), ())), preferred_element_type=jnp.float32)
    width = table.shape[1]
    hot = jax.ops.segment_sum(dz[:, :width][bag], indices, num_segments=table.shape[0])
    return (top, hot)

def reference(serving, serving_scale, hot_blocks, bag_lengths, bag_indices, dense_act, labels, w_top, w_out, master, accum):
    span = BLK_DEV * BLOCK
    quarter = span // N_GRP
    shard_of = jnp.arange(N_ROW * HOT_DEV, dtype=jnp.int32) // HOT_DEV * BLK_DEV
    block_ids = (shard_of[None, :] + hot_blocks).astype(jnp.int32)
    blocks = serving.reshape(N_ROW * BLK_DEV, BLOCK, D)
    tables = (blocks[block_ids].astype(jnp.float32) * serving_scale[block_ids].astype(jnp.float32)[..., None, None]).reshape(N_GRP, HOTROWS, D)
    dense = dense_act.reshape(DEVICES, BAGS_DEV, DENSE_W)
    label_rows = labels.reshape(DEVICES, BAGS_DEV)

    def one_device(carry, xs):
        top_sum, hot_sums = carry
        device, lengths, indices, dense_d, labels_d = xs
        group = (device // N_ROW).astype(jnp.int32)
        table = lax.dynamic_index_in_dim(tables, group, 0, keepdims=False)
        top, hot = pool_grad(table, lengths, indices, dense_d, labels_d, w_top, w_out)
        old = lax.dynamic_index_in_dim(hot_sums, group, 0, keepdims=True)
        hot_sums = lax.dynamic_update_index_in_dim(hot_sums, old + hot[None], group, 0)
        return ((top_sum + top, hot_sums), None)
    start = (jnp.zeros((D + DENSE_W, FF), jnp.float32), jnp.zeros((N_GRP, HOTROWS, D), jnp.float32))
    xs = (jnp.arange(DEVICES, dtype=jnp.int32), bag_lengths, bag_indices, dense, label_rows)
    (top_grad, hot_sums), _ = lax.scan(one_device, start, xs)
    row_grad = jnp.zeros((N_ROW * BLK_DEV, BLOCK, D), jnp.float32).at[block_ids.reshape(-1)].add(hot_sums.reshape(N_GRP * N_ROW * HOT_DEV, BLOCK, D))
    row_grad = row_grad.reshape(ROWS, D)
    table_master = master.reshape(N_GRP, N_ROW, quarter, D).transpose(1, 0, 2, 3).reshape(ROWS, D)
    table_accum = accum.reshape(N_GRP, N_ROW, quarter).transpose(1, 0, 2).reshape(ROWS)
    new_state = table_accum + lax.optimization_barrier(jnp.mean(row_grad * row_grad, axis=1))
    new_weights = table_master - lr_step * row_grad / jnp.sqrt(new_state)[:, None]
    scale_new = (lax.optimization_barrier(jnp.max(jnp.abs(new_weights.reshape(ROWS // BLOCK, BLOCK * D)), axis=1)) + 1e-06).astype(jnp.bfloat16)
    coded = (new_weights.reshape(ROWS // BLOCK, BLOCK, D) / scale_new.astype(jnp.float32)[:, None, None]).astype(jnp.bfloat16).reshape(ROWS, D)
    out_master = new_weights.reshape(N_ROW, N_GRP, quarter, D).transpose(1, 0, 2, 3).reshape(N_GRP, ROWS // N_GRP, D)
    out_accum = new_state.reshape(N_ROW, N_GRP, quarter).transpose(1, 0, 2).reshape(N_GRP, ROWS // N_GRP)
    return (out_master, out_accum, coded, scale_new, top_grad)
```

```python
import jax
import jax.numpy as jnp
from jax import lax
from jax.experimental import pallas as pl
from jax.experimental.pallas import tpu as pltpu
from jax.sharding import Mesh
from jax.sharding import PartitionSpec as P

ROW = ("row_0", "row_1", "row_2")
GRP_ROW = ("grp", "row_0", "row_1", "row_2")
N_GRP = 4
N_ROW = 64
BLOCK = 128
SPAN = 256
CAP = 8
BAGS = 256
NNZ = 1024
SLOTS = N_ROW * CAP
D = 128
FF = 1024
QUARTER = 512
LR = 0.05
F32 = jnp.float32
BF16 = jnp.bfloat16
I32 = jnp.int32
VM = pl.BlockSpec(memory_space=pltpu.VMEM)
SM = pl.BlockSpec(memory_space=pltpu.SMEM)


def iota(shape, dim):
    return lax.broadcasted_iota(I32, shape, dim)


def dot(a, b, ca=1, cb=0):
    return lax.dot_general(a, b, (((ca,), (cb,)), ((), ())), preferred_element_type=F32)


def ones_where(mask):
    return jnp.where(mask, 1.0, 0.0).astype(BF16)


def call(kernel, outs, specs, args, flops, name):
    bytes_accessed = sum(a.size * a.dtype.itemsize for a in args) + sum(
        o.size * o.dtype.itemsize for o in outs
    )
    return pl.pallas_call(
        kernel,
        out_shape=outs,
        in_specs=specs,
        out_specs=[VM] * len(outs),
        cost_estimate=pl.CostEstimate(
            flops=flops, bytes_accessed=bytes_accessed, transcendentals=0
        ),
        name=name,
    )(*args)


def shard_and_row(idx_ref):
    idx = idx_ref[...]
    shard = lax.shift_right_logical(idx, 8)
    return shard, idx & (SPAN - 1)


def ids_kernel(idx_ref, ids_ref, rank_ref):
    shard, row = shard_and_row(idx_ref)
    in_shard = ones_where(iota((N_ROW, NNZ), 0) == shard)
    at_row = ones_where(iota((SPAN, NNZ), 0) == row)
    used = dot(in_shard, at_row, 1, 1) > 0.5
    before = ones_where(iota((SPAN, SPAN), 0) < iota((SPAN, SPAN), 1))
    rank = dot(ones_where(used), before)
    column = iota((N_ROW, SPAN), 1).astype(F32)
    lane = iota((N_ROW, D), 1)
    ids = jnp.zeros((N_ROW, D), F32)
    for k in range(CAP):
        mine = jnp.sum(
            jnp.where(used & (rank == float(k)), column, 0.0), axis=1, keepdims=True
        )
        ids = jnp.where(lane == k, mine, ids)
    ids_ref[...] = ids.astype(I32)
    rank_ref[...] = rank.astype(BF16)


def counts_kernel(idx_ref, len_ref, rank_ref, use_ref, use_t_ref):
    shard, row = shard_and_row(idx_ref)
    in_shard = ones_where(iota((N_ROW, NNZ), 0) == shard)
    rank_at = dot(rank_ref[...], in_shard, 0, 0)
    rank = jnp.sum(jnp.where(iota((SPAN, NNZ), 0) == row, rank_at, 0.0), axis=0, keepdims=True)
    slot = shard * CAP + rank.astype(I32)
    at_slot = ones_where(iota((SLOTS, NNZ), 0) == slot)
    lengths = jnp.broadcast_to(len_ref[...].astype(F32), (BAGS, BAGS))
    a, b = iota((BAGS, BAGS), 0), iota((BAGS, BAGS), 1)
    starts = jnp.sum(jnp.where(b < a, lengths, 0.0), axis=1, keepdims=True).astype(I32)
    ends = jnp.sum(jnp.where(b <= a, lengths, 0.0), axis=1, keepdims=True).astype(I32)
    place = iota((BAGS, NNZ), 1)
    in_bag = ones_where((place >= starts) & (place < ends))
    use_ref[...] = dot(in_bag, at_slot, 1, 1).astype(BF16)
    use_t_ref[...] = dot(at_slot, in_bag, 1, 1).astype(BF16)


def table_kernel(hot_ref, serving_ref, scale_ref, table_ref, buf, sem):
    copies = [
        pltpu.make_async_copy(
            serving_ref.at[pl.ds(pl.multiple_of(hot_ref[0, j] * BLOCK, BLOCK), BLOCK)],
            buf.at[j],
            sem.at[j],
        )
        for j in range(2)
    ]
    for c in copies:
        c.start()
    scales = scale_ref[...].astype(F32)
    lane = iota(scales.shape, 1)
    for j, c in enumerate(copies):
        own = jnp.sum(jnp.where(lane == hot_ref[0, j], scales, 0.0), axis=1, keepdims=True)
        c.wait()
        table_ref[j * BLOCK : (j + 1) * BLOCK, :] = (buf[j].astype(F32) * own).astype(BF16)


def pick_kernel(ids_ref, table_ref, rows_ref):
    owner = ones_where(lax.shift_right_logical(iota((SLOTS, N_ROW), 0), 3) == iota((SLOTS, N_ROW), 1))
    spread = dot(owner, ids_ref[...].astype(F32).astype(BF16))
    mine = iota((SLOTS, D), 1) == (iota((SLOTS, D), 0) & (CAP - 1))
    column = jnp.sum(jnp.where(mine, spread, 0.0), axis=1, keepdims=True).astype(I32)
    onehot = ones_where(iota((SLOTS, SPAN), 1) == column)
    rows_ref[...] = dot(onehot, table_ref[...]).astype(BF16)


def place_kernel(ids_ref, place_ref):
    owner = ones_where(lax.shift_right_logical(iota((SLOTS, N_ROW), 0), 3) == iota((SLOTS, N_ROW), 1))
    spread = dot(ids_ref[...].astype(F32).astype(BF16), owner, 0, 1)
    mine = iota((D, SLOTS), 0) == (iota((D, SLOTS), 1) & (CAP - 1))
    line = jnp.sum(jnp.where(mine, spread, 0.0), axis=0, keepdims=True).astype(I32)
    place_ref[...] = ones_where(iota((SPAN, SLOTS), 0) == line)


def step_kernel(
    rows_ref, use_ref, use_t_ref, dense_ref, labels_ref, w_ref, w_out_ref, out_ref
):
    pooled = dot(use_ref[...], rows_ref[...]).astype(BF16)
    joined = jnp.concatenate([pooled, dense_ref[...]], axis=1)
    pre = dot(joined, w_ref[...])
    sig = jax.nn.sigmoid(pre)
    w_out = w_out_ref[...]
    logit = jnp.sum(pre * sig * w_out, axis=1, keepdims=True)
    a, b = iota((BAGS, BAGS), 0), iota((BAGS, BAGS), 1)
    labels = jnp.sum(
        jnp.where(a == b, jnp.broadcast_to(labels_ref[...], (BAGS, BAGS)), 0.0),
        axis=1,
        keepdims=True,
    )
    dlogit = jax.nn.sigmoid(logit) - labels
    dpre = (dlogit * w_out * (sig * (1.0 + pre * (1.0 - sig)))).astype(BF16)
    pooled_grad = dot(dpre, w_ref[0:D, :], 1, 1)
    high = pooled_grad.astype(BF16)
    low = (pooled_grad - high.astype(F32)).astype(BF16)
    use_t = use_t_ref[...]
    row_grad = dot(use_t, high) + dot(use_t, low)
    out_ref[:, 32:40, :] = row_grad.reshape(N_ROW, CAP, D).astype(BF16)
    top = dot(joined, dpre, 0, 0).astype(BF16)
    for i in range(16):
        for j in range(8):
            at = (j % 2) * 16
            out_ref[i * 4 + j // 2, at : at + 16, :] = top[
                i * 16 : (i + 1) * 16, j * 128 : (j + 1) * 128
            ]


def owned_kernel(got_ref, place_ref, hot_ref, out_ref):
    grads = got_ref[:, 32:40, :].astype(F32).reshape(SLOTS, D).astype(BF16)
    out_ref[0:SPAN, :] = dot(place_ref[...], grads).astype(BF16)
    out_ref[SPAN : SPAN + 32, :] = jnp.sum(got_ref[:, 0:32, :].astype(F32), axis=0).astype(BF16)
    lane = iota((16, D), 1)
    hot = jnp.where(lane == 0, hot_ref[0, 0], jnp.where(lane == 1, hot_ref[0, 1], 0))
    out_ref[SPAN + 32 : SPAN + 48, :] = hot.astype(F32).astype(BF16)


def update_kernel(
    me_ref, x0_ref, x1_ref, x2_ref, x3_ref, master_ref, accum_ref,
    new_master_ref, new_accum_ref, coded_ref, top_ref, by_group,
):
    me = me_ref[0]
    for o, ref in enumerate((x0_ref, x1_ref, x2_ref, x3_ref)):
        by_group[(me - o) & 3] = ref[...]
    top = jnp.zeros((32, D), F32)
    for g in range(N_GRP):
        top = top + by_group[g, SPAN : SPAN + 32, :].astype(F32)
    top_ref[...] = jnp.broadcast_to(top.astype(BF16)[None], (N_ROW, 32, D))
    hot = [by_group[g, SPAN + 32 : SPAN + 48, :].astype(F32)[0:1, :] for g in range(N_GRP)]
    a, b = iota((BLOCK, BLOCK), 0), iota((BLOCK, BLOCK), 1)
    diagonal = a == b
    lane = iota((16, D), 1)
    scale_row = jnp.zeros((16, D), F32)
    for q in range(4):
        grad = jnp.zeros((BLOCK, D), F32)
        number = (me * 4 + q).astype(F32)
        for g in range(N_GRP):
            for j in range(2):
                block = by_group[g, j * BLOCK : (j + 1) * BLOCK, :].astype(F32)
                grad = grad + jnp.where(hot[g][:, j : j + 1] == number, block, 0.0)
        at = pl.ds(q * BLOCK, BLOCK)
        accum = jnp.broadcast_to(accum_ref[:, q * BLOCK : (q + 1) * BLOCK], (BLOCK, BLOCK))
        state = jnp.sum(jnp.where(diagonal, accum, 0.0), axis=1, keepdims=True) + jnp.mean(
            grad * grad, axis=1, keepdims=True
        )
        new_accum_ref[:, q * BLOCK : (q + 1) * BLOCK] = jnp.sum(
            jnp.where(diagonal, jnp.broadcast_to(state, (BLOCK, BLOCK)), 0.0), axis=0, keepdims=True
        )
        weights = master_ref[at, :] - grad * (LR / jnp.sqrt(state))
        new_master_ref[at, :] = weights
        largest = jnp.max(jnp.max(jnp.abs(weights), axis=0, keepdims=True), axis=1, keepdims=True)
        scale = (largest + 1e-06).astype(BF16).astype(F32)
        coded_ref[at, :] = (weights / scale).astype(BF16)
        scale_row = jnp.where(lane == me * 4 + q, scale, scale_row)
    coded_ref[pl.ds(QUARTER, 16), :] = scale_row.astype(BF16)


def last_kernel(
    me_ref, s0_ref, s1_ref, s2_ref, s3_ref, top_in_ref, serving_ref, scale_ref, top_ref
):
    me = me_ref[0]
    scales = jnp.zeros((16, D), F32)
    for o, ref in enumerate((s0_ref, s1_ref, s2_ref, s3_ref)):
        start = pl.multiple_of(((me - o) & 3) * QUARTER, QUARTER)
        serving_ref[pl.ds(start, QUARTER), :] = ref[0:QUARTER, :]
        scales = scales + ref[QUARTER : QUARTER + 16, :].astype(F32)
    scale_ref[...] = scales[0:8, :]
    for i in range(16):
        for j in range(8):
            at = (j % 2) * 16
            top_ref[i * 16 : (i + 1) * 16, j * 128 : (j + 1) * 128] = top_in_ref[
                i * 4 + j // 2, at : at + 16, :
            ].astype(F32)


def like(shape, dtype):
    return jax.ShapeDtypeStruct(shape, dtype)


def over_groups(x):
    return [x] + [
        lax.ppermute(x, "grp", [(g, (g + o) % N_GRP) for g in range(N_GRP)]) for o in (1, 2, 3)
    ]


def exchange(x):
    return lax.all_to_all(x, ROW, 0, 0, tiled=True)


def on_device(
    serving, serving_scale, hot_blocks, bag_lengths, bag_indices, dense_act, labels, w_top, w_out, master, accum,
):
    me = lax.axis_index("grp").astype(I32).reshape(1)
    ids, rank = call(
        ids_kernel,
        [like((N_ROW, D), I32), like((N_ROW, SPAN), BF16)],
        [VM],
        (bag_indices,),
        1 << 26,
        "ids",
    )
    wanted = exchange(ids.reshape(N_ROW, 1, D)).reshape(N_ROW, D)
    use, use_t = call(
        counts_kernel,
        [like((BAGS, SLOTS), BF16), like((SLOTS, BAGS), BF16)],
        [VM] * 3,
        (bag_indices, bag_lengths, rank),
        1 << 29,
        "counts",
    )
    (table,) = pl.pallas_call(
        table_kernel,
        out_shape=[like((SPAN, D), BF16)],
        in_specs=[SM, pl.BlockSpec(memory_space=pl.ANY), VM],
        out_specs=[VM],
        scratch_shapes=[pltpu.VMEM((2, BLOCK, D), BF16), pltpu.SemaphoreType.DMA((2,))],
        name="table",
    )(hot_blocks, serving, serving_scale.reshape(1, 16))
    (rows,) = call(
        pick_kernel, [like((SLOTS, D), BF16)], [VM] * 2, (wanted, table), 1 << 26, "pick"
    )
    fetched = exchange(rows.reshape(N_ROW, CAP, D)).reshape(SLOTS, D)
    (place,) = call(
        place_kernel, [like((SPAN, SLOTS), BF16)], [VM], (wanted,), 1 << 26, "place"
    )
    (parts,) = call(
        step_kernel,
        [like((N_ROW, 40, D), BF16)],
        [VM] * 7,
        (fetched, use, use_t, dense_act, labels.reshape(1, BAGS), w_top, w_out.reshape(1, FF)),
        1 << 29,
        "step",
    )
    got = exchange(parts)
    (own,) = call(
        owned_kernel,
        [like((SPAN + 48, D), BF16)],
        [VM, VM, SM],
        (got, place, hot_blocks),
        1 << 26,
        "owned",
    )
    new_master, new_accum, coded, top_part = pl.pallas_call(
        update_kernel,
        out_shape=[
            like((QUARTER, D), F32),
            like((1, QUARTER), F32),
            like((QUARTER + 16, D), BF16),
            like((N_ROW, 32, D), BF16),
        ],
        in_specs=[SM] + [VM] * 6,
        out_specs=[VM] * 4,
        scratch_shapes=[pltpu.VMEM((N_GRP, SPAN + 48, D), BF16)],
        name="update",
    )(me, *over_groups(own), master[0], accum)
    quarters = over_groups(coded)
    top_all = exchange(top_part)
    fresh, fresh_scale, top_grad = call(
        last_kernel,
        [like((4 * QUARTER, D), BF16), like((8, D), F32), like((2 * D, FF), F32)],
        [SM] + [VM] * 5,
        (me, *quarters, top_all),
        1 << 20,
        "last",
    )
    return (
        new_master[None], new_accum, fresh, fresh_scale[0, :16].astype(BF16), top_grad,
    )


def solution(mesh):
    finer = Mesh(
        mesh.devices.reshape(mesh.shape["grp"], 4, 8, 2), ("grp", "row_0", "row_1", "row_2")
    )
    in_specs = (
        P(ROW, None),
        P(ROW),
        P("grp", ROW),
        P(GRP_ROW, None),
        P(GRP_ROW, None),
        P(GRP_ROW, None),
        P(GRP_ROW),
        P(),
        P(),
        P("grp", ROW, None),
        P("grp", ROW),
    )
    out_specs = (P("grp", ROW, None), P("grp", ROW), P(ROW, None), P(ROW), P())
    return jax.shard_map(
        on_device, mesh=finer, in_specs=in_specs, out_specs=out_specs, check_vma=False
    )
```

```python
import jax
import jax.numpy as jnp
from jax import lax
from jax.experimental import pallas as pl
from jax.experimental.pallas import tpu as pltpu
from jax.sharding import Mesh
from jax.sharding import PartitionSpec as P

ROW = ("row_0", "row_1", "row_2")
GRP_ROW = ("grp", "row_0", "row_1", "row_2")
N_GRP = 4
N_ROW = 64
BLOCK = 128
SPAN = 256
CAP = 8
BAGS = 256
NNZ = 1024
SLOTS = N_ROW * CAP
D = 128
FF = 1024
QUARTER = 512
LR = 0.05
GRANT = 16 << 20
F32 = jnp.float32
BF16 = jnp.bfloat16
I32 = jnp.int32
VM = pl.BlockSpec(memory_space=pltpu.VMEM)
SM = pl.BlockSpec(memory_space=pltpu.SMEM)


def iota(shape, dim):
    return lax.broadcasted_iota(I32, shape, dim)


def dot(a, b, ca=1, cb=0):
    return lax.dot_general(a, b, (((ca,), (cb,)), ((), ())), preferred_element_type=F32)


def ones_where(mask):
    return jnp.where(mask, 1.0, 0.0).astype(BF16)


def call(kernel, outs, specs, args, flops, name, scratch=()):
    bytes_accessed = sum(a.size * a.dtype.itemsize for a in args) + sum(
        o.size * o.dtype.itemsize for o in outs
    )
    return pl.pallas_call(
        kernel,
        out_shape=outs,
        in_specs=specs,
        out_specs=[VM] * len(outs),
        cost_estimate=pl.CostEstimate(
            flops=flops, bytes_accessed=bytes_accessed, transcendentals=0
        ),
        scratch_shapes=scratch,
        compiler_params=pltpu.CompilerParams(vmem_limit_bytes=GRANT),
        name=name,
    )(*args)


def shard_and_row(idx_ref):
    idx = idx_ref[...]
    shard = lax.shift_right_logical(idx, 8)
    return shard, idx & (SPAN - 1)


def ids_kernel(idx_ref, ids_ref, rank_ref):
    shard, row = shard_and_row(idx_ref)
    in_shard = ones_where(iota((N_ROW, NNZ), 0) == shard)
    at_row = ones_where(iota((SPAN, NNZ), 0) == row)
    used = dot(in_shard, at_row, 1, 1) > 0.5
    before = ones_where(iota((SPAN, SPAN), 0) < iota((SPAN, SPAN), 1))
    rank = dot(ones_where(used), before)
    column = iota((N_ROW, SPAN), 1).astype(F32)
    lane = iota((N_ROW, D), 1)
    ids = jnp.zeros((N_ROW, D), F32)
    for k in range(CAP):
        mine = jnp.sum(
            jnp.where(used & (rank == float(k)), column, 0.0), axis=1, keepdims=True
        )
        ids = jnp.where(lane == k, mine, ids)
    ids_ref[...] = ids.astype(I32)
    rank_ref[...] = rank.astype(BF16)


def counts_kernel(idx_ref, len_ref, rank_ref, use_ref, use_t_ref):
    shard, row = shard_and_row(idx_ref)
    in_shard = ones_where(iota((N_ROW, NNZ), 0) == shard)
    rank_at = dot(rank_ref[...], in_shard, 0, 0)
    rank = jnp.sum(jnp.where(iota((SPAN, NNZ), 0) == row, rank_at, 0.0), axis=0, keepdims=True)
    slot = shard * CAP + rank.astype(I32)
    at_slot = ones_where(iota((SLOTS, NNZ), 0) == slot)
    lengths = jnp.broadcast_to(len_ref[...].astype(F32), (BAGS, BAGS))
    a, b = iota((BAGS, BAGS), 0), iota((BAGS, BAGS), 1)
    starts = jnp.sum(jnp.where(b < a, lengths, 0.0), axis=1, keepdims=True).astype(I32)
    ends = jnp.sum(jnp.where(b <= a, lengths, 0.0), axis=1, keepdims=True).astype(I32)
    place = iota((BAGS, NNZ), 1)
    in_bag = ones_where((place >= starts) & (place < ends))
    use_ref[...] = dot(in_bag, at_slot, 1, 1).astype(BF16)
    use_t_ref[...] = dot(at_slot, in_bag, 1, 1).astype(BF16)


def table_kernel(hot_ref, serving_ref, scale_ref, table_ref, buf, sem):
    copies = [
        pltpu.make_async_copy(
            serving_ref.at[pl.ds(pl.multiple_of(hot_ref[0, j] * BLOCK, BLOCK), BLOCK)],
            buf.at[j],
            sem.at[j],
        )
        for j in range(2)
    ]
    for c in copies:
        c.start()
    scales = scale_ref[...].astype(F32)
    lane = iota(scales.shape, 1)
    for j, c in enumerate(copies):
        own = jnp.sum(jnp.where(lane == hot_ref[0, j], scales, 0.0), axis=1, keepdims=True)
        c.wait()
        table_ref[j * BLOCK : (j + 1) * BLOCK, :] = (buf[j].astype(F32) * own).astype(BF16)


def pick_kernel(ids_ref, table_ref, rows_ref):
    owner = ones_where(lax.shift_right_logical(iota((SLOTS, N_ROW), 0), 3) == iota((SLOTS, N_ROW), 1))
    spread = dot(owner, ids_ref[...].astype(F32).astype(BF16))
    mine = iota((SLOTS, D), 1) == (iota((SLOTS, D), 0) & (CAP - 1))
    column = jnp.sum(jnp.where(mine, spread, 0.0), axis=1, keepdims=True).astype(I32)
    onehot = ones_where(iota((SLOTS, SPAN), 1) == column)
    rows_ref[...] = dot(onehot, table_ref[...]).astype(BF16)


def place_kernel(ids_ref, place_ref):
    owner = ones_where(lax.shift_right_logical(iota((SLOTS, N_ROW), 0), 3) == iota((SLOTS, N_ROW), 1))
    spread = dot(ids_ref[...].astype(F32).astype(BF16), owner, 0, 1)
    mine = iota((D, SLOTS), 0) == (iota((D, SLOTS), 1) & (CAP - 1))
    line = jnp.sum(jnp.where(mine, spread, 0.0), axis=0, keepdims=True).astype(I32)
    place_ref[...] = ones_where(iota((SPAN, SLOTS), 0) == line)


def step_kernel(
    rows_ref, use_ref, use_t_ref, dense_ref, labels_ref, w_ref, w_out_ref, out_ref
):
    pooled = dot(use_ref[...], rows_ref[...]).astype(BF16)
    joined = jnp.concatenate([pooled, dense_ref[...]], axis=1)
    pre = dot(joined, w_ref[...])
    sig = jax.nn.sigmoid(pre)
    w_out = w_out_ref[...]
    logit = jnp.sum(pre * sig * w_out, axis=1, keepdims=True)
    a, b = iota((BAGS, BAGS), 0), iota((BAGS, BAGS), 1)
    labels = jnp.sum(
        jnp.where(a == b, jnp.broadcast_to(labels_ref[...], (BAGS, BAGS)), 0.0),
        axis=1,
        keepdims=True,
    )
    dlogit = jax.nn.sigmoid(logit) - labels
    dpre = (dlogit * w_out * (sig * (1.0 + pre * (1.0 - sig)))).astype(BF16)
    pooled_grad = dot(dpre, w_ref[0:D, :], 1, 1)
    high = pooled_grad.astype(BF16)
    low = (pooled_grad - high.astype(F32)).astype(BF16)
    use_t = use_t_ref[...]
    row_grad = dot(use_t, high) + dot(use_t, low)
    out_ref[:, 32:40, :] = row_grad.reshape(N_ROW, CAP, D).astype(BF16)
    top = dot(joined, dpre, 0, 0).astype(BF16)
    for i in range(16):
        for j in range(8):
            at = (j % 2) * 16
            out_ref[i * 4 + j // 2, at : at + 16, :] = top[
                i * 16 : (i + 1) * 16, j * 128 : (j + 1) * 128
            ]


def owned_kernel(got_ref, place_ref, hot_ref, out_ref):
    grads = got_ref[:, 32:40, :].astype(F32).reshape(SLOTS, D).astype(BF16)
    out_ref[0:SPAN, :] = dot(place_ref[...], grads).astype(BF16)
    out_ref[SPAN : SPAN + 32, :] = jnp.sum(got_ref[:, 0:32, :].astype(F32), axis=0).astype(BF16)
    lane = iota((16, D), 1)
    hot = jnp.where(lane == 0, hot_ref[0, 0], jnp.where(lane == 1, hot_ref[0, 1], 0))
    out_ref[SPAN + 32 : SPAN + 48, :] = hot.astype(F32).astype(BF16)


def top_kernel(me_ref, x0_ref, x1_ref, x2_ref, x3_ref, top_ref, by_group):
    me = me_ref[0]
    for o, ref in enumerate((x0_ref, x1_ref, x2_ref, x3_ref)):
        by_group[(me - o) & 3] = ref[SPAN : SPAN + 32, :]
    top = jnp.zeros((32, D), F32)
    for g in range(N_GRP):
        top = top + by_group[g].astype(F32)
    top_ref[...] = jnp.broadcast_to(top.astype(BF16)[None], (N_ROW, 32, D))


def update_kernel(
    me_ref, x0_ref, x1_ref, x2_ref, x3_ref, master_ref, accum_ref,
    new_master_ref, new_accum_ref, coded_ref, by_group,
):
    me = me_ref[0]
    for o, ref in enumerate((x0_ref, x1_ref, x2_ref, x3_ref)):
        by_group[(me - o) & 3] = ref[...]
    hot = [by_group[g, SPAN + 32 : SPAN + 48, :].astype(F32)[0:1, :] for g in range(N_GRP)]
    a, b = iota((BLOCK, BLOCK), 0), iota((BLOCK, BLOCK), 1)
    diagonal = a == b
    lane = iota((16, D), 1)
    scale_row = jnp.zeros((16, D), F32)
    for q in range(4):
        grad = jnp.zeros((BLOCK, D), F32)
        number = (me * 4 + q).astype(F32)
        for g in range(N_GRP):
            for j in range(2):
                block = by_group[g, j * BLOCK : (j + 1) * BLOCK, :].astype(F32)
                grad = grad + jnp.where(hot[g][:, j : j + 1] == number, block, 0.0)
        at = pl.ds(q * BLOCK, BLOCK)
        accum = jnp.broadcast_to(accum_ref[:, q * BLOCK : (q + 1) * BLOCK], (BLOCK, BLOCK))
        state = jnp.sum(jnp.where(diagonal, accum, 0.0), axis=1, keepdims=True) + jnp.mean(
            grad * grad, axis=1, keepdims=True
        )
        new_accum_ref[:, q * BLOCK : (q + 1) * BLOCK] = jnp.sum(
            jnp.where(diagonal, jnp.broadcast_to(state, (BLOCK, BLOCK)), 0.0), axis=0, keepdims=True
        )
        weights = master_ref[at, :] - grad * (LR / jnp.sqrt(state))
        new_master_ref[at, :] = weights
        largest = jnp.max(jnp.max(jnp.abs(weights), axis=0, keepdims=True), axis=1, keepdims=True)
        scale = (largest + 1e-06).astype(BF16).astype(F32)
        coded_ref[at, :] = (weights / scale).astype(BF16)
        scale_row = jnp.where(lane == me * 4 + q, scale, scale_row)
    coded_ref[pl.ds(QUARTER, 16), :] = scale_row.astype(BF16)


def fresh_kernel(me_ref, s0_ref, s1_ref, s2_ref, s3_ref, serving_ref, scale_ref):
    me = me_ref[0]
    scales = jnp.zeros((16, D), F32)
    for o, ref in enumerate((s0_ref, s1_ref, s2_ref, s3_ref)):
        start = pl.multiple_of(((me - o) & 3) * QUARTER, QUARTER)
        serving_ref[pl.ds(start, QUARTER), :] = ref[0:QUARTER, :]
        scales = scales + ref[QUARTER : QUARTER + 16, :].astype(F32)
    scale_ref[...] = scales[0:1, 0:16].astype(BF16)


def last_kernel(top_in_ref, top_ref):
    for i in range(16):
        for j in range(8):
            at = (j % 2) * 16
            top_ref[i * 16 : (i + 1) * 16, j * 128 : (j + 1) * 128] = top_in_ref[
                i * 4 + j // 2, at : at + 16, :
            ].astype(F32)


def like(shape, dtype):
    return jax.ShapeDtypeStruct(shape, dtype)


def over_groups(x):
    return [x] + [
        lax.ppermute(x, "grp", [(g, (g + o) % N_GRP) for g in range(N_GRP)]) for o in (1, 2, 3)
    ]


def exchange(x):
    return lax.all_to_all(x, ROW, 0, 0, tiled=True)


def on_device(
    serving, serving_scale, hot_blocks, bag_lengths, bag_indices, dense_act, labels, w_top, w_out, master, accum,
):
    me = lax.axis_index("grp").astype(I32).reshape(1)
    ids, rank = call(
        ids_kernel,
        [like((N_ROW, D), I32), like((N_ROW, SPAN), BF16)],
        [VM],
        (bag_indices,),
        1 << 26,
        "ids",
    )
    wanted = exchange(ids.reshape(N_ROW, 1, D)).reshape(N_ROW, D)
    use, use_t = call(
        counts_kernel,
        [like((BAGS, SLOTS), BF16), like((SLOTS, BAGS), BF16)],
        [VM] * 3,
        (bag_indices, bag_lengths, rank),
        1 << 29,
        "counts",
    )
    (table,) = call(
        table_kernel,
        [like((SPAN, D), BF16)],
        [SM, pl.BlockSpec(memory_space=pl.ANY), VM],
        (hot_blocks, serving, serving_scale.reshape(1, 16)),
        1 << 20,
        "table",
        [pltpu.VMEM((2, BLOCK, D), BF16), pltpu.SemaphoreType.DMA((2,))],
    )
    (rows,) = call(
        pick_kernel, [like((SLOTS, D), BF16)], [VM] * 2, (wanted, table), 1 << 26, "pick"
    )
    fetched = exchange(rows.reshape(N_ROW, CAP, D)).reshape(SLOTS, D)
    (place,) = call(
        place_kernel, [like((SPAN, SLOTS), BF16)], [VM], (wanted,), 1 << 26, "place"
    )
    (parts,) = call(
        step_kernel,
        [like((N_ROW, 40, D), BF16)],
        [VM] * 7,
        (fetched, use, use_t, dense_act, labels.reshape(1, BAGS), w_top, w_out.reshape(1, FF)),
        1 << 29,
        "step",
    )
    got = exchange(parts)
    (own,) = call(
        owned_kernel,
        [like((SPAN + 48, D), BF16)],
        [VM, VM, SM],
        (got, place, hot_blocks),
        1 << 26,
        "owned",
    )
    owned = over_groups(own)
    (top_part,) = call(
        top_kernel,
        [like((N_ROW, 32, D), BF16)],
        [SM] + [VM] * 4,
        (me, *owned),
        1 << 16,
        "top",
        [pltpu.VMEM((N_GRP, 32, D), BF16)],
    )
    top_all = exchange(top_part)
    new_master, new_accum, coded = call(
        update_kernel,
        [like((QUARTER, D), F32), like((1, QUARTER), F32), like((QUARTER + 16, D), BF16)],
        [SM] + [VM] * 6,
        (me, *owned, master[0], accum),
        1 << 22,
        "update",
        [pltpu.VMEM((N_GRP, SPAN + 48, D), BF16)],
    )
    fresh, fresh_scale = call(
        fresh_kernel,
        [like((4 * QUARTER, D), BF16), like((1, 16), BF16)],
        [SM] + [VM] * 4,
        (me, *over_groups(coded)),
        1 << 20,
        "fresh",
    )
    (top_grad,) = call(
        last_kernel, [like((2 * D, FF), F32)], [VM], (top_all,), 1 << 20, "last"
    )
    return new_master[None], new_accum, fresh, fresh_scale.reshape(16), top_grad


def solution(mesh):
    finer = Mesh(
        mesh.devices.reshape(mesh.shape["grp"], 4, 8, 2), ("grp", "row_0", "row_1", "row_2")
    )
    in_specs = (
        P(ROW, None),
        P(ROW),
        P("grp", ROW),
        P(GRP_ROW, None),
        P(GRP_ROW, None),
        P(GRP_ROW, None),
        P(GRP_ROW),
        P(),
        P(),
        P("grp", ROW, None),
        P("grp", ROW),
    )
    out_specs = (P("grp", ROW, None), P("grp", ROW), P(ROW, None), P(ROW), P())
    return jax.shard_map(
        on_device, mesh=finer, in_specs=in_specs, out_specs=out_specs, check_vma=False
    )
```

```python
import jax
import jax.numpy as jnp
from jax import lax
from jax.experimental import pallas as pl
from jax.experimental.pallas import tpu as pltpu
from jax.sharding import Mesh
from jax.sharding import PartitionSpec as P

ROW = ("row_0", "row_1", "row_2")
CHIPS = ("row_0", "row_1")
GRP_ROW = ("grp", "row_0", "row_1", "row_2")
N_GRP = 4
N_ROW = 64
BLOCK = 128
SPAN = 256
CAP = 8
BAGS = 256
NNZ = 1024
SLOTS = N_ROW * CAP
D = 128
FF = 1024
QUARTER = 512
LR = 0.05
GRANT = 16 << 20
F32 = jnp.float32
BF16 = jnp.bfloat16
I32 = jnp.int32
VM = pl.BlockSpec(memory_space=pltpu.VMEM)
SM = pl.BlockSpec(memory_space=pltpu.SMEM)


def iota(shape, dim):
    return lax.broadcasted_iota(I32, shape, dim)


def dot(a, b, ca=1, cb=0):
    return lax.dot_general(a, b, (((ca,), (cb,)), ((), ())), preferred_element_type=F32)


def ones_where(mask):
    return jnp.where(mask, 1.0, 0.0).astype(BF16)


def call(kernel, outs, specs, args, flops, name, scratch=()):
    bytes_accessed = sum(a.size * a.dtype.itemsize for a in args) + sum(
        o.size * o.dtype.itemsize for o in outs
    )
    return pl.pallas_call(
        kernel,
        out_shape=outs,
        in_specs=specs,
        out_specs=[VM] * len(outs),
        cost_estimate=pl.CostEstimate(
            flops=flops, bytes_accessed=bytes_accessed, transcendentals=0
        ),
        scratch_shapes=scratch,
        compiler_params=pltpu.CompilerParams(vmem_limit_bytes=GRANT),
        name=name,
    )(*args)


def shard_and_row(idx_ref):
    idx = idx_ref[...]
    shard = lax.shift_right_logical(idx, 8)
    return shard, idx & (SPAN - 1)


def ids_kernel(idx_ref, ids_ref, rank_ref):
    shard, row = shard_and_row(idx_ref)
    in_shard = ones_where(iota((N_ROW, NNZ), 0) == shard)
    at_row = ones_where(iota((SPAN, NNZ), 0) == row)
    used = dot(in_shard, at_row, 1, 1) > 0.5
    before = ones_where(iota((SPAN, SPAN), 0) < iota((SPAN, SPAN), 1))
    rank = dot(ones_where(used), before)
    column = iota((N_ROW, SPAN), 1).astype(F32)
    lane = iota((N_ROW, D), 1)
    ids = jnp.zeros((N_ROW, D), F32)
    for k in range(CAP):
        mine = jnp.sum(
            jnp.where(used & (rank == float(k)), column, 0.0), axis=1, keepdims=True
        )
        ids = jnp.where(lane == k, mine, ids)
    ids_ref[...] = ids.astype(I32)
    rank_ref[...] = rank.astype(BF16)


def counts_kernel(idx_ref, len_ref, rank_ref, use_ref, use_t_ref):
    shard, row = shard_and_row(idx_ref)
    in_shard = ones_where(iota((N_ROW, NNZ), 0) == shard)
    rank_at = dot(rank_ref[...], in_shard, 0, 0)
    rank = jnp.sum(jnp.where(iota((SPAN, NNZ), 0) == row, rank_at, 0.0), axis=0, keepdims=True)
    slot = shard * CAP + rank.astype(I32)
    at_slot = ones_where(iota((SLOTS, NNZ), 0) == slot)
    lengths = jnp.broadcast_to(len_ref[...].astype(F32), (BAGS, BAGS))
    a, b = iota((BAGS, BAGS), 0), iota((BAGS, BAGS), 1)
    starts = jnp.sum(jnp.where(b < a, lengths, 0.0), axis=1, keepdims=True).astype(I32)
    ends = jnp.sum(jnp.where(b <= a, lengths, 0.0), axis=1, keepdims=True).astype(I32)
    place = iota((BAGS, NNZ), 1)
    in_bag = ones_where((place >= starts) & (place < ends))
    use_ref[...] = dot(in_bag, at_slot, 1, 1).astype(BF16)
    use_t_ref[...] = dot(at_slot, in_bag, 1, 1).astype(BF16)


def table_kernel(hot_ref, serving_ref, scale_ref, table_ref, buf, sem):
    copies = [
        pltpu.make_async_copy(
            serving_ref.at[pl.ds(pl.multiple_of(hot_ref[0, j] * BLOCK, BLOCK), BLOCK)],
            buf.at[j],
            sem.at[j],
        )
        for j in range(2)
    ]
    for c in copies:
        c.start()
    scales = scale_ref[...].astype(F32)
    lane = iota(scales.shape, 1)
    for j, c in enumerate(copies):
        own = jnp.sum(jnp.where(lane == hot_ref[0, j], scales, 0.0), axis=1, keepdims=True)
        c.wait()
        table_ref[j * BLOCK : (j + 1) * BLOCK, :] = (buf[j].astype(F32) * own).astype(BF16)


def pick_kernel(ids_ref, table_ref, rows_ref):
    owner = ones_where(lax.shift_right_logical(iota((SLOTS, N_ROW), 0), 3) == iota((SLOTS, N_ROW), 1))
    spread = dot(owner, ids_ref[...].astype(F32).astype(BF16))
    mine = iota((SLOTS, D), 1) == (iota((SLOTS, D), 0) & (CAP - 1))
    column = jnp.sum(jnp.where(mine, spread, 0.0), axis=1, keepdims=True).astype(I32)
    onehot = ones_where(iota((SLOTS, SPAN), 1) == column)
    rows_ref[...] = dot(onehot, table_ref[...]).astype(BF16)


def place_kernel(ids_ref, place_ref):
    owner = ones_where(lax.shift_right_logical(iota((SLOTS, N_ROW), 0), 3) == iota((SLOTS, N_ROW), 1))
    spread = dot(ids_ref[...].astype(F32).astype(BF16), owner, 0, 1)
    mine = iota((D, SLOTS), 0) == (iota((D, SLOTS), 1) & (CAP - 1))
    line = jnp.sum(jnp.where(mine, spread, 0.0), axis=0, keepdims=True).astype(I32)
    place_ref[...] = ones_where(iota((SPAN, SLOTS), 0) == line)


def dense_kernel(dense_ref, w_ref, labels_ref, w_out_ref, pre_ref, labels_out_ref, w_out_out_ref):
    pre_ref[...] = dot(dense_ref[...], w_ref[D : 2 * D, :])
    a, b = iota((BAGS, BAGS), 0), iota((BAGS, BAGS), 1)
    labels = jnp.sum(
        jnp.where(a == b, jnp.broadcast_to(labels_ref[...], (BAGS, BAGS)), 0.0),
        axis=1,
        keepdims=True,
    )
    labels_out_ref[...] = jnp.broadcast_to(labels, (BAGS, D))
    w_out_out_ref[...] = w_out_ref[...]


def step_kernel(
    core_ref, rows_ref, use_ref, dense_ref, pre_ref, labels_ref, w_ref, w_out_ref,
    give_ref, keep_ref, pooled_grad_ref,
):
    pooled = dot(use_ref[...], rows_ref[...]).astype(BF16)
    pre = pre_ref[...] + dot(pooled, w_ref[0:D, :])
    sig = jax.nn.sigmoid(pre)
    w_out = w_out_ref[...]
    logit = jnp.sum(pre * sig * w_out, axis=1, keepdims=True)
    dlogit = jax.nn.sigmoid(logit) - labels_ref[:, 0:1]
    dpre = (dlogit * w_out * (sig * (1.0 + pre * (1.0 - sig)))).astype(BF16)
    first = core_ref[0] == 0
    dense = dense_ref[...]
    give = dot(jnp.where(first, dense, pooled), dpre, 0, 0).astype(BF16)
    keep = dot(jnp.where(first, pooled, dense), dpre, 0, 0)
    for i in range(8):
        for j in range(8):
            tile = slice(i * 16, (i + 1) * 16), slice(j * 128, (j + 1) * 128)
            give_ref[i * 8 + j] = give[tile]
            keep_ref[i * 8 + j] = keep[tile]
    pooled_grad_ref[...] = dot(dpre, w_ref[0:D, :], 1, 1)


def row_grad_kernel(pooled_grad_ref, use_t_ref, out_ref):
    pooled_grad = pooled_grad_ref[...]
    high = pooled_grad.astype(BF16)
    low = (pooled_grad - high.astype(F32)).astype(BF16)
    use_t = use_t_ref[...]
    out_ref[...] = (dot(use_t, high) + dot(use_t, low)).astype(BF16)


def parts_kernel(keep_ref, given_ref, row_grad_ref, out_ref):
    out_ref[:, 0:16, :] = (keep_ref[...] + given_ref[...].astype(F32)).astype(BF16)
    out_ref[:, 16:24, :] = row_grad_ref[...]


def owned_kernel(got_ref, place_ref, hot_ref, out_ref):
    grads = got_ref[:, :, 16:24, :].astype(F32).reshape(SLOTS, D).astype(BF16)
    out_ref[0:SPAN, :] = dot(place_ref[...], grads).astype(BF16)
    for half in range(2):
        at = SPAN + 16 * half
        out_ref[at : at + 16, :] = jnp.sum(
            got_ref[:, half, 0:16, :].astype(F32), axis=0
        ).astype(BF16)
    lane = iota((16, D), 1)
    hot = jnp.where(lane == 0, hot_ref[0, 0], jnp.where(lane == 1, hot_ref[0, 1], 0))
    out_ref[SPAN + 32 : SPAN + 48, :] = hot.astype(F32).astype(BF16)


def top_kernel(me_ref, x0_ref, x1_ref, x2_ref, x3_ref, top_ref, by_group):
    me = me_ref[0]
    for o, ref in enumerate((x0_ref, x1_ref, x2_ref, x3_ref)):
        by_group[(me - o) & 3] = ref[SPAN : SPAN + 32, :]
    top = jnp.zeros((32, D), F32)
    for g in range(N_GRP):
        top = top + by_group[g].astype(F32)
    top_ref[...] = jnp.broadcast_to(top.astype(BF16)[None], (N_ROW // 2, 32, D))


def owner_kernel(master_ref, accum_ref, out_ref):
    out_ref[0:QUARTER, :] = master_ref[...]
    line = iota((8, D), 0)
    accum = jnp.zeros((8, D), F32)
    for q in range(4):
        accum = jnp.where(line == q, accum_ref[:, q * BLOCK : (q + 1) * BLOCK], accum)
    out_ref[QUARTER : QUARTER + 8, :] = accum


def update_kernel(
    me_ref, x0_ref, x1_ref, x2_ref, x3_ref, m0_ref, m1_ref, m2_ref, m3_ref,
    new_master_ref, new_accum_ref, serving_ref, scale_ref, by_group, grads,
):
    me = me_ref[0]
    for o, ref in enumerate((x0_ref, x1_ref, x2_ref, x3_ref)):
        by_group[(me - o) & 3] = ref[...]
    grads[...] = jnp.zeros((16, BLOCK, D), F32)
    for g in range(N_GRP):
        hot = by_group[g, SPAN + 32 : SPAN + 48, :].astype(F32).astype(I32)
        for j in range(2):
            number = jnp.clip(hot[0, j], 0, 15)
            grads[number] = grads[number] + by_group[g, j * BLOCK : (j + 1) * BLOCK, :].astype(F32)
    a, b = iota((BLOCK, BLOCK), 0), iota((BLOCK, BLOCK), 1)
    diagonal = a == b
    lane = iota((1, 16), 1)
    scales = jnp.zeros((1, 16), F32)
    for o, ref in enumerate((m0_ref, m1_ref, m2_ref, m3_ref)):
        for q in range(4):
            number = ((me - o) & 3) * 4 + q
            grad = grads[number]
            accum = jnp.broadcast_to(ref[QUARTER + q : QUARTER + q + 1, :], (BLOCK, BLOCK))
            state = jnp.sum(jnp.where(diagonal, accum, 0.0), axis=1, keepdims=True) + jnp.mean(
                grad * grad, axis=1, keepdims=True
            )
            weights = ref[q * BLOCK : (q + 1) * BLOCK, :] - grad * (LR / jnp.sqrt(state))
            if o == 0:
                new_master_ref[q * BLOCK : (q + 1) * BLOCK, :] = weights
                new_accum_ref[:, q * BLOCK : (q + 1) * BLOCK] = jnp.sum(
                    jnp.where(diagonal, jnp.broadcast_to(state, (BLOCK, BLOCK)), 0.0),
                    axis=0,
                    keepdims=True,
                )
            largest = jnp.max(jnp.max(jnp.abs(weights), axis=0, keepdims=True), axis=1, keepdims=True)
            scale = (largest + 1e-06).astype(BF16).astype(F32)
            at = pl.ds(pl.multiple_of(number * BLOCK, BLOCK), BLOCK)
            serving_ref[at, :] = (weights / scale).astype(BF16)
            scales = jnp.where(lane == number, scale, scales)
    scale_ref[...] = scales.astype(BF16)


def last_kernel(core_ref, mine_ref, other_ref, top_ref):
    for ref, core in ((mine_ref, core_ref[0]), (other_ref, 1 - core_ref[0])):
        for s in range(N_ROW // 2):
            column = pl.multiple_of((s % 4 * 2 + core) * 128, 128)
            for half in range(2):
                line = half * 128 + s // 4 * 16
                top_ref[line : line + 16, pl.ds(column, 128)] = ref[
                    s, half * 16 : (half + 1) * 16, :
                ].astype(F32)


def like(shape, dtype):
    return jax.ShapeDtypeStruct(shape, dtype)


def over_groups(x):
    return [x] + [
        lax.ppermute(x, "grp", [(g, (g + o) % N_GRP) for g in range(N_GRP)]) for o in (1, 2, 3)
    ]


def other_core(x):
    return lax.ppermute(x, "row_2", [(0, 1), (1, 0)])


def exchange(x, axes=ROW):
    return lax.all_to_all(x, axes, 0, 0, tiled=True)


def on_device(
    serving, serving_scale, hot_blocks, bag_lengths, bag_indices, dense_act, labels, w_top, w_out, master, accum,
):
    me = lax.axis_index("grp").astype(I32).reshape(1)
    core = lax.axis_index("row_2").astype(I32).reshape(1)
    (owner,) = call(
        owner_kernel, [like((QUARTER + 8, D), F32)], [VM] * 2, (master[0], accum), 1 << 16, "owner"
    )
    owners = over_groups(owner)
    ids, rank = call(
        ids_kernel,
        [like((N_ROW, D), I32), like((N_ROW, SPAN), BF16)],
        [VM],
        (bag_indices,),
        1 << 26,
        "ids",
    )
    wanted = exchange(ids.reshape(N_ROW, 1, D)).reshape(N_ROW, D)
    use, use_t = call(
        counts_kernel,
        [like((BAGS, SLOTS), BF16), like((SLOTS, BAGS), BF16)],
        [VM] * 3,
        (bag_indices, bag_lengths, rank),
        1 << 29,
        "counts",
    )
    (table,) = call(
        table_kernel,
        [like((SPAN, D), BF16)],
        [SM, pl.BlockSpec(memory_space=pl.ANY), VM],
        (hot_blocks, serving, serving_scale.reshape(1, 16)),
        1 << 20,
        "table",
        [pltpu.VMEM((2, BLOCK, D), BF16), pltpu.SemaphoreType.DMA((2,))],
    )
    (rows,) = call(
        pick_kernel, [like((SLOTS, D), BF16)], [VM] * 2, (wanted, table), 1 << 26, "pick"
    )
    fetched = exchange(rows.reshape(N_ROW, CAP, D)).reshape(SLOTS, D)
    fetched, *owners = lax.optimization_barrier((fetched, *owners))
    (place,) = call(
        place_kernel, [like((SPAN, SLOTS), BF16)], [VM], (wanted,), 1 << 26, "place"
    )
    pre, labels_column, w_out_line = call(
        dense_kernel,
        [like((BAGS, FF), F32), like((BAGS, D), F32), like((1, FF), F32)],
        [VM] * 4,
        (dense_act, w_top, labels.reshape(1, BAGS), w_out.reshape(1, FF)),
        1 << 27,
        "dense",
    )
    give, keep, pooled_grad = call(
        step_kernel,
        [like((N_ROW, 16, D), BF16), like((N_ROW, 16, D), F32), like((BAGS, D), F32)],
        [SM] + [VM] * 7,
        (core, fetched, use, dense_act, pre, labels_column, w_top, w_out_line),
        1 << 29,
        "step",
    )
    given = other_core(give)
    (row_grad,) = call(
        row_grad_kernel, [like((SLOTS, D), BF16)], [VM] * 2, (pooled_grad, use_t), 1 << 27, "row_grad"
    )
    (parts,) = call(
        parts_kernel,
        [like((N_ROW, 24, D), BF16)],
        [VM] * 3,
        (keep, given, row_grad.reshape(N_ROW, CAP, D)),
        1 << 20,
        "parts",
    )
    got = exchange(parts)
    (own,) = call(
        owned_kernel,
        [like((SPAN + 48, D), BF16)],
        [VM, VM, SM],
        (got.reshape(N_ROW // 2, 2, 24, D), place, hot_blocks),
        1 << 26,
        "owned",
    )
    owned = over_groups(own)
    (top_part,) = call(
        top_kernel,
        [like((N_ROW // 2, 32, D), BF16)],
        [SM] + [VM] * 4,
        (me, *owned),
        1 << 16,
        "top",
        [pltpu.VMEM((N_GRP, 32, D), BF16)],
    )
    top_mine = exchange(top_part, CHIPS)
    new_master, new_accum, fresh, fresh_scale = call(
        update_kernel,
        [
            like((QUARTER, D), F32),
            like((1, QUARTER), F32),
            like((4 * QUARTER, D), BF16),
            like((1, 16), BF16),
        ],
        [SM] + [VM] * 8,
        (me, *owned, *owners),
        1 << 22,
        "update",
        [pltpu.VMEM((N_GRP, SPAN + 48, D), BF16), pltpu.VMEM((16, BLOCK, D), F32)],
    )
    top_mine, fresh_scale = lax.optimization_barrier((top_mine, fresh_scale))
    (top_grad,) = call(
        last_kernel,
        [like((2 * D, FF), F32)],
        [SM] + [VM] * 2,
        (core, top_mine, other_core(top_mine)),
        1 << 20,
        "last",
    )
    return new_master[None], new_accum, fresh, fresh_scale.reshape(16), top_grad


def solution(mesh):
    finer = Mesh(
        mesh.devices.reshape(mesh.shape["grp"], 4, 8, 2), ("grp", "row_0", "row_1", "row_2")
    )
    in_specs = (
        P(ROW, None),
        P(ROW),
        P("grp", ROW),
        P(GRP_ROW, None),
        P(GRP_ROW, None),
        P(GRP_ROW, None),
        P(GRP_ROW),
        P(),
        P(),
        P("grp", ROW, None),
        P("grp", ROW),
    )
    out_specs = (P("grp", ROW, None), P("grp", ROW), P(ROW, None), P(ROW), P())
    return jax.shard_map(
        on_device, mesh=finer, in_specs=in_specs, out_specs=out_specs, check_vma=False
    )
```

```python
import jax
import jax.numpy as jnp
from jax import lax
from jax.experimental import pallas as pl
from jax.experimental.pallas import tpu as pltpu
from jax.sharding import Mesh
from jax.sharding import PartitionSpec as P


ROW = ("row_0", "row_1", "row_2")
CHIPS = ("row_0", "row_1")
GRP_ROW = ("grp", "row_0", "row_1", "row_2")
N_GRP = 4
N_ROW = 64
BLOCK = 128
SPAN = 256
CAP = 8
BAGS = 256
NNZ = 1024
SLOTS = N_ROW * CAP
D = 128
FF = 1024
QUARTER = 512
LR = 0.05
GRANT = 16 << 20
F32 = jnp.float32
BF16 = jnp.bfloat16
I32 = jnp.int32
VM = pl.BlockSpec(memory_space=pltpu.VMEM)
SM = pl.BlockSpec(memory_space=pltpu.SMEM)


def iota(shape, dim):
    return lax.broadcasted_iota(I32, shape, dim)


def dot(a, b, ca=1, cb=0):
    return lax.dot_general(a, b, (((ca,), (cb,)), ((), ())), preferred_element_type=F32)


def ones_where(mask):
    return jnp.where(mask, 1.0, 0.0).astype(BF16)


def call(kernel, outs, specs, args, flops, scratch=()):
    bytes_accessed = sum(a.size * a.dtype.itemsize for a in args) + sum(
        o.size * o.dtype.itemsize for o in outs
    )
    return pl.pallas_call(
        kernel,
        out_shape=outs,
        in_specs=specs,
        out_specs=[VM] * len(outs),
        cost_estimate=pl.CostEstimate(
            flops=flops, bytes_accessed=bytes_accessed, transcendentals=0
        ),
        scratch_shapes=scratch,
        compiler_params=pltpu.CompilerParams(vmem_limit_bytes=GRANT),
    )(*args)


def shard_and_row(idx_ref):
    idx = idx_ref[...]
    shard = lax.shift_right_logical(idx, 8)
    return shard, idx & (SPAN - 1)


def ids_kernel(idx_ref, ids_ref, rank_ref):
    shard, row = shard_and_row(idx_ref)
    in_shard = ones_where(iota((N_ROW, NNZ), 0) == shard)
    at_row = ones_where(iota((SPAN, NNZ), 0) == row)
    used = dot(in_shard, at_row, 1, 1) > 0.5
    before = ones_where(iota((SPAN, SPAN), 0) < iota((SPAN, SPAN), 1))
    rank = dot(ones_where(used), before)
    column = iota((N_ROW, SPAN), 1).astype(F32)
    lane = iota((N_ROW, D), 1)
    ids = jnp.zeros((N_ROW, D), F32)
    for k in range(CAP):
        mine = jnp.sum(
            jnp.where(used & (rank == float(k)), column, 0.0), axis=1, keepdims=True
        )
        ids = jnp.where(lane == k, mine, ids)
    ids_ref[...] = ids.astype(I32)
    rank_ref[...] = rank.astype(BF16)


def counts_kernel(idx_ref, len_ref, rank_ref, use_ref, use_t_ref):
    shard, row = shard_and_row(idx_ref)
    in_shard = ones_where(iota((N_ROW, NNZ), 0) == shard)
    rank_at = dot(rank_ref[...], in_shard, 0, 0)
    rank = jnp.sum(jnp.where(iota((SPAN, NNZ), 0) == row, rank_at, 0.0), axis=0, keepdims=True)
    slot = shard * CAP + rank.astype(I32)
    at_slot = ones_where(iota((SLOTS, NNZ), 0) == slot)
    lengths = jnp.broadcast_to(len_ref[...].astype(F32), (BAGS, BAGS))
    a, b = iota((BAGS, BAGS), 0), iota((BAGS, BAGS), 1)
    starts = jnp.sum(jnp.where(b < a, lengths, 0.0), axis=1, keepdims=True).astype(I32)
    ends = jnp.sum(jnp.where(b <= a, lengths, 0.0), axis=1, keepdims=True).astype(I32)
    place = iota((BAGS, NNZ), 1)
    in_bag = ones_where((place >= starts) & (place < ends))
    use_ref[...] = dot(in_bag, at_slot, 1, 1).astype(BF16)
    use_t_ref[...] = dot(at_slot, in_bag, 1, 1).astype(BF16)


def table_kernel(hot_ref, serving_ref, scale_ref, table_ref, buf, sem):
    copies = [
        pltpu.make_async_copy(
            serving_ref.at[pl.ds(pl.multiple_of(hot_ref[0, j] * BLOCK, BLOCK), BLOCK)],
            buf.at[j],
            sem.at[j],
        )
        for j in range(2)
    ]
    for c in copies:
        c.start()
    scales = scale_ref[...].astype(F32)
    lane = iota(scales.shape, 1)
    for j, c in enumerate(copies):
        own = jnp.sum(jnp.where(lane == hot_ref[0, j], scales, 0.0), axis=1, keepdims=True)
        c.wait()
        table_ref[j * BLOCK : (j + 1) * BLOCK, :] = (buf[j].astype(F32) * own).astype(BF16)


def pick_kernel(ids_ref, table_ref, rows_ref):
    owner = ones_where(lax.shift_right_logical(iota((SLOTS, N_ROW), 0), 3) == iota((SLOTS, N_ROW), 1))
    spread = dot(owner, ids_ref[...].astype(F32).astype(BF16))
    mine = iota((SLOTS, D), 1) == (iota((SLOTS, D), 0) & (CAP - 1))
    column = jnp.sum(jnp.where(mine, spread, 0.0), axis=1, keepdims=True).astype(I32)
    onehot = ones_where(iota((SLOTS, SPAN), 1) == column)
    rows_ref[...] = dot(onehot, table_ref[...]).astype(BF16)


def place_kernel(ids_ref, place_ref):
    owner = ones_where(lax.shift_right_logical(iota((SLOTS, N_ROW), 0), 3) == iota((SLOTS, N_ROW), 1))
    spread = dot(ids_ref[...].astype(F32).astype(BF16), owner, 0, 1)
    mine = iota((D, SLOTS), 0) == (iota((D, SLOTS), 1) & (CAP - 1))
    line = jnp.sum(jnp.where(mine, spread, 0.0), axis=0, keepdims=True).astype(I32)
    place_ref[...] = ones_where(iota((SPAN, SLOTS), 0) == line)


def dense_kernel(dense_ref, w_ref, labels_ref, w_out_ref, pre_ref, labels_out_ref, w_out_out_ref):
    pre_ref[...] = dot(dense_ref[...], w_ref[D : 2 * D, :])
    a, b = iota((BAGS, BAGS), 0), iota((BAGS, BAGS), 1)
    labels = jnp.sum(
        jnp.where(a == b, jnp.broadcast_to(labels_ref[...], (BAGS, BAGS)), 0.0),
        axis=1,
        keepdims=True,
    )
    labels_out_ref[...] = jnp.broadcast_to(labels, (BAGS, D))
    w_out_out_ref[...] = w_out_ref[...]


def step_kernel(
    core_ref, rows_ref, use_ref, dense_ref, pre_ref, labels_ref, w_ref, w_out_ref,
    give_ref, keep_ref, pooled_grad_ref,
):
    pooled = dot(use_ref[...], rows_ref[...]).astype(BF16)
    pre = pre_ref[...] + dot(pooled, w_ref[0:D, :])
    sig = jax.nn.sigmoid(pre)
    w_out = w_out_ref[...]
    logit = jnp.sum(pre * sig * w_out, axis=1, keepdims=True)
    dlogit = jax.nn.sigmoid(logit) - labels_ref[:, 0:1]
    dpre = (dlogit * w_out * (sig * (1.0 + pre * (1.0 - sig)))).astype(BF16)
    first = core_ref[0] == 0
    dense = dense_ref[...]
    give = dot(jnp.where(first, dense, pooled), dpre, 0, 0).astype(BF16)
    keep = dot(jnp.where(first, pooled, dense), dpre, 0, 0)
    for i in range(8):
        for j in range(8):
            tile = slice(i * 16, (i + 1) * 16), slice(j * 128, (j + 1) * 128)
            give_ref[i * 8 + j] = give[tile]
            keep_ref[i * 8 + j] = keep[tile]
    pooled_grad_ref[...] = dot(dpre, w_ref[0:D, :], 1, 1)


def row_grad_kernel(pooled_grad_ref, use_t_ref, out_ref):
    pooled_grad = pooled_grad_ref[...]
    high = pooled_grad.astype(BF16)
    low = (pooled_grad - high.astype(F32)).astype(BF16)
    use_t = use_t_ref[...]
    out_ref[...] = (dot(use_t, high) + dot(use_t, low)).astype(BF16)


def parts_kernel(keep_ref, given_ref, row_grad_ref, out_ref):
    out_ref[:, 0:16, :] = (keep_ref[...] + given_ref[...].astype(F32)).astype(BF16)
    out_ref[:, 16:24, :] = row_grad_ref[...]


def owned_kernel(got_ref, place_ref, hot_ref, out_ref):
    grads = got_ref[:, :, 16:24, :].astype(F32).reshape(SLOTS, D).astype(BF16)
    out_ref[0:SPAN, :] = dot(place_ref[...], grads).astype(BF16)
    for half in range(2):
        at = SPAN + 16 * half
        out_ref[at : at + 16, :] = jnp.sum(
            got_ref[:, half, 0:16, :].astype(F32), axis=0
        ).astype(BF16)
    lane = iota((16, D), 1)
    hot = jnp.where(lane == 0, hot_ref[0, 0], jnp.where(lane == 1, hot_ref[0, 1], 0))
    out_ref[SPAN + 32 : SPAN + 48, :] = hot.astype(F32).astype(BF16)


def top_kernel(me_ref, x0_ref, x1_ref, x2_ref, x3_ref, top_ref, by_group):
    me = me_ref[0]
    for o, ref in enumerate((x0_ref, x1_ref, x2_ref, x3_ref)):
        by_group[(me - o) & 3] = ref[SPAN : SPAN + 32, :]
    top = jnp.zeros((32, D), F32)
    for g in range(N_GRP):
        top = top + by_group[g].astype(F32)
    top_ref[...] = jnp.broadcast_to(top.astype(BF16)[None], (N_ROW // 2, 32, D))


def owner_kernel(master_ref, accum_ref, out_ref):
    out_ref[0:QUARTER, :] = master_ref[...]
    line = iota((8, D), 0)
    accum = jnp.zeros((8, D), F32)
    for q in range(4):
        accum = jnp.where(line == q, accum_ref[:, q * BLOCK : (q + 1) * BLOCK], accum)
    out_ref[QUARTER : QUARTER + 8, :] = accum


def update_kernel(
    me_ref, x0_ref, x1_ref, x2_ref, x3_ref, m0_ref, m1_ref, m2_ref, m3_ref,
    new_master_ref, new_accum_ref, serving_ref, scale_ref, by_group, grads,
):
    me = me_ref[0]
    for o, ref in enumerate((x0_ref, x1_ref, x2_ref, x3_ref)):
        by_group[(me - o) & 3] = ref[...]
    grads[...] = jnp.zeros((16, BLOCK, D), F32)
    for g in range(N_GRP):
        hot = by_group[g, SPAN + 32 : SPAN + 48, :].astype(F32).astype(I32)
        for j in range(2):
            number = jnp.clip(hot[0, j], 0, 15)
            grads[number] = grads[number] + by_group[g, j * BLOCK : (j + 1) * BLOCK, :].astype(F32)
    a, b = iota((BLOCK, BLOCK), 0), iota((BLOCK, BLOCK), 1)
    diagonal = a == b
    lane = iota((1, 16), 1)
    scales = jnp.zeros((1, 16), F32)
    for o, ref in enumerate((m0_ref, m1_ref, m2_ref, m3_ref)):
        for q in range(4):
            number = ((me - o) & 3) * 4 + q
            grad = grads[number]
            accum = jnp.broadcast_to(ref[QUARTER + q : QUARTER + q + 1, :], (BLOCK, BLOCK))
            state = jnp.sum(jnp.where(diagonal, accum, 0.0), axis=1, keepdims=True) + jnp.mean(
                grad * grad, axis=1, keepdims=True
            )
            weights = ref[q * BLOCK : (q + 1) * BLOCK, :] - grad * (LR / jnp.sqrt(state))
            if o == 0:
                new_master_ref[q * BLOCK : (q + 1) * BLOCK, :] = weights
                new_accum_ref[:, q * BLOCK : (q + 1) * BLOCK] = jnp.sum(
                    jnp.where(diagonal, jnp.broadcast_to(state, (BLOCK, BLOCK)), 0.0),
                    axis=0,
                    keepdims=True,
                )
            largest = jnp.max(jnp.max(jnp.abs(weights), axis=0, keepdims=True), axis=1, keepdims=True)
            scale = (largest + 1e-06).astype(BF16).astype(F32)
            at = pl.ds(pl.multiple_of(number * BLOCK, BLOCK), BLOCK)
            serving_ref[at, :] = (weights / scale).astype(BF16)
            scales = jnp.where(lane == number, scale, scales)
    scale_ref[...] = scales.astype(BF16)


def last_kernel(core_ref, mine_ref, other_ref, top_ref):
    for ref, core in ((mine_ref, core_ref[0]), (other_ref, 1 - core_ref[0])):
        for s in range(N_ROW // 2):
            column = pl.multiple_of((s % 4 * 2 + core) * 128, 128)
            for half in range(2):
                line = half * 128 + s // 4 * 16
                top_ref[line : line + 16, pl.ds(column, 128)] = ref[
                    s, half * 16 : (half + 1) * 16, :
                ].astype(F32)


def like(shape, dtype):
    return jax.ShapeDtypeStruct(shape, dtype)


def over_groups(x):
    return [x] + [
        lax.ppermute(x, "grp", [(g, (g + o) % N_GRP) for g in range(N_GRP)]) for o in (1, 2, 3)
    ]


def other_core(x):
    return lax.ppermute(x, "row_2", [(0, 1), (1, 0)])


def exchange(x, axes=ROW):
    return lax.all_to_all(x, axes, 0, 0, tiled=True)


def on_device(
    serving, serving_scale, hot_blocks, bag_lengths, bag_indices, dense_act, labels, w_top, w_out, master, accum,
):
    me = lax.axis_index("grp").astype(I32).reshape(1)
    core = lax.axis_index("row_2").astype(I32).reshape(1)
    ids, rank = call(
        ids_kernel,
        [like((N_ROW, D), I32), like((N_ROW, SPAN), BF16)],
        [VM],
        (bag_indices,),
        1 << 26,
    )
    wanted = exchange(ids.reshape(N_ROW, 1, D)).reshape(N_ROW, D)
    (owner,) = call(
        owner_kernel, [like((QUARTER + 8, D), F32)], [VM] * 2, (master[0], accum), 1 << 16
    )
    use, use_t = call(
        counts_kernel,
        [like((BAGS, SLOTS), BF16), like((SLOTS, BAGS), BF16)],
        [VM] * 3,
        (bag_indices, bag_lengths, rank),
        1 << 29,
    )
    (table,) = call(
        table_kernel,
        [like((SPAN, D), BF16)],
        [SM, pl.BlockSpec(memory_space=pl.ANY), VM],
        (hot_blocks, serving, serving_scale.reshape(1, 16)),
        1 << 20,
        [pltpu.VMEM((2, BLOCK, D), BF16), pltpu.SemaphoreType.DMA((2,))],
    )
    pre, labels_column, w_out_line = call(
        dense_kernel,
        [like((BAGS, FF), F32), like((BAGS, D), F32), like((1, FF), F32)],
        [VM] * 4,
        (dense_act, w_top, labels.reshape(1, BAGS), w_out.reshape(1, FF)),
        1 << 27,
    )
    wanted, table, pre, labels_column, w_out_line = lax.optimization_barrier(
        (wanted, table, pre, labels_column, w_out_line)
    )
    owners = over_groups(owner)
    (rows,) = call(pick_kernel, [like((SLOTS, D), BF16)], [VM] * 2, (wanted, table), 1 << 26)
    fetched = exchange(rows.reshape(N_ROW, CAP, D)).reshape(SLOTS, D)
    (place,) = call(place_kernel, [like((SPAN, SLOTS), BF16)], [VM], (wanted,), 1 << 26)
    give, keep, pooled_grad = call(
        step_kernel,
        [like((N_ROW, 16, D), BF16), like((N_ROW, 16, D), F32), like((BAGS, D), F32)],
        [SM] + [VM] * 7,
        (core, fetched, use, dense_act, pre, labels_column, w_top, w_out_line),
        1 << 29,
    )
    given = other_core(give)
    (row_grad,) = call(
        row_grad_kernel, [like((SLOTS, D), BF16)], [VM] * 2, (pooled_grad, use_t), 1 << 27
    )
    (parts,) = call(
        parts_kernel,
        [like((N_ROW, 24, D), BF16)],
        [VM] * 3,
        (keep, given, row_grad.reshape(N_ROW, CAP, D)),
        1 << 20,
    )
    got = exchange(parts)
    (own,) = call(
        owned_kernel,
        [like((SPAN + 48, D), BF16)],
        [VM, VM, SM],
        (got.reshape(N_ROW // 2, 2, 24, D), place, hot_blocks),
        1 << 26,
    )
    owned = over_groups(own)
    (top_part,) = call(
        top_kernel,
        [like((N_ROW // 2, 32, D), BF16)],
        [SM] + [VM] * 4,
        (me, *owned),
        1 << 16,
        [pltpu.VMEM((N_GRP, 32, D), BF16)],
    )
    top_mine = exchange(top_part, CHIPS)
    new_master, new_accum, fresh, fresh_scale = call(
        update_kernel,
        [
            like((QUARTER, D), F32),
            like((1, QUARTER), F32),
            like((4 * QUARTER, D), BF16),
            like((1, 16), BF16),
        ],
        [SM] + [VM] * 8,
        (me, *owned, *owners),
        1 << 22,
        [pltpu.VMEM((N_GRP, SPAN + 48, D), BF16), pltpu.VMEM((16, BLOCK, D), F32)],
    )
    top_mine, fresh_scale = lax.optimization_barrier((top_mine, fresh_scale))
    (top_grad,) = call(
        last_kernel,
        [like((2 * D, FF), F32)],
        [SM] + [VM] * 2,
        (core, top_mine, other_core(top_mine)),
        1 << 20,
    )
    return new_master[None], new_accum, fresh, fresh_scale.reshape(16), top_grad


def solution(mesh):
    finer = Mesh(
        mesh.devices.reshape(mesh.shape["grp"], 4, 8, 2), ("grp", "row_0", "row_1", "row_2")
    )
    in_specs = (
        P(ROW, None),
        P(ROW),
        P("grp", ROW),
        P(GRP_ROW, None),
        P(GRP_ROW, None),
        P(GRP_ROW, None),
        P(GRP_ROW),
        P(),
        P(),
        P("grp", ROW, None),
        P("grp", ROW),
    )
    out_specs = (P("grp", ROW, None), P("grp", ROW), P(ROW, None), P(ROW), P())
    return jax.shard_map(
        on_device, mesh=finer, in_specs=in_specs, out_specs=out_specs, check_vma=False
    )
```

```python
import jax
import jax.numpy as jnp
from jax import lax
from jax.experimental import pallas as pl
from jax.experimental.pallas import tpu as pltpu
from jax.sharding import Mesh
from jax.sharding import PartitionSpec as P


ROW = ("row_0", "row_1", "row_2")
CHIPS = ("row_0", "row_1")
GRP_ROW = ("grp", "row_0", "row_1", "row_2")
N_GRP = 4
N_ROW = 64
BLOCK = 128
SPAN = 256
CAP = 8
BAGS = 256
NNZ = 1024
SLOTS = N_ROW * CAP
D = 128
FF = 1024
QUARTER = 512
LR = 0.05
GRANT = 16 << 20
F32 = jnp.float32
BF16 = jnp.bfloat16
I32 = jnp.int32
VM = pl.BlockSpec(memory_space=pltpu.VMEM)
SM = pl.BlockSpec(memory_space=pltpu.SMEM)


def iota(shape, dim):
    return lax.broadcasted_iota(I32, shape, dim)


def dot(a, b, ca=1, cb=0):
    return lax.dot_general(a, b, (((ca,), (cb,)), ((), ())), preferred_element_type=F32)


def ones_where(mask):
    return jnp.where(mask, 1.0, 0.0).astype(BF16)


def call(kernel, outs, specs, args, flops, scratch=()):
    bytes_accessed = sum(a.size * a.dtype.itemsize for a in args) + sum(
        o.size * o.dtype.itemsize for o in outs
    )
    return pl.pallas_call(
        kernel,
        out_shape=outs,
        in_specs=specs,
        out_specs=[VM] * len(outs),
        cost_estimate=pl.CostEstimate(
            flops=flops, bytes_accessed=bytes_accessed, transcendentals=0
        ),
        scratch_shapes=scratch,
        compiler_params=pltpu.CompilerParams(vmem_limit_bytes=GRANT),
    )(*args)


def shard_and_row(idx_ref):
    idx = idx_ref[...]
    shard = lax.shift_right_logical(idx, 8)
    return shard, idx & (SPAN - 1)


def ranks(shard, row):
    in_shard = ones_where(iota((N_ROW, NNZ), 0) == shard)
    at_row = ones_where(iota((SPAN, NNZ), 0) == row)
    used = dot(in_shard, at_row, 1, 1) > 0.5
    before = ones_where(iota((SPAN, SPAN), 0) < iota((SPAN, SPAN), 1))
    return in_shard, used, dot(ones_where(used), before)


def ids_kernel(idx_ref, ids_ref):
    _, used, rank = ranks(*shard_and_row(idx_ref))
    column = iota((N_ROW, SPAN), 1).astype(F32)
    lane = iota((N_ROW, D), 1)
    ids = jnp.zeros((N_ROW, D), F32)
    for k in range(CAP):
        mine = jnp.sum(
            jnp.where(used & (rank == float(k)), column, 0.0), axis=1, keepdims=True
        )
        ids = jnp.where(lane == k, mine, ids)
    ids_ref[...] = ids.astype(I32)


def counts_kernel(idx_ref, len_ref, use_ref, use_t_ref):
    shard, row = shard_and_row(idx_ref)
    in_shard, _, rank = ranks(shard, row)
    rank_at = dot(rank.astype(BF16), in_shard, 0, 0)
    rank = jnp.sum(jnp.where(iota((SPAN, NNZ), 0) == row, rank_at, 0.0), axis=0, keepdims=True)
    slot = shard * CAP + rank.astype(I32)
    at_slot = ones_where(iota((SLOTS, NNZ), 0) == slot)
    lengths = jnp.broadcast_to(len_ref[...].astype(F32), (BAGS, BAGS))
    a, b = iota((BAGS, BAGS), 0), iota((BAGS, BAGS), 1)
    starts = jnp.sum(jnp.where(b < a, lengths, 0.0), axis=1, keepdims=True).astype(I32)
    ends = jnp.sum(jnp.where(b <= a, lengths, 0.0), axis=1, keepdims=True).astype(I32)
    place = iota((BAGS, NNZ), 1)
    in_bag = ones_where((place >= starts) & (place < ends))
    use_ref[...] = dot(in_bag, at_slot, 1, 1).astype(BF16)
    use_t_ref[...] = dot(at_slot, in_bag, 1, 1).astype(BF16)


def table_kernel(hot_ref, serving_ref, scale_ref, table_ref, buf, sem):
    copies = [
        pltpu.make_async_copy(
            serving_ref.at[pl.ds(pl.multiple_of(hot_ref[0, j] * BLOCK, BLOCK), BLOCK)],
            buf.at[j],
            sem.at[j],
        )
        for j in range(2)
    ]
    for c in copies:
        c.start()
    scales = scale_ref[...].astype(F32)
    lane = iota(scales.shape, 1)
    for j, c in enumerate(copies):
        own = jnp.sum(jnp.where(lane == hot_ref[0, j], scales, 0.0), axis=1, keepdims=True)
        c.wait()
        table_ref[j * BLOCK : (j + 1) * BLOCK, :] = (buf[j].astype(F32) * own).astype(BF16)


def pick_kernel(ids_ref, table_ref, rows_ref):
    owner = ones_where(lax.shift_right_logical(iota((SLOTS, N_ROW), 0), 3) == iota((SLOTS, N_ROW), 1))
    spread = dot(owner, ids_ref[...].astype(F32).astype(BF16))
    mine = iota((SLOTS, D), 1) == (iota((SLOTS, D), 0) & (CAP - 1))
    column = jnp.sum(jnp.where(mine, spread, 0.0), axis=1, keepdims=True).astype(I32)
    onehot = ones_where(iota((SLOTS, SPAN), 1) == column)
    rows_ref[...] = dot(onehot, table_ref[...]).astype(BF16)


def place_kernel(ids_ref, place_ref):
    owner = ones_where(lax.shift_right_logical(iota((SLOTS, N_ROW), 0), 3) == iota((SLOTS, N_ROW), 1))
    spread = dot(ids_ref[...].astype(F32).astype(BF16), owner, 0, 1)
    mine = iota((D, SLOTS), 0) == (iota((D, SLOTS), 1) & (CAP - 1))
    line = jnp.sum(jnp.where(mine, spread, 0.0), axis=0, keepdims=True).astype(I32)
    place_ref[...] = ones_where(iota((SPAN, SLOTS), 0) == line)


def dense_kernel(dense_ref, w_ref, labels_ref, w_out_ref, pre_ref, labels_out_ref, w_out_out_ref):
    pre_ref[...] = dot(dense_ref[...], w_ref[D : 2 * D, :])
    a, b = iota((BAGS, BAGS), 0), iota((BAGS, BAGS), 1)
    labels = jnp.sum(
        jnp.where(a == b, jnp.broadcast_to(labels_ref[...], (BAGS, BAGS)), 0.0),
        axis=1,
        keepdims=True,
    )
    labels_out_ref[...] = jnp.broadcast_to(labels, (BAGS, D))
    w_out_out_ref[...] = w_out_ref[...]


def step_kernel(
    core_ref, rows_ref, use_ref, dense_ref, pre_ref, labels_ref, w_ref, w_out_ref,
    give_ref, keep_ref, pooled_grad_ref,
):
    pooled = dot(use_ref[...], rows_ref[...]).astype(BF16)
    pre = pre_ref[...] + dot(pooled, w_ref[0:D, :])
    sig = jax.nn.sigmoid(pre)
    w_out = w_out_ref[...]
    logit = jnp.sum(pre * sig * w_out, axis=1, keepdims=True)
    dlogit = jax.nn.sigmoid(logit) - labels_ref[:, 0:1]
    dpre = (dlogit * w_out * (sig * (1.0 + pre * (1.0 - sig)))).astype(BF16)
    first = core_ref[0] == 0
    dense = dense_ref[...]
    give = dot(jnp.where(first, dense, pooled), dpre, 0, 0).astype(BF16)
    keep = dot(jnp.where(first, pooled, dense), dpre, 0, 0)
    for i in range(8):
        for j in range(8):
            tile = slice(i * 16, (i + 1) * 16), slice(j * 128, (j + 1) * 128)
            give_ref[i * 8 + j] = give[tile]
            keep_ref[i * 8 + j] = keep[tile]
    pooled_grad_ref[...] = dot(dpre, w_ref[0:D, :], 1, 1)


def row_grad_kernel(pooled_grad_ref, use_t_ref, out_ref):
    pooled_grad = pooled_grad_ref[...]
    high = pooled_grad.astype(BF16)
    low = (pooled_grad - high.astype(F32)).astype(BF16)
    use_t = use_t_ref[...]
    out_ref[...] = (dot(use_t, high) + dot(use_t, low)).astype(BF16)


def parts_kernel(keep_ref, given_ref, row_grad_ref, out_ref):
    out_ref[:, 0:16, :] = (keep_ref[...] + given_ref[...].astype(F32)).astype(BF16)
    out_ref[:, 16:24, :] = row_grad_ref[...]


def owned_kernel(got_ref, place_ref, hot_ref, out_ref):
    grads = got_ref[:, :, 16:24, :].astype(F32).reshape(SLOTS, D).astype(BF16)
    out_ref[0:SPAN, :] = dot(place_ref[...], grads).astype(BF16)
    for half in range(2):
        at = SPAN + 16 * half
        out_ref[at : at + 16, :] = jnp.sum(
            got_ref[:, half, 0:16, :].astype(F32), axis=0
        ).astype(BF16)
    lane = iota((16, D), 1)
    hot = jnp.where(lane == 0, hot_ref[0, 0], jnp.where(lane == 1, hot_ref[0, 1], 0))
    out_ref[SPAN + 32 : SPAN + 48, :] = hot.astype(F32).astype(BF16)


def top_kernel(me_ref, x0_ref, x1_ref, x2_ref, x3_ref, top_ref, by_group):
    me = me_ref[0]
    for o, ref in enumerate((x0_ref, x1_ref, x2_ref, x3_ref)):
        by_group[(me - o) & 3] = ref[SPAN : SPAN + 32, :]
    top = jnp.zeros((32, D), F32)
    for g in range(N_GRP):
        top = top + by_group[g].astype(F32)
    top_ref[...] = jnp.broadcast_to(top.astype(BF16)[None], (N_ROW // 2, 32, D))


def update_kernel(
    me_ref, x0_ref, x1_ref, x2_ref, x3_ref, master_ref, accum_ref,
    new_master_ref, new_accum_ref, coded_ref, by_group,
):
    me = me_ref[0]
    for o, ref in enumerate((x0_ref, x1_ref, x2_ref, x3_ref)):
        by_group[(me - o) & 3] = ref[...]
    hot = [by_group[g, SPAN + 32 : SPAN + 48, :].astype(F32)[0:1, :] for g in range(N_GRP)]
    a, b = iota((BLOCK, BLOCK), 0), iota((BLOCK, BLOCK), 1)
    diagonal = a == b
    lane = iota((16, D), 1)
    scale_row = jnp.zeros((16, D), F32)
    for q in range(4):
        grad = jnp.zeros((BLOCK, D), F32)
        number = (me * 4 + q).astype(F32)
        for g in range(N_GRP):
            for j in range(2):
                block = by_group[g, j * BLOCK : (j + 1) * BLOCK, :].astype(F32)
                grad = grad + jnp.where(hot[g][:, j : j + 1] == number, block, 0.0)
        at = pl.ds(q * BLOCK, BLOCK)
        accum = jnp.broadcast_to(accum_ref[:, q * BLOCK : (q + 1) * BLOCK], (BLOCK, BLOCK))
        state = jnp.sum(jnp.where(diagonal, accum, 0.0), axis=1, keepdims=True) + jnp.mean(
            grad * grad, axis=1, keepdims=True
        )
        new_accum_ref[:, q * BLOCK : (q + 1) * BLOCK] = jnp.sum(
            jnp.where(diagonal, jnp.broadcast_to(state, (BLOCK, BLOCK)), 0.0), axis=0, keepdims=True
        )
        weights = master_ref[at, :] - grad * (LR / jnp.sqrt(state))
        new_master_ref[at, :] = weights
        largest = jnp.max(jnp.max(jnp.abs(weights), axis=0, keepdims=True), axis=1, keepdims=True)
        scale = (largest + 1e-06).astype(BF16).astype(F32)
        coded_ref[at, :] = (weights / scale).astype(BF16)
        scale_row = jnp.where(lane == me * 4 + q, scale, scale_row)
    coded_ref[pl.ds(QUARTER, 16), :] = scale_row.astype(BF16)


def fresh_kernel(me_ref, s0_ref, s1_ref, s2_ref, s3_ref, serving_ref, scale_ref):
    me = me_ref[0]
    scales = jnp.zeros((16, D), F32)
    for o, ref in enumerate((s0_ref, s1_ref, s2_ref, s3_ref)):
        start = pl.multiple_of(((me - o) & 3) * QUARTER, QUARTER)
        serving_ref[pl.ds(start, QUARTER), :] = ref[0:QUARTER, :]
        scales = scales + ref[QUARTER : QUARTER + 16, :].astype(F32)
    scale_ref[...] = scales[0:1, 0:16].astype(BF16)


def last_kernel(core_ref, mine_ref, other_ref, top_ref):
    for ref, core in ((mine_ref, core_ref[0]), (other_ref, 1 - core_ref[0])):
        for s in range(N_ROW // 2):
            column = pl.multiple_of((s % 4 * 2 + core) * 128, 128)
            for half in range(2):
                line = half * 128 + s // 4 * 16
                top_ref[line : line + 16, pl.ds(column, 128)] = ref[
                    s, half * 16 : (half + 1) * 16, :
                ].astype(F32)


def like(shape, dtype):
    return jax.ShapeDtypeStruct(shape, dtype)


def over_groups(x):
    return [x] + [
        lax.ppermute(x, "grp", [(g, (g + o) % N_GRP) for g in range(N_GRP)]) for o in (1, 2, 3)
    ]


def other_core(x):
    return lax.ppermute(x, "row_2", [(0, 1), (1, 0)])


def exchange(x, axes=ROW):
    return lax.all_to_all(x, axes, 0, 0, tiled=True)


def on_device(
    serving, serving_scale, hot_blocks, bag_lengths, bag_indices, dense_act, labels, w_top, w_out, master, accum,
):
    me = lax.axis_index("grp").astype(I32).reshape(1)
    core = lax.axis_index("row_2").astype(I32).reshape(1)
    (ids,) = call(ids_kernel, [like((N_ROW, D), I32)], [VM], (bag_indices,), 1 << 26)
    wanted = exchange(ids.reshape(N_ROW, 1, D)).reshape(N_ROW, D)
    use, use_t = call(
        counts_kernel,
        [like((BAGS, SLOTS), BF16), like((SLOTS, BAGS), BF16)],
        [VM] * 2,
        (bag_indices, bag_lengths),
        1 << 29,
    )
    (table,) = call(
        table_kernel,
        [like((SPAN, D), BF16)],
        [SM, pl.BlockSpec(memory_space=pl.ANY), VM],
        (hot_blocks, serving, serving_scale.reshape(1, 16)),
        1 << 20,
        [pltpu.VMEM((2, BLOCK, D), BF16), pltpu.SemaphoreType.DMA((2,))],
    )
    pre, labels_column, w_out_line = call(
        dense_kernel,
        [like((BAGS, FF), F32), like((BAGS, D), F32), like((1, FF), F32)],
        [VM] * 4,
        (dense_act, w_top, labels.reshape(1, BAGS), w_out.reshape(1, FF)),
        1 << 27,
    )
    wanted, table, pre, labels_column, w_out_line = lax.optimization_barrier(
        (wanted, table, pre, labels_column, w_out_line)
    )
    (rows,) = call(pick_kernel, [like((SLOTS, D), BF16)], [VM] * 2, (wanted, table), 1 << 26)
    fetched = exchange(rows.reshape(N_ROW, CAP, D)).reshape(SLOTS, D)
    (place,) = call(place_kernel, [like((SPAN, SLOTS), BF16)], [VM], (wanted,), 1 << 26)
    give, keep, pooled_grad = call(
        step_kernel,
        [like((N_ROW, 16, D), BF16), like((N_ROW, 16, D), F32), like((BAGS, D), F32)],
        [SM] + [VM] * 7,
        (core, fetched, use, dense_act, pre, labels_column, w_top, w_out_line),
        1 << 29,
    )
    given = other_core(give)
    (row_grad,) = call(
        row_grad_kernel, [like((SLOTS, D), BF16)], [VM] * 2, (pooled_grad, use_t), 1 << 27
    )
    (parts,) = call(
        parts_kernel,
        [like((N_ROW, 24, D), BF16)],
        [VM] * 3,
        (keep, given, row_grad.reshape(N_ROW, CAP, D)),
        1 << 20,
    )
    got = exchange(parts)
    (own,) = call(
        owned_kernel,
        [like((SPAN + 48, D), BF16)],
        [VM, VM, SM],
        (got.reshape(N_ROW // 2, 2, 24, D), place, hot_blocks),
        1 << 26,
    )
    owned = over_groups(own)
    (top_part,) = call(
        top_kernel,
        [like((N_ROW // 2, 32, D), BF16)],
        [SM] + [VM] * 4,
        (me, *owned),
        1 << 16,
        [pltpu.VMEM((N_GRP, 32, D), BF16)],
    )
    top_mine = exchange(top_part, CHIPS)
    new_master, new_accum, coded = call(
        update_kernel,
        [like((QUARTER, D), F32), like((1, QUARTER), F32), like((QUARTER + 16, D), BF16)],
        [SM] + [VM] * 6,
        (me, *owned, master[0], accum),
        1 << 22,
        [pltpu.VMEM((N_GRP, SPAN + 48, D), BF16)],
    )
    quarters = over_groups(coded)
    fresh, fresh_scale = call(
        fresh_kernel,
        [like((4 * QUARTER, D), BF16), like((1, 16), BF16)],
        [SM] + [VM] * 4,
        (me, *quarters),
        1 << 20,
    )
    top_other = other_core(top_mine)
    (top_grad,) = call(
        last_kernel, [like((2 * D, FF), F32)], [SM] + [VM] * 2, (core, top_mine, top_other), 1 << 20
    )
    return new_master[None], new_accum, fresh, fresh_scale.reshape(16), top_grad


def solution(mesh):
    finer = Mesh(
        mesh.devices.reshape(mesh.shape["grp"], 4, 8, 2), ("grp", "row_0", "row_1", "row_2")
    )
    in_specs = (
        P(ROW, None),
        P(ROW),
        P("grp", ROW),
        P(GRP_ROW, None),
        P(GRP_ROW, None),
        P(GRP_ROW, None),
        P(GRP_ROW),
        P(),
        P(),
        P("grp", ROW, None),
        P("grp", ROW),
    )
    out_specs = (P("grp", ROW, None), P("grp", ROW), P(ROW, None), P(ROW), P())
    return jax.shard_map(
        on_device, mesh=finer, in_specs=in_specs, out_specs=out_specs, check_vma=False
    )
```

```python
import jax
import jax.numpy as jnp
from jax import lax
from jax.experimental import pallas as pl
from jax.experimental.pallas import tpu as pltpu
from jax.sharding import Mesh
from jax.sharding import PartitionSpec as P


ROW = ("row_0", "row_1", "row_2")
CHIPS = ("row_0", "row_1")
GRP_ROW = ("grp", "row_0", "row_1", "row_2")
N_GRP = 4
N_ROW = 64
BLOCK = 128
SPAN = 256
CAP = 8
BAGS = 256
NNZ = 1024
SLOTS = N_ROW * CAP
D = 128
FF = 1024
QUARTER = 512
LR = 0.05
GRANT = 16 << 20
F32 = jnp.float32
BF16 = jnp.bfloat16
I32 = jnp.int32
VM = pl.BlockSpec(memory_space=pltpu.VMEM)
SM = pl.BlockSpec(memory_space=pltpu.SMEM)


def iota(shape, dim):
    return lax.broadcasted_iota(I32, shape, dim)


def dot(a, b, ca=1, cb=0):
    return lax.dot_general(a, b, (((ca,), (cb,)), ((), ())), preferred_element_type=F32)


def ones_where(mask):
    return jnp.where(mask, 1.0, 0.0).astype(BF16)


def call(kernel, outs, specs, args, flops, scratch=()):
    bytes_accessed = sum(a.size * a.dtype.itemsize for a in args) + sum(
        o.size * o.dtype.itemsize for o in outs
    )
    return pl.pallas_call(
        kernel,
        out_shape=outs,
        in_specs=specs,
        out_specs=[VM] * len(outs),
        cost_estimate=pl.CostEstimate(
            flops=flops, bytes_accessed=bytes_accessed, transcendentals=0
        ),
        scratch_shapes=scratch,
        compiler_params=pltpu.CompilerParams(vmem_limit_bytes=GRANT),
    )(*args)


def shard_and_row(idx_ref):
    idx = idx_ref[...]
    shard = lax.shift_right_logical(idx, 8)
    return shard, idx & (SPAN - 1)


def ranks(shard, row):
    in_shard = ones_where(iota((N_ROW, NNZ), 0) == shard)
    at_row = ones_where(iota((SPAN, NNZ), 0) == row)
    used = dot(in_shard, at_row, 1, 1) > 0.5
    before = ones_where(iota((SPAN, SPAN), 0) < iota((SPAN, SPAN), 1))
    return in_shard, used, dot(ones_where(used), before)


def ids_kernel(idx_ref, ids_ref):
    _, used, rank = ranks(*shard_and_row(idx_ref))
    column = iota((N_ROW, SPAN), 1).astype(F32)
    lane = iota((N_ROW, D), 1)
    ids = jnp.zeros((N_ROW, D), F32)
    for k in range(CAP):
        mine = jnp.sum(
            jnp.where(used & (rank == float(k)), column, 0.0), axis=1, keepdims=True
        )
        ids = jnp.where(lane == k, mine, ids)
    ids_ref[...] = ids.astype(I32)


def counts_kernel(idx_ref, len_ref, use_ref, use_t_ref):
    shard, row = shard_and_row(idx_ref)
    in_shard, _, rank = ranks(shard, row)
    rank_at = dot(rank.astype(BF16), in_shard, 0, 0)
    rank = jnp.sum(jnp.where(iota((SPAN, NNZ), 0) == row, rank_at, 0.0), axis=0, keepdims=True)
    slot = shard * CAP + rank.astype(I32)
    at_slot = ones_where(iota((SLOTS, NNZ), 0) == slot)
    lengths = jnp.broadcast_to(len_ref[...].astype(F32), (BAGS, BAGS))
    a, b = iota((BAGS, BAGS), 0), iota((BAGS, BAGS), 1)
    starts = jnp.sum(jnp.where(b < a, lengths, 0.0), axis=1, keepdims=True).astype(I32)
    ends = jnp.sum(jnp.where(b <= a, lengths, 0.0), axis=1, keepdims=True).astype(I32)
    place = iota((BAGS, NNZ), 1)
    in_bag = ones_where((place >= starts) & (place < ends))
    use_ref[...] = dot(in_bag, at_slot, 1, 1).astype(BF16)
    use_t_ref[...] = dot(at_slot, in_bag, 1, 1).astype(BF16)


def table_kernel(hot_ref, serving_ref, scale_ref, table_ref, buf, sem):
    copies = [
        pltpu.make_async_copy(
            serving_ref.at[pl.ds(pl.multiple_of(hot_ref[0, j] * BLOCK, BLOCK), BLOCK)],
            buf.at[j],
            sem.at[j],
        )
        for j in range(2)
    ]
    for c in copies:
        c.start()
    scales = scale_ref[...].astype(F32)
    lane = iota(scales.shape, 1)
    for j, c in enumerate(copies):
        own = jnp.sum(jnp.where(lane == hot_ref[0, j], scales, 0.0), axis=1, keepdims=True)
        c.wait()
        table_ref[j * BLOCK : (j + 1) * BLOCK, :] = (buf[j].astype(F32) * own).astype(BF16)


def pick_kernel(core_ref, ids_ref, table_ref, other_ref, rows_ref):
    owner = ones_where(lax.shift_right_logical(iota((SLOTS, N_ROW), 0), 3) == iota((SLOTS, N_ROW), 1))
    spread = dot(owner, ids_ref[...].astype(F32).astype(BF16))
    mine = iota((SLOTS, D), 1) == (iota((SLOTS, D), 0) & (CAP - 1))
    column = jnp.sum(jnp.where(mine, spread, 0.0), axis=1, keepdims=True).astype(I32)
    here = lax.shift_right_logical(iota((SLOTS, SPAN), 0), 3) & 1 == core_ref[0]
    match = iota((SLOTS, SPAN), 1) == column
    rows = dot(ones_where(match & here), table_ref[...])
    rows_ref[...] = (rows + dot(ones_where(match & ~here), other_ref[...])).astype(BF16)


def place_kernel(core_ref, ids_ref, other_ref, place_ref):
    slot = iota((SLOTS, N_ROW), 0)
    line = lax.shift_right_logical(slot, 4) * 2 + core_ref[0] == iota((SLOTS, N_ROW), 1)
    here = lax.shift_right_logical(slot, 3) & 1 == core_ref[0]
    spread = dot(ids_ref[...].astype(F32).astype(BF16), ones_where(line & here), 0, 1)
    spread = spread + dot(other_ref[...].astype(F32).astype(BF16), ones_where(line & ~here), 0, 1)
    mine = iota((D, SLOTS), 0) == (iota((D, SLOTS), 1) & (CAP - 1))
    line = jnp.sum(jnp.where(mine, spread, 0.0), axis=0, keepdims=True).astype(I32)
    place_ref[...] = ones_where(iota((SPAN, SLOTS), 0) == line)


def dense_kernel(dense_ref, w_ref, labels_ref, w_out_ref, pre_ref, labels_out_ref, w_out_out_ref):
    pre_ref[...] = dot(dense_ref[...], w_ref[D : 2 * D, :])
    a, b = iota((BAGS, BAGS), 0), iota((BAGS, BAGS), 1)
    labels = jnp.sum(
        jnp.where(a == b, jnp.broadcast_to(labels_ref[...], (BAGS, BAGS)), 0.0),
        axis=1,
        keepdims=True,
    )
    labels_out_ref[...] = jnp.broadcast_to(labels, (BAGS, D))
    w_out_out_ref[...] = w_out_ref[...]


def step_kernel(
    core_ref, rows_ref, use_ref, dense_ref, pre_ref, labels_ref, w_ref, w_out_ref,
    give_ref, keep_ref, pooled_grad_ref,
):
    pooled = dot(use_ref[...], rows_ref[...]).astype(BF16)
    pre = pre_ref[...] + dot(pooled, w_ref[0:D, :])
    sig = jax.nn.sigmoid(pre)
    w_out = w_out_ref[...]
    logit = jnp.sum(pre * sig * w_out, axis=1, keepdims=True)
    dlogit = jax.nn.sigmoid(logit) - labels_ref[:, 0:1]
    dpre = (dlogit * w_out * (sig * (1.0 + pre * (1.0 - sig)))).astype(BF16)
    first = core_ref[0] == 0
    dense = dense_ref[...]
    give = dot(jnp.where(first, dense, pooled), dpre, 0, 0).astype(BF16)
    keep = dot(jnp.where(first, pooled, dense), dpre, 0, 0)
    for i in range(8):
        for j in range(8):
            tile = slice(i * 16, (i + 1) * 16), slice(j * 128, (j + 1) * 128)
            give_ref[i * 8 + j] = give[tile]
            keep_ref[i * 8 + j] = keep[tile]
    pooled_grad_ref[...] = dot(dpre, w_ref[0:D, :], 1, 1)


def row_grad_kernel(pooled_grad_ref, use_t_ref, out_ref):
    pooled_grad = pooled_grad_ref[...]
    high = pooled_grad.astype(BF16)
    low = (pooled_grad - high.astype(F32)).astype(BF16)
    use_t = use_t_ref[...]
    out_ref[...] = (dot(use_t, high) + dot(use_t, low)).astype(BF16)


def parts_kernel(keep_ref, given_ref, row_grad_ref, out_ref):
    out_ref[:, 0:16, :] = (keep_ref[...] + given_ref[...].astype(F32)).astype(BF16)
    out_ref[:, 16:24, :] = row_grad_ref[...]


def owned_kernel(got_ref, place_ref, hot_ref, out_ref):
    grads = got_ref[:, :, 16:24, :].astype(F32).reshape(SLOTS, D).astype(BF16)
    out_ref[0:SPAN, :] = dot(place_ref[...], grads).astype(BF16)
    for half in range(2):
        at = SPAN + 16 * half
        out_ref[at : at + 16, :] = jnp.sum(
            got_ref[:, half, 0:16, :].astype(F32), axis=0
        ).astype(BF16)
    lane = iota((16, D), 1)
    hot = jnp.where(lane == 0, hot_ref[0, 0], jnp.where(lane == 1, hot_ref[0, 1], 0))
    out_ref[SPAN + 32 : SPAN + 48, :] = hot.astype(F32).astype(BF16)


def top_kernel(me_ref, x0_ref, x1_ref, x2_ref, x3_ref, top_ref, by_group):
    me = me_ref[0]
    for o, ref in enumerate((x0_ref, x1_ref, x2_ref, x3_ref)):
        by_group[(me - o) & 3] = ref[SPAN : SPAN + 32, :]
    top = jnp.zeros((32, D), F32)
    for g in range(N_GRP):
        top = top + by_group[g].astype(F32)
    top_ref[...] = jnp.broadcast_to(top.astype(BF16)[None], (N_ROW // 2, 32, D))


def update_kernel(
    me_ref, x0_ref, x1_ref, x2_ref, x3_ref, master_ref, accum_ref,
    new_master_ref, new_accum_ref, coded_ref, by_group,
):
    me = me_ref[0]
    for o, ref in enumerate((x0_ref, x1_ref, x2_ref, x3_ref)):
        by_group[(me - o) & 3] = ref[...]
    hot = [by_group[g, SPAN + 32 : SPAN + 48, :].astype(F32)[0:1, :] for g in range(N_GRP)]
    a, b = iota((BLOCK, BLOCK), 0), iota((BLOCK, BLOCK), 1)
    diagonal = a == b
    lane = iota((16, D), 1)
    scale_row = jnp.zeros((16, D), F32)
    for q in range(4):
        grad = jnp.zeros((BLOCK, D), F32)
        number = (me * 4 + q).astype(F32)
        for g in range(N_GRP):
            for j in range(2):
                block = by_group[g, j * BLOCK : (j + 1) * BLOCK, :].astype(F32)
                grad = grad + jnp.where(hot[g][:, j : j + 1] == number, block, 0.0)
        at = pl.ds(q * BLOCK, BLOCK)
        accum = jnp.broadcast_to(accum_ref[:, q * BLOCK : (q + 1) * BLOCK], (BLOCK, BLOCK))
        state = jnp.sum(jnp.where(diagonal, accum, 0.0), axis=1, keepdims=True) + jnp.mean(
            grad * grad, axis=1, keepdims=True
        )
        new_accum_ref[:, q * BLOCK : (q + 1) * BLOCK] = jnp.sum(
            jnp.where(diagonal, jnp.broadcast_to(state, (BLOCK, BLOCK)), 0.0), axis=0, keepdims=True
        )
        weights = master_ref[at, :] - grad * (LR / jnp.sqrt(state))
        new_master_ref[at, :] = weights
        largest = jnp.max(jnp.max(jnp.abs(weights), axis=0, keepdims=True), axis=1, keepdims=True)
        scale = (largest + 1e-06).astype(BF16).astype(F32)
        coded_ref[at, :] = (weights / scale).astype(BF16)
        scale_row = jnp.where(lane == me * 4 + q, scale, scale_row)
    coded_ref[pl.ds(QUARTER, 16), :] = scale_row.astype(BF16)


def fresh_kernel(me_ref, s0_ref, s1_ref, s2_ref, s3_ref, serving_ref, scale_ref):
    me = me_ref[0]
    scales = jnp.zeros((16, D), F32)
    for o, ref in enumerate((s0_ref, s1_ref, s2_ref, s3_ref)):
        start = pl.multiple_of(((me - o) & 3) * QUARTER, QUARTER)
        serving_ref[pl.ds(start, QUARTER), :] = ref[0:QUARTER, :]
        scales = scales + ref[QUARTER : QUARTER + 16, :].astype(F32)
    scale_ref[...] = scales[0:1, 0:16].astype(BF16)


def last_kernel(core_ref, mine_ref, other_ref, top_ref):
    for ref, core in ((mine_ref, core_ref[0]), (other_ref, 1 - core_ref[0])):
        for s in range(N_ROW // 2):
            column = pl.multiple_of((s % 4 * 2 + core) * 128, 128)
            for half in range(2):
                line = half * 128 + s // 4 * 16
                top_ref[line : line + 16, pl.ds(column, 128)] = ref[
                    s, half * 16 : (half + 1) * 16, :
                ].astype(F32)


def like(shape, dtype):
    return jax.ShapeDtypeStruct(shape, dtype)


def over_groups(x):
    parts = [x]
    for o in (1, 2, 3):
        parts.append(lax.ppermute(x, "grp", [(g, (g + o) % N_GRP) for g in range(N_GRP)]))
    return parts


def other_core(x):
    return lax.ppermute(x, "row_2", [(0, 1), (1, 0)])


def exchange(x, axes=ROW):
    return lax.all_to_all(x, axes, 0, 0, tiled=True)


def on_device(
    serving, serving_scale, hot_blocks, bag_lengths, bag_indices, dense_act, labels, w_top, w_out, master, accum,
):
    me = lax.axis_index("grp").astype(I32).reshape(1)
    core = lax.axis_index("row_2").astype(I32).reshape(1)
    (ids,) = call(ids_kernel, [like((N_ROW, D), I32)], [VM], (bag_indices,), 1 << 26)
    wanted = exchange(ids.reshape(N_ROW // 2, 2, D), CHIPS).reshape(N_ROW, D)
    use, use_t = call(
        counts_kernel,
        [like((BAGS, SLOTS), BF16), like((SLOTS, BAGS), BF16)],
        [VM] * 2,
        (bag_indices, bag_lengths),
        1 << 29,
    )
    (table,) = call(
        table_kernel,
        [like((SPAN, D), BF16)],
        [SM, pl.BlockSpec(memory_space=pl.ANY), VM],
        (hot_blocks, serving, serving_scale.reshape(1, 16)),
        1 << 20,
        [pltpu.VMEM((2, BLOCK, D), BF16), pltpu.SemaphoreType.DMA((2,))],
    )
    pre, labels_column, w_out_line = call(
        dense_kernel,
        [like((BAGS, FF), F32), like((BAGS, D), F32), like((1, FF), F32)],
        [VM] * 4,
        (dense_act, w_top, labels.reshape(1, BAGS), w_out.reshape(1, FF)),
        1 << 27,
    )
    other_table = other_core(table)
    wanted, table, other_table, pre, labels_column, w_out_line = lax.optimization_barrier(
        (wanted, table, other_table, pre, labels_column, w_out_line)
    )
    (rows,) = call(
        pick_kernel,
        [like((SLOTS, D), BF16)],
        [SM] + [VM] * 3,
        (core, wanted, table, other_table),
        1 << 26,
    )
    fetched = exchange(rows.reshape(N_ROW // 2, 2 * CAP, D), CHIPS).reshape(SLOTS, D)
    other_wanted = other_core(wanted)
    (place,) = call(
        place_kernel,
        [like((SPAN, SLOTS), BF16)],
        [SM] + [VM] * 2,
        (core, wanted, other_wanted),
        1 << 26,
    )
    give, keep, pooled_grad = call(
        step_kernel,
        [like((N_ROW, 16, D), BF16), like((N_ROW, 16, D), F32), like((BAGS, D), F32)],
        [SM] + [VM] * 7,
        (core, fetched, use, dense_act, pre, labels_column, w_top, w_out_line),
        1 << 29,
    )
    given = other_core(give)
    (row_grad,) = call(
        row_grad_kernel, [like((SLOTS, D), BF16)], [VM] * 2, (pooled_grad, use_t), 1 << 27
    )
    (parts,) = call(
        parts_kernel,
        [like((N_ROW, 24, D), BF16)],
        [VM] * 3,
        (keep, given, row_grad.reshape(N_ROW, CAP, D)),
        1 << 20,
    )
    got = exchange(parts)
    (own,) = call(
        owned_kernel,
        [like((SPAN + 48, D), BF16)],
        [VM, VM, SM],
        (got.reshape(N_ROW // 2, 2, 24, D), place, hot_blocks),
        1 << 26,
    )
    owned = over_groups(own)
    (top_part,) = call(
        top_kernel,
        [like((N_ROW // 2, 32, D), BF16)],
        [SM] + [VM] * 4,
        (me, *owned),
        1 << 16,
        [pltpu.VMEM((N_GRP, 32, D), BF16)],
    )
    top_mine = exchange(top_part, CHIPS)
    new_master, new_accum, coded = call(
        update_kernel,
        [like((QUARTER, D), F32), like((1, QUARTER), F32), like((QUARTER + 16, D), BF16)],
        [SM] + [VM] * 6,
        (me, *owned, master[0], accum),
        1 << 22,
        [pltpu.VMEM((N_GRP, SPAN + 48, D), BF16)],
    )
    quarters = over_groups(coded)
    fresh, fresh_scale = call(
        fresh_kernel,
        [like((4 * QUARTER, D), BF16), like((1, 16), BF16)],
        [SM] + [VM] * 4,
        (me, *quarters),
        1 << 20,
    )
    top_other = other_core(top_mine)
    (top_grad,) = call(
        last_kernel, [like((2 * D, FF), F32)], [SM] + [VM] * 2, (core, top_mine, top_other), 1 << 20
    )
    return new_master[None], new_accum, fresh, fresh_scale.reshape(16), top_grad


def solution(mesh):
    finer = Mesh(
        mesh.devices.reshape(mesh.shape["grp"], 4, 8, 2), ("grp", "row_0", "row_1", "row_2")
    )
    in_specs = (
        P(ROW, None),
        P(ROW),
        P("grp", ROW),
        P(GRP_ROW, None),
        P(GRP_ROW, None),
        P(GRP_ROW, None),
        P(GRP_ROW),
        P(),
        P(),
        P("grp", ROW, None),
        P("grp", ROW),
    )
    out_specs = (P("grp", ROW, None), P("grp", ROW), P(ROW, None), P(ROW), P())
    return jax.shard_map(
        on_device, mesh=finer, in_specs=in_specs, out_specs=out_specs, check_vma=False
    )
```

```python
import jax
import jax.numpy as jnp
from jax import lax
from jax.experimental import pallas as pl
from jax.experimental.pallas import tpu as pltpu
from jax.sharding import Mesh
from jax.sharding import PartitionSpec as P


ROW = ("row_0", "row_1", "row_2")
CHIPS = ("row_0", "row_1")
GRP_ROW = ("grp", "row_0", "row_1", "row_2")
N_GRP = 4
N_ROW = 64
BLOCK = 128
SPAN = 256
CAP = 8
BAGS = 256
NNZ = 1024
SLOTS = N_ROW * CAP
D = 128
FF = 1024
QUARTER = 512
LR = 0.05
GRANT = 16 << 20
F32 = jnp.float32
BF16 = jnp.bfloat16
I32 = jnp.int32
VM = pl.BlockSpec(memory_space=pltpu.VMEM)
SM = pl.BlockSpec(memory_space=pltpu.SMEM)


def iota(shape, dim):
    return lax.broadcasted_iota(I32, shape, dim)


def dot(a, b, ca=1, cb=0):
    return lax.dot_general(a, b, (((ca,), (cb,)), ((), ())), preferred_element_type=F32)


def ones_where(mask):
    return jnp.where(mask, 1.0, 0.0).astype(BF16)


def call(kernel, outs, specs, args, flops, scratch=()):
    bytes_accessed = sum(a.size * a.dtype.itemsize for a in args) + sum(
        o.size * o.dtype.itemsize for o in outs
    )
    return pl.pallas_call(
        kernel,
        out_shape=outs,
        in_specs=specs,
        out_specs=[VM] * len(outs),
        cost_estimate=pl.CostEstimate(
            flops=flops, bytes_accessed=bytes_accessed, transcendentals=0
        ),
        scratch_shapes=scratch,
        compiler_params=pltpu.CompilerParams(vmem_limit_bytes=GRANT),
    )(*args)


def shard_and_row(idx_ref):
    idx = idx_ref[...]
    shard = lax.shift_right_logical(idx, 8)
    return shard, idx & (SPAN - 1)


def ranks(shard, row):
    in_shard = ones_where(iota((N_ROW, NNZ), 0) == shard)
    at_row = ones_where(iota((SPAN, NNZ), 0) == row)
    used = dot(in_shard, at_row, 1, 1) > 0.5
    before = ones_where(iota((SPAN, SPAN), 0) < iota((SPAN, SPAN), 1))
    return in_shard, used, dot(ones_where(used), before)


def ids_kernel(idx_ref, ids_ref):
    _, used, rank = ranks(*shard_and_row(idx_ref))
    column = iota((N_ROW, SPAN), 1).astype(F32)
    lane = iota((N_ROW, D), 1)
    ids = jnp.zeros((N_ROW, D), F32)
    for k in range(CAP):
        mine = jnp.sum(
            jnp.where(used & (rank == float(k)), column, 0.0), axis=1, keepdims=True
        )
        ids = jnp.where(lane == k, mine, ids)
    ids_ref[...] = ids.astype(I32)


def counts_kernel(idx_ref, len_ref, use_ref, use_t_ref):
    shard, row = shard_and_row(idx_ref)
    in_shard, _, rank = ranks(shard, row)
    rank_at = dot(rank.astype(BF16), in_shard, 0, 0)
    rank = jnp.sum(jnp.where(iota((SPAN, NNZ), 0) == row, rank_at, 0.0), axis=0, keepdims=True)
    slot = shard * CAP + rank.astype(I32)
    at_slot = ones_where(iota((SLOTS, NNZ), 0) == slot)
    lengths = jnp.broadcast_to(len_ref[...].astype(F32), (BAGS, BAGS))
    a, b = iota((BAGS, BAGS), 0), iota((BAGS, BAGS), 1)
    starts = jnp.sum(jnp.where(b < a, lengths, 0.0), axis=1, keepdims=True).astype(I32)
    ends = jnp.sum(jnp.where(b <= a, lengths, 0.0), axis=1, keepdims=True).astype(I32)
    place = iota((BAGS, NNZ), 1)
    in_bag = ones_where((place >= starts) & (place < ends))
    use_ref[...] = dot(in_bag, at_slot, 1, 1).astype(BF16)
    use_t_ref[...] = dot(at_slot, in_bag, 1, 1).astype(BF16)


def table_kernel(hot_ref, serving_ref, scale_ref, table_ref, buf, sem):
    copies = [
        pltpu.make_async_copy(
            serving_ref.at[pl.ds(pl.multiple_of(hot_ref[0, j] * BLOCK, BLOCK), BLOCK)],
            buf.at[j],
            sem.at[j],
        )
        for j in range(2)
    ]
    for c in copies:
        c.start()
    scales = scale_ref[...].astype(F32)
    lane = iota(scales.shape, 1)
    for j, c in enumerate(copies):
        own = jnp.sum(jnp.where(lane == hot_ref[0, j], scales, 0.0), axis=1, keepdims=True)
        c.wait()
        table_ref[j * BLOCK : (j + 1) * BLOCK, :] = (buf[j].astype(F32) * own).astype(BF16)


def pick_kernel(core_ref, ids_ref, table_ref, other_ref, rows_ref):
    owner = ones_where(lax.shift_right_logical(iota((SLOTS, N_ROW), 0), 3) == iota((SLOTS, N_ROW), 1))
    spread = dot(owner, ids_ref[...].astype(F32).astype(BF16))
    mine = iota((SLOTS, D), 1) == (iota((SLOTS, D), 0) & (CAP - 1))
    column = jnp.sum(jnp.where(mine, spread, 0.0), axis=1, keepdims=True).astype(I32)
    here = lax.shift_right_logical(iota((SLOTS, SPAN), 0), 3) & 1 == core_ref[0]
    match = iota((SLOTS, SPAN), 1) == column
    rows = dot(ones_where(match & here), table_ref[...])
    rows_ref[...] = (rows + dot(ones_where(match & ~here), other_ref[...])).astype(BF16)


def place_kernel(core_ref, ids_ref, other_ref, place_ref):
    slot = iota((SLOTS, N_ROW), 0)
    line = lax.shift_right_logical(slot, 4) * 2 + core_ref[0] == iota((SLOTS, N_ROW), 1)
    here = lax.shift_right_logical(slot, 3) & 1 == core_ref[0]
    spread = dot(ids_ref[...].astype(F32).astype(BF16), ones_where(line & here), 0, 1)
    spread = spread + dot(other_ref[...].astype(F32).astype(BF16), ones_where(line & ~here), 0, 1)
    mine = iota((D, SLOTS), 0) == (iota((D, SLOTS), 1) & (CAP - 1))
    line = jnp.sum(jnp.where(mine, spread, 0.0), axis=0, keepdims=True).astype(I32)
    place_ref[...] = ones_where(iota((SPAN, SLOTS), 0) == line)


def dense_kernel(dense_ref, w_ref, labels_ref, w_out_ref, pre_ref, labels_out_ref, w_out_out_ref):
    pre_ref[...] = dot(dense_ref[...], w_ref[D : 2 * D, :])
    a, b = iota((BAGS, BAGS), 0), iota((BAGS, BAGS), 1)
    labels = jnp.sum(
        jnp.where(a == b, jnp.broadcast_to(labels_ref[...], (BAGS, BAGS)), 0.0),
        axis=1,
        keepdims=True,
    )
    labels_out_ref[...] = jnp.broadcast_to(labels, (BAGS, D))
    w_out_out_ref[...] = w_out_ref[...]


def by_tile(ref, value):
    for i in range(8):
        for j in range(8):
            ref[i * 8 + j] = value[i * 16 : (i + 1) * 16, j * 128 : (j + 1) * 128]


def step_kernel(
    core_ref, rows_ref, use_ref, dense_ref, pre_ref, labels_ref, w_ref, w_out_ref,
    give_ref, keep_ref, dpre_ref,
):
    pooled = dot(use_ref[...], rows_ref[...]).astype(BF16)
    pre = pre_ref[...] + dot(pooled, w_ref[0:D, :])
    sig = jax.nn.sigmoid(pre)
    w_out = w_out_ref[...]
    logit = jnp.sum(pre * sig * w_out, axis=1, keepdims=True)
    dlogit = jax.nn.sigmoid(logit) - labels_ref[:, 0:1]
    dpre = (dlogit * w_out * (sig * (1.0 + pre * (1.0 - sig)))).astype(BF16)
    dpre_ref[...] = dpre
    first = core_ref[0] == 0
    dense = dense_ref[...]
    by_tile(give_ref, dot(jnp.where(first, dense, pooled), dpre, 0, 0).astype(BF16))
    keep_ref[...] = jnp.where(first, pooled, dense)


def rest_kernel(keep_ref, dpre_ref, w_ref, use_t_ref, kept_ref, out_ref):
    dpre = dpre_ref[...]
    pooled_grad = dot(dpre, w_ref[0:D, :], 1, 1)
    high = pooled_grad.astype(BF16)
    low = (pooled_grad - high.astype(F32)).astype(BF16)
    use_t = use_t_ref[...]
    out_ref[...] = (dot(use_t, high) + dot(use_t, low)).astype(BF16)
    by_tile(kept_ref, dot(keep_ref[...], dpre, 0, 0))


def parts_kernel(keep_ref, given_ref, row_grad_ref, out_ref):
    out_ref[:, 0:16, :] = (keep_ref[...] + given_ref[...].astype(F32)).astype(BF16)
    out_ref[:, 16:24, :] = row_grad_ref[...]


def owned_kernel(got_ref, place_ref, hot_ref, out_ref):
    grads = got_ref[:, :, 16:24, :].astype(F32).reshape(SLOTS, D).astype(BF16)
    out_ref[0:SPAN, :] = dot(place_ref[...], grads).astype(BF16)
    for half in range(2):
        at = SPAN + 16 * half
        out_ref[at : at + 16, :] = jnp.sum(
            got_ref[:, half, 0:16, :].astype(F32), axis=0
        ).astype(BF16)
    lane = iota((16, D), 1)
    hot = jnp.where(lane == 0, hot_ref[0, 0], jnp.where(lane == 1, hot_ref[0, 1], 0))
    out_ref[SPAN + 32 : SPAN + 48, :] = hot.astype(F32).astype(BF16)


def top_kernel(me_ref, x0_ref, x1_ref, x2_ref, x3_ref, top_ref, by_group):
    me = me_ref[0]
    for o, ref in enumerate((x0_ref, x1_ref, x2_ref, x3_ref)):
        by_group[(me - o) & 3] = ref[SPAN : SPAN + 32, :]
    top = jnp.zeros((32, D), F32)
    for g in range(N_GRP):
        top = top + by_group[g].astype(F32)
    top_ref[...] = jnp.broadcast_to(top.astype(BF16)[None], (N_ROW // 2, 32, D))


def update_kernel(
    me_ref, x0_ref, x1_ref, x2_ref, x3_ref, master_ref, accum_ref,
    new_master_ref, new_accum_ref, coded_ref, by_group,
):
    me = me_ref[0]
    for o, ref in enumerate((x0_ref, x1_ref, x2_ref, x3_ref)):
        by_group[(me - o) & 3] = ref[...]
    hot = [by_group[g, SPAN + 32 : SPAN + 48, :].astype(F32)[0:1, :] for g in range(N_GRP)]
    a, b = iota((BLOCK, BLOCK), 0), iota((BLOCK, BLOCK), 1)
    diagonal = a == b
    lane = iota((16, D), 1)
    scale_row = jnp.zeros((16, D), F32)
    for q in range(4):
        grad = jnp.zeros((BLOCK, D), F32)
        number = (me * 4 + q).astype(F32)
        for g in range(N_GRP):
            for j in range(2):
                block = by_group[g, j * BLOCK : (j + 1) * BLOCK, :].astype(F32)
                grad = grad + jnp.where(hot[g][:, j : j + 1] == number, block, 0.0)
        at = pl.ds(q * BLOCK, BLOCK)
        accum = jnp.broadcast_to(accum_ref[:, q * BLOCK : (q + 1) * BLOCK], (BLOCK, BLOCK))
        state = jnp.sum(jnp.where(diagonal, accum, 0.0), axis=1, keepdims=True) + jnp.mean(
            grad * grad, axis=1, keepdims=True
        )
        new_accum_ref[:, q * BLOCK : (q + 1) * BLOCK] = jnp.sum(
            jnp.where(diagonal, jnp.broadcast_to(state, (BLOCK, BLOCK)), 0.0), axis=0, keepdims=True
        )
        weights = master_ref[at, :] - grad * (LR / jnp.sqrt(state))
        new_master_ref[at, :] = weights
        largest = jnp.max(jnp.max(jnp.abs(weights), axis=0, keepdims=True), axis=1, keepdims=True)
        scale = (largest + 1e-06).astype(BF16).astype(F32)
        coded_ref[at, :] = (weights / scale).astype(BF16)
        scale_row = jnp.where(lane == me * 4 + q, scale, scale_row)
    coded_ref[pl.ds(QUARTER, 16), :] = scale_row.astype(BF16)


def fresh_kernel(me_ref, s0_ref, s1_ref, s2_ref, s3_ref, serving_ref, scale_ref):
    me = me_ref[0]
    scales = jnp.zeros((16, D), F32)
    for o, ref in enumerate((s0_ref, s1_ref, s2_ref, s3_ref)):
        start = pl.multiple_of(((me - o) & 3) * QUARTER, QUARTER)
        serving_ref[pl.ds(start, QUARTER), :] = ref[0:QUARTER, :]
        scales = scales + ref[QUARTER : QUARTER + 16, :].astype(F32)
    scale_ref[...] = scales[0:1, 0:16].astype(BF16)


def last_kernel(core_ref, mine_ref, other_ref, top_ref):
    for ref, core in ((mine_ref, core_ref[0]), (other_ref, 1 - core_ref[0])):
        for s in range(N_ROW // 2):
            column = pl.multiple_of((s % 4 * 2 + core) * 128, 128)
            for half in range(2):
                line = half * 128 + s // 4 * 16
                top_ref[line : line + 16, pl.ds(column, 128)] = ref[
                    s, half * 16 : (half + 1) * 16, :
                ].astype(F32)


def like(shape, dtype):
    return jax.ShapeDtypeStruct(shape, dtype)


def over_groups(x):
    parts = [x]
    for o in (1, 2, 3):
        parts.append(lax.ppermute(x, "grp", [(g, (g + o) % N_GRP) for g in range(N_GRP)]))
    return parts


def other_core(x):
    return lax.ppermute(x, "row_2", [(0, 1), (1, 0)])


def exchange(x, axes=ROW):
    return lax.all_to_all(x, axes, 0, 0, tiled=True)


def on_device(
    serving, serving_scale, hot_blocks, bag_lengths, bag_indices, dense_act, labels, w_top, w_out, master, accum,
):
    me = lax.axis_index("grp").astype(I32).reshape(1)
    core = lax.axis_index("row_2").astype(I32).reshape(1)
    (ids,) = call(ids_kernel, [like((N_ROW, D), I32)], [VM], (bag_indices,), 1 << 26)
    wanted = exchange(ids.reshape(N_ROW // 2, 2, D), CHIPS).reshape(N_ROW, D)
    use, use_t = call(
        counts_kernel,
        [like((BAGS, SLOTS), BF16), like((SLOTS, BAGS), BF16)],
        [VM] * 2,
        (bag_indices, bag_lengths),
        1 << 29,
    )
    (table,) = call(
        table_kernel,
        [like((SPAN, D), BF16)],
        [SM, pl.BlockSpec(memory_space=pl.ANY), VM],
        (hot_blocks, serving, serving_scale.reshape(1, 16)),
        1 << 20,
        [pltpu.VMEM((2, BLOCK, D), BF16), pltpu.SemaphoreType.DMA((2,))],
    )
    pre, labels_column, w_out_line = call(
        dense_kernel,
        [like((BAGS, FF), F32), like((BAGS, D), F32), like((1, FF), F32)],
        [VM] * 4,
        (dense_act, w_top, labels.reshape(1, BAGS), w_out.reshape(1, FF)),
        1 << 27,
    )
    other_table = other_core(table)
    wanted, table, other_table, pre, labels_column, w_out_line = lax.optimization_barrier(
        (wanted, table, other_table, pre, labels_column, w_out_line)
    )
    (rows,) = call(
        pick_kernel,
        [like((SLOTS, D), BF16)],
        [SM] + [VM] * 3,
        (core, wanted, table, other_table),
        1 << 26,
    )
    fetched = exchange(rows.reshape(N_ROW // 2, 2 * CAP, D), CHIPS).reshape(SLOTS, D)
    other_wanted = other_core(wanted)
    (place,) = call(
        place_kernel,
        [like((SPAN, SLOTS), BF16)],
        [SM] + [VM] * 2,
        (core, wanted, other_wanted),
        1 << 26,
    )
    give, keep, dpre = call(
        step_kernel,
        [like((N_ROW, 16, D), BF16), like((BAGS, D), BF16), like((BAGS, FF), BF16)],
        [SM] + [VM] * 7,
        (core, fetched, use, dense_act, pre, labels_column, w_top, w_out_line),
        1 << 29,
    )
    given = other_core(give)
    kept, row_grad = call(
        rest_kernel,
        [like((N_ROW, 16, D), F32), like((SLOTS, D), BF16)],
        [VM] * 4,
        (keep, dpre, w_top, use_t),
        1 << 28,
    )
    (parts,) = call(
        parts_kernel,
        [like((N_ROW, 24, D), BF16)],
        [VM] * 3,
        (kept, given, row_grad.reshape(N_ROW, CAP, D)),
        1 << 20,
    )
    got = exchange(parts)
    (own,) = call(
        owned_kernel,
        [like((SPAN + 48, D), BF16)],
        [VM, VM, SM],
        (got.reshape(N_ROW // 2, 2, 24, D), place, hot_blocks),
        1 << 26,
    )
    owned = over_groups(own)
    (top_part,) = call(
        top_kernel,
        [like((N_ROW // 2, 32, D), BF16)],
        [SM] + [VM] * 4,
        (me, *owned),
        1 << 16,
        [pltpu.VMEM((N_GRP, 32, D), BF16)],
    )
    top_mine = exchange(top_part, CHIPS)
    new_master, new_accum, coded = call(
        update_kernel,
        [like((QUARTER, D), F32), like((1, QUARTER), F32), like((QUARTER + 16, D), BF16)],
        [SM] + [VM] * 6,
        (me, *owned, master[0], accum),
        1 << 22,
        [pltpu.VMEM((N_GRP, SPAN + 48, D), BF16)],
    )
    quarters = over_groups(coded)
    fresh, fresh_scale = call(
        fresh_kernel,
        [like((4 * QUARTER, D), BF16), like((1, 16), BF16)],
        [SM] + [VM] * 4,
        (me, *quarters),
        1 << 20,
    )
    top_other = other_core(top_mine)
    (top_grad,) = call(
        last_kernel, [like((2 * D, FF), F32)], [SM] + [VM] * 2, (core, top_mine, top_other), 1 << 20
    )
    return new_master[None], new_accum, fresh, fresh_scale.reshape(16), top_grad


def solution(mesh):
    finer = Mesh(
        mesh.devices.reshape(mesh.shape["grp"], 4, 8, 2), ("grp", "row_0", "row_1", "row_2")
    )
    in_specs = (
        P(ROW, None),
        P(ROW),
        P("grp", ROW),
        P(GRP_ROW, None),
        P(GRP_ROW, None),
        P(GRP_ROW, None),
        P(GRP_ROW),
        P(),
        P(),
        P("grp", ROW, None),
        P("grp", ROW),
    )
    out_specs = (P("grp", ROW, None), P("grp", ROW), P(ROW, None), P(ROW), P())
    return jax.shard_map(
        on_device, mesh=finer, in_specs=in_specs, out_specs=out_specs, check_vma=False
    )
```

```python
import jax
import jax.numpy as jnp
from jax import lax
from jax.experimental import pallas as pl
from jax.experimental.pallas import tpu as pltpu
from jax.sharding import Mesh
from jax.sharding import PartitionSpec as P


ROW = ("row_0", "row_1", "row_2")
CHIPS = ("row_0", "row_1")
GRP_ROW = ("grp", "row_0", "row_1", "row_2")
N_GRP = 4
N_ROW = 64
BLOCK = 128
SPAN = 256
CAP = 8
BAGS = 256
NNZ = 1024
SLOTS = N_ROW * CAP
D = 128
FF = 1024
QUARTER = 512
LR = 0.05
GRANT = 16 << 20
F32 = jnp.float32
BF16 = jnp.bfloat16
I32 = jnp.int32
VM = pl.BlockSpec(memory_space=pltpu.VMEM)
SM = pl.BlockSpec(memory_space=pltpu.SMEM)


def iota(shape, dim):
    return lax.broadcasted_iota(I32, shape, dim)


def dot(a, b, ca=1, cb=0):
    return lax.dot_general(a, b, (((ca,), (cb,)), ((), ())), preferred_element_type=F32)


def ones_where(mask):
    return jnp.where(mask, 1.0, 0.0).astype(BF16)


def call(kernel, outs, specs, args, flops, scratch=()):
    bytes_accessed = sum(a.size * a.dtype.itemsize for a in args) + sum(
        o.size * o.dtype.itemsize for o in outs
    )
    return pl.pallas_call(
        kernel,
        out_shape=outs,
        in_specs=specs,
        out_specs=[VM] * len(outs),
        cost_estimate=pl.CostEstimate(
            flops=flops, bytes_accessed=bytes_accessed, transcendentals=0
        ),
        scratch_shapes=scratch,
        compiler_params=pltpu.CompilerParams(vmem_limit_bytes=GRANT),
    )(*args)


def shard_and_row(idx_ref):
    idx = idx_ref[...]
    shard = lax.shift_right_logical(idx, 8)
    return shard, idx & (SPAN - 1)


def ranks(shard, row):
    in_shard = ones_where(iota((N_ROW, NNZ), 0) == shard)
    at_row = ones_where(iota((SPAN, NNZ), 0) == row)
    used = dot(in_shard, at_row, 1, 1) > 0.5
    before = ones_where(iota((SPAN, SPAN), 0) < iota((SPAN, SPAN), 1))
    return in_shard, used, dot(ones_where(used), before)


def ids_kernel(idx_ref, ids_ref):
    _, used, rank = ranks(*shard_and_row(idx_ref))
    column = iota((N_ROW, SPAN), 1).astype(F32)
    lane = iota((N_ROW, D), 1)
    ids = jnp.zeros((N_ROW, D), F32)
    for k in range(CAP):
        mine = jnp.sum(
            jnp.where(used & (rank == float(k)), column, 0.0), axis=1, keepdims=True
        )
        ids = jnp.where(lane == k, mine, ids)
    ids_ref[...] = ids.astype(I32)


def counts_kernel(idx_ref, len_ref, use_ref, use_t_ref):
    shard, row = shard_and_row(idx_ref)
    in_shard, _, rank = ranks(shard, row)
    rank_at = dot(rank.astype(BF16), in_shard, 0, 0)
    rank = jnp.sum(jnp.where(iota((SPAN, NNZ), 0) == row, rank_at, 0.0), axis=0, keepdims=True)
    slot = shard * CAP + rank.astype(I32)
    at_slot = ones_where(iota((SLOTS, NNZ), 0) == slot)
    lengths = jnp.broadcast_to(len_ref[...].astype(F32), (BAGS, BAGS))
    a, b = iota((BAGS, BAGS), 0), iota((BAGS, BAGS), 1)
    starts = jnp.sum(jnp.where(b < a, lengths, 0.0), axis=1, keepdims=True).astype(I32)
    ends = jnp.sum(jnp.where(b <= a, lengths, 0.0), axis=1, keepdims=True).astype(I32)
    place = iota((BAGS, NNZ), 1)
    in_bag = ones_where((place >= starts) & (place < ends))
    use_ref[...] = dot(in_bag, at_slot, 1, 1).astype(BF16)
    use_t_ref[...] = dot(at_slot, in_bag, 1, 1).astype(BF16)


def table_kernel(hot_ref, serving_ref, scale_ref, table_ref, buf, sem):
    copies = [
        pltpu.make_async_copy(
            serving_ref.at[pl.ds(pl.multiple_of(hot_ref[0, j] * BLOCK, BLOCK), BLOCK)],
            buf.at[j],
            sem.at[j],
        )
        for j in range(2)
    ]
    for c in copies:
        c.start()
    scales = scale_ref[...].astype(F32)
    lane = iota(scales.shape, 1)
    for j, c in enumerate(copies):
        own = jnp.sum(jnp.where(lane == hot_ref[0, j], scales, 0.0), axis=1, keepdims=True)
        c.wait()
        table_ref[j * BLOCK : (j + 1) * BLOCK, :] = (buf[j].astype(F32) * own).astype(BF16)


def pick_kernel(core_ref, ids_ref, table_ref, other_ref, rows_ref):
    owner = ones_where(lax.shift_right_logical(iota((SLOTS, N_ROW), 0), 3) == iota((SLOTS, N_ROW), 1))
    spread = dot(owner, ids_ref[...].astype(F32).astype(BF16))
    mine = iota((SLOTS, D), 1) == (iota((SLOTS, D), 0) & (CAP - 1))
    column = jnp.sum(jnp.where(mine, spread, 0.0), axis=1, keepdims=True).astype(I32)
    here = lax.shift_right_logical(iota((SLOTS, SPAN), 0), 3) & 1 == core_ref[0]
    match = iota((SLOTS, SPAN), 1) == column
    rows = dot(ones_where(match & here), table_ref[...])
    rows_ref[...] = (rows + dot(ones_where(match & ~here), other_ref[...])).astype(BF16)


def place_kernel(core_ref, hot_ref, ids_ref, other_ref, place_ref, hot_out_ref):
    lane = iota((8, D), 1)
    hot_out_ref[...] = jnp.where(lane == 0, hot_ref[0, 0], jnp.where(lane == 1, hot_ref[0, 1], 0))
    slot = iota((SLOTS, N_ROW), 0)
    line = lax.shift_right_logical(slot, 4) * 2 + core_ref[0] == iota((SLOTS, N_ROW), 1)
    here = lax.shift_right_logical(slot, 3) & 1 == core_ref[0]
    spread = dot(ids_ref[...].astype(F32).astype(BF16), ones_where(line & here), 0, 1)
    spread = spread + dot(other_ref[...].astype(F32).astype(BF16), ones_where(line & ~here), 0, 1)
    mine = iota((D, SLOTS), 0) == (iota((D, SLOTS), 1) & (CAP - 1))
    line = jnp.sum(jnp.where(mine, spread, 0.0), axis=0, keepdims=True).astype(I32)
    place_ref[...] = ones_where(iota((SPAN, SLOTS), 0) == line)


def dense_kernel(dense_ref, w_ref, labels_ref, w_out_ref, pre_ref, labels_out_ref, w_out_out_ref):
    pre_ref[...] = dot(dense_ref[...], w_ref[D : 2 * D, :])
    a, b = iota((BAGS, BAGS), 0), iota((BAGS, BAGS), 1)
    labels = jnp.sum(
        jnp.where(a == b, jnp.broadcast_to(labels_ref[...], (BAGS, BAGS)), 0.0),
        axis=1,
        keepdims=True,
    )
    labels_out_ref[...] = jnp.broadcast_to(labels, (BAGS, D))
    w_out_out_ref[...] = w_out_ref[...]


def by_tile(ref, value):
    for i in range(8):
        for j in range(8):
            ref[i * 8 + j] = value[i * 16 : (i + 1) * 16, j * 128 : (j + 1) * 128]


def step_kernel(
    core_ref, rows_ref, use_ref, dense_ref, pre_ref, labels_ref, w_ref, w_out_ref,
    give_ref, keep_ref, dpre_ref,
):
    pooled = dot(use_ref[...], rows_ref[...]).astype(BF16)
    pre = pre_ref[...] + dot(pooled, w_ref[0:D, :])
    sig = jax.nn.sigmoid(pre)
    w_out = w_out_ref[...]
    logit = jnp.sum(pre * sig * w_out, axis=1, keepdims=True)
    dlogit = jax.nn.sigmoid(logit) - labels_ref[:, 0:1]
    dpre = (dlogit * w_out * (sig * (1.0 + pre * (1.0 - sig)))).astype(BF16)
    dpre_ref[...] = dpre
    first = core_ref[0] == 0
    dense = dense_ref[...]
    by_tile(give_ref, dot(jnp.where(first, dense, pooled), dpre, 0, 0).astype(BF16))
    keep_ref[...] = jnp.where(first, pooled, dense)


def rest_kernel(keep_ref, dpre_ref, w_ref, use_t_ref, kept_ref, out_ref):
    dpre = dpre_ref[...]
    pooled_grad = dot(dpre, w_ref[0:D, :], 1, 1)
    high = pooled_grad.astype(BF16)
    low = (pooled_grad - high.astype(F32)).astype(BF16)
    use_t = use_t_ref[...]
    out_ref[...] = (dot(use_t, high) + dot(use_t, low)).astype(BF16)
    by_tile(kept_ref, dot(keep_ref[...], dpre, 0, 0))


def parts_kernel(keep_ref, given_ref, row_grad_ref, out_ref):
    out_ref[:, 0:16, :] = (keep_ref[...] + given_ref[...].astype(F32)).astype(BF16)
    out_ref[:, 16:24, :] = row_grad_ref[...]


def hots_kernel(me_ref, h0_ref, h1_ref, h2_ref, h3_ref, out_ref):
    me = me_ref[0]
    for o, ref in enumerate((h0_ref, h1_ref, h2_ref, h3_ref)):
        out_ref[(me - o) & 3] = ref[...]


def owned_kernel(got_ref, place_ref, out_ref):
    grads = got_ref[:, :, 16:24, :].astype(F32).reshape(SLOTS, D).astype(BF16)
    out_ref[0:SPAN, :] = dot(place_ref[...], grads).astype(BF16)
    for half in range(2):
        at = SPAN + 16 * half
        out_ref[at : at + 16, :] = jnp.sum(
            got_ref[:, half, 0:16, :].astype(F32), axis=0
        ).astype(BF16)


def top_kernel(me_ref, x0_ref, x1_ref, x2_ref, x3_ref, top_ref, by_group):
    me = me_ref[0]
    for o, ref in enumerate((x0_ref, x1_ref, x2_ref, x3_ref)):
        by_group[(me - o) & 3] = ref[SPAN : SPAN + 32, :]
    top = jnp.zeros((32, D), F32)
    for g in range(N_GRP):
        top = top + by_group[g].astype(F32)
    top_ref[...] = jnp.broadcast_to(top.astype(BF16)[None], (N_ROW // 2, 32, D))


def update_kernel(
    me_ref, x0_ref, x1_ref, x2_ref, x3_ref, hots_ref, master_ref, accum_ref,
    new_master_ref, new_accum_ref, coded_ref, by_group,
):
    me = me_ref[0]
    for o, ref in enumerate((x0_ref, x1_ref, x2_ref, x3_ref)):
        by_group[(me - o) & 3] = ref[...]
    hot = [hots_ref[g, 0:1, :] for g in range(N_GRP)]
    a, b = iota((BLOCK, BLOCK), 0), iota((BLOCK, BLOCK), 1)
    diagonal = a == b
    lane = iota((16, D), 1)
    scale_row = jnp.zeros((16, D), F32)
    for q in range(4):
        grad = jnp.zeros((BLOCK, D), F32)
        number = me * 4 + q
        for g in range(N_GRP):
            for j in range(2):
                block = by_group[g, j * BLOCK : (j + 1) * BLOCK, :].astype(F32)
                grad = grad + jnp.where(hot[g][:, j : j + 1] == number, block, 0.0)
        at = pl.ds(q * BLOCK, BLOCK)
        accum = jnp.broadcast_to(accum_ref[:, q * BLOCK : (q + 1) * BLOCK], (BLOCK, BLOCK))
        state = jnp.sum(jnp.where(diagonal, accum, 0.0), axis=1, keepdims=True) + jnp.mean(
            grad * grad, axis=1, keepdims=True
        )
        new_accum_ref[:, q * BLOCK : (q + 1) * BLOCK] = jnp.sum(
            jnp.where(diagonal, jnp.broadcast_to(state, (BLOCK, BLOCK)), 0.0), axis=0, keepdims=True
        )
        weights = master_ref[at, :] - grad * (LR / jnp.sqrt(state))
        new_master_ref[at, :] = weights
        largest = jnp.max(jnp.max(jnp.abs(weights), axis=0, keepdims=True), axis=1, keepdims=True)
        scale = (largest + 1e-06).astype(BF16).astype(F32)
        coded_ref[at, :] = (weights / scale).astype(BF16)
        scale_row = jnp.where(lane == me * 4 + q, scale, scale_row)
    coded_ref[pl.ds(QUARTER, 16), :] = scale_row.astype(BF16)


def fresh_kernel(me_ref, s0_ref, s1_ref, s2_ref, s3_ref, serving_ref, scale_ref):
    me = me_ref[0]
    scales = jnp.zeros((16, D), F32)
    for o, ref in enumerate((s0_ref, s1_ref, s2_ref, s3_ref)):
        start = pl.multiple_of(((me - o) & 3) * QUARTER, QUARTER)
        serving_ref[pl.ds(start, QUARTER), :] = ref[0:QUARTER, :]
        scales = scales + ref[QUARTER : QUARTER + 16, :].astype(F32)
    scale_ref[...] = scales[0:1, 0:16].astype(BF16)


def last_kernel(core_ref, mine_ref, other_ref, top_ref):
    for ref, core in ((mine_ref, core_ref[0]), (other_ref, 1 - core_ref[0])):
        for s in range(N_ROW // 2):
            column = pl.multiple_of((s % 4 * 2 + core) * 128, 128)
            for half in range(2):
                line = half * 128 + s // 4 * 16
                top_ref[line : line + 16, pl.ds(column, 128)] = ref[
                    s, half * 16 : (half + 1) * 16, :
                ].astype(F32)


def like(shape, dtype):
    return jax.ShapeDtypeStruct(shape, dtype)


def over_groups(x):
    parts = [x]
    for o in (1, 2, 3):
        parts.append(lax.ppermute(x, "grp", [(g, (g + o) % N_GRP) for g in range(N_GRP)]))
    return parts


def other_core(x):
    return lax.ppermute(x, "row_2", [(0, 1), (1, 0)])


def exchange(x, axes=ROW):
    return lax.all_to_all(x, axes, 0, 0, tiled=True)


def on_device(
    serving, serving_scale, hot_blocks, bag_lengths, bag_indices, dense_act, labels, w_top, w_out, master, accum,
):
    me = lax.axis_index("grp").astype(I32).reshape(1)
    core = lax.axis_index("row_2").astype(I32).reshape(1)
    (ids,) = call(ids_kernel, [like((N_ROW, D), I32)], [VM], (bag_indices,), 1 << 26)
    wanted = exchange(ids.reshape(N_ROW // 2, 2, D), CHIPS).reshape(N_ROW, D)
    use, use_t = call(
        counts_kernel,
        [like((BAGS, SLOTS), BF16), like((SLOTS, BAGS), BF16)],
        [VM] * 2,
        (bag_indices, bag_lengths),
        1 << 29,
    )
    (table,) = call(
        table_kernel,
        [like((SPAN, D), BF16)],
        [SM, pl.BlockSpec(memory_space=pl.ANY), VM],
        (hot_blocks, serving, serving_scale.reshape(1, 16)),
        1 << 20,
        [pltpu.VMEM((2, BLOCK, D), BF16), pltpu.SemaphoreType.DMA((2,))],
    )
    pre, labels_column, w_out_line = call(
        dense_kernel,
        [like((BAGS, FF), F32), like((BAGS, D), F32), like((1, FF), F32)],
        [VM] * 4,
        (dense_act, w_top, labels.reshape(1, BAGS), w_out.reshape(1, FF)),
        1 << 27,
    )
    other_table = other_core(table)
    wanted, table, other_table, pre, labels_column, w_out_line = lax.optimization_barrier(
        (wanted, table, other_table, pre, labels_column, w_out_line)
    )
    (rows,) = call(
        pick_kernel,
        [like((SLOTS, D), BF16)],
        [SM] + [VM] * 3,
        (core, wanted, table, other_table),
        1 << 26,
    )
    fetched = exchange(rows.reshape(N_ROW // 2, 2 * CAP, D), CHIPS).reshape(SLOTS, D)
    other_wanted = other_core(wanted)
    place, hot = call(
        place_kernel,
        [like((SPAN, SLOTS), BF16), like((8, D), I32)],
        [SM] * 2 + [VM] * 2,
        (core, hot_blocks, wanted, other_wanted),
        1 << 26,
    )
    give, keep, dpre = call(
        step_kernel,
        [like((N_ROW, 16, D), BF16), like((BAGS, D), BF16), like((BAGS, FF), BF16)],
        [SM] + [VM] * 7,
        (core, fetched, use, dense_act, pre, labels_column, w_top, w_out_line),
        1 << 29,
    )
    given = other_core(give)
    kept, row_grad = call(
        rest_kernel,
        [like((N_ROW, 16, D), F32), like((SLOTS, D), BF16)],
        [VM] * 4,
        (keep, dpre, w_top, use_t),
        1 << 28,
    )
    (parts,) = call(
        parts_kernel,
        [like((N_ROW, 24, D), BF16)],
        [VM] * 3,
        (kept, given, row_grad.reshape(N_ROW, CAP, D)),
        1 << 20,
    )
    got = exchange(parts)
    (hots,) = call(
        hots_kernel, [like((N_GRP, 8, D), I32)], [SM] + [VM] * 4, (me, *over_groups(hot)), 1 << 12
    )
    (own,) = call(
        owned_kernel,
        [like((SPAN + 32, D), BF16)],
        [VM, VM],
        (got.reshape(N_ROW // 2, 2, 24, D), place),
        1 << 26,
    )
    owned = over_groups(own)
    (top_part,) = call(
        top_kernel,
        [like((N_ROW // 2, 32, D), BF16)],
        [SM] + [VM] * 4,
        (me, *owned),
        1 << 16,
        [pltpu.VMEM((N_GRP, 32, D), BF16)],
    )
    top_mine = exchange(top_part, CHIPS)
    new_master, new_accum, coded = call(
        update_kernel,
        [like((QUARTER, D), F32), like((1, QUARTER), F32), like((QUARTER + 16, D), BF16)],
        [SM] + [VM] * 7,
        (me, *owned, hots, master[0], accum),
        1 << 22,
        [pltpu.VMEM((N_GRP, SPAN + 32, D), BF16)],
    )
    quarters = over_groups(coded)
    fresh, fresh_scale = call(
        fresh_kernel,
        [like((4 * QUARTER, D), BF16), like((1, 16), BF16)],
        [SM] + [VM] * 4,
        (me, *quarters),
        1 << 20,
    )
    top_other = other_core(top_mine)
    (top_grad,) = call(
        last_kernel, [like((2 * D, FF), F32)], [SM] + [VM] * 2, (core, top_mine, top_other), 1 << 20
    )
    return new_master[None], new_accum, fresh, fresh_scale.reshape(16), top_grad


def solution(mesh):
    finer = Mesh(
        mesh.devices.reshape(mesh.shape["grp"], 4, 8, 2), ("grp", "row_0", "row_1", "row_2")
    )
    in_specs = (
        P(ROW, None),
        P(ROW),
        P("grp", ROW),
        P(GRP_ROW, None),
        P(GRP_ROW, None),
        P(GRP_ROW, None),
        P(GRP_ROW),
        P(),
        P(),
        P("grp", ROW, None),
        P("grp", ROW),
    )
    out_specs = (P("grp", ROW, None), P("grp", ROW), P(ROW, None), P(ROW), P())
    return jax.shard_map(
        on_device, mesh=finer, in_specs=in_specs, out_specs=out_specs, check_vma=False
    )
```

```python
import jax
import jax.numpy as jnp
from jax import lax
from jax.experimental import pallas as pl
from jax.experimental.pallas import tpu as pltpu
from jax.sharding import Mesh
from jax.sharding import PartitionSpec as P


ROW = ("row_0", "row_1", "row_2")
CHIPS = ("row_0", "row_1")
GRP_ROW = ("grp", "row_0", "row_1", "row_2")
N_GRP = 4
N_ROW = 64
BLOCK = 128
SPAN = 256
CAP = 8
BAGS = 256
NNZ = 1024
SLOTS = N_ROW * CAP
D = 128
FF = 1024
QUARTER = 512
LR = 0.05
GRANT = 16 << 20
F32 = jnp.float32
BF16 = jnp.bfloat16
I32 = jnp.int32
VM = pl.BlockSpec(memory_space=pltpu.VMEM)
SM = pl.BlockSpec(memory_space=pltpu.SMEM)


def iota(shape, dim):
    return lax.broadcasted_iota(I32, shape, dim)


def dot(a, b, ca=1, cb=0):
    return lax.dot_general(a, b, (((ca,), (cb,)), ((), ())), preferred_element_type=F32)


def ones_where(mask):
    return jnp.where(mask, 1.0, 0.0).astype(BF16)


def call(kernel, outs, specs, args, flops, scratch=()):
    bytes_accessed = sum(a.size * a.dtype.itemsize for a in args) + sum(
        o.size * o.dtype.itemsize for o in outs
    )
    return pl.pallas_call(
        kernel,
        out_shape=outs,
        in_specs=specs,
        out_specs=[VM] * len(outs),
        cost_estimate=pl.CostEstimate(
            flops=flops, bytes_accessed=bytes_accessed, transcendentals=0
        ),
        scratch_shapes=scratch,
        compiler_params=pltpu.CompilerParams(vmem_limit_bytes=GRANT),
    )(*args)


def shard_and_row(idx_ref):
    idx = idx_ref[...]
    shard = lax.shift_right_logical(idx, 8)
    return shard, idx & (SPAN - 1)


def ranks(shard, row):
    in_shard = ones_where(iota((N_ROW, NNZ), 0) == shard)
    at_row = ones_where(iota((SPAN, NNZ), 0) == row)
    used = dot(in_shard, at_row, 1, 1) > 0.5
    before = ones_where(iota((SPAN, SPAN), 0) < iota((SPAN, SPAN), 1))
    return in_shard, used, dot(ones_where(used), before)


def ids_kernel(idx_ref, ids_ref):
    _, used, rank = ranks(*shard_and_row(idx_ref))
    column = iota((N_ROW, SPAN), 1).astype(F32)
    lane = iota((N_ROW, D), 1)
    ids = jnp.zeros((N_ROW, D), F32)
    for k in range(CAP):
        mine = jnp.sum(
            jnp.where(used & (rank == float(k)), column, 0.0), axis=1, keepdims=True
        )
        ids = jnp.where(lane == k, mine, ids)
    ids_ref[...] = ids.astype(I32)


def counts_kernel(idx_ref, len_ref, use_ref, use_t_ref):
    shard, row = shard_and_row(idx_ref)
    in_shard, _, rank = ranks(shard, row)
    rank_at = dot(rank.astype(BF16), in_shard, 0, 0)
    rank = jnp.sum(jnp.where(iota((SPAN, NNZ), 0) == row, rank_at, 0.0), axis=0, keepdims=True)
    slot = shard * CAP + rank.astype(I32)
    at_slot = ones_where(iota((SLOTS, NNZ), 0) == slot)
    lengths = jnp.broadcast_to(len_ref[...].astype(F32), (BAGS, BAGS))
    a, b = iota((BAGS, BAGS), 0), iota((BAGS, BAGS), 1)
    starts = jnp.sum(jnp.where(b < a, lengths, 0.0), axis=1, keepdims=True).astype(I32)
    ends = jnp.sum(jnp.where(b <= a, lengths, 0.0), axis=1, keepdims=True).astype(I32)
    place = iota((BAGS, NNZ), 1)
    in_bag = ones_where((place >= starts) & (place < ends))
    use_ref[...] = dot(in_bag, at_slot, 1, 1).astype(BF16)
    use_t_ref[...] = dot(at_slot, in_bag, 1, 1).astype(BF16)


def table_kernel(hot_ref, serving_ref, scale_ref, table_ref, buf, sem):
    copies = [
        pltpu.make_async_copy(
            serving_ref.at[pl.ds(pl.multiple_of(hot_ref[0, j] * BLOCK, BLOCK), BLOCK)],
            buf.at[j],
            sem.at[j],
        )
        for j in range(2)
    ]
    for c in copies:
        c.start()
    scales = scale_ref[...].astype(F32)
    lane = iota(scales.shape, 1)
    for j, c in enumerate(copies):
        own = jnp.sum(jnp.where(lane == hot_ref[0, j], scales, 0.0), axis=1, keepdims=True)
        c.wait()
        table_ref[j * BLOCK : (j + 1) * BLOCK, :] = (buf[j].astype(F32) * own).astype(BF16)


def pick_kernel(core_ref, ids_ref, table_ref, other_ref, rows_ref):
    owner = ones_where(lax.shift_right_logical(iota((SLOTS, N_ROW), 0), 3) == iota((SLOTS, N_ROW), 1))
    spread = dot(owner, ids_ref[...].astype(F32).astype(BF16))
    mine = iota((SLOTS, D), 1) == (iota((SLOTS, D), 0) & (CAP - 1))
    column = jnp.sum(jnp.where(mine, spread, 0.0), axis=1, keepdims=True).astype(I32)
    here = lax.shift_right_logical(iota((SLOTS, SPAN), 0), 3) & 1 == core_ref[0]
    match = iota((SLOTS, SPAN), 1) == column
    rows = dot(ones_where(match & here), table_ref[...])
    rows_ref[...] = (rows + dot(ones_where(match & ~here), other_ref[...])).astype(BF16)


def place_kernel(core_ref, ids_ref, other_ref, place_ref):
    slot = iota((SLOTS, N_ROW), 0)
    line = lax.shift_right_logical(slot, 4) * 2 + core_ref[0] == iota((SLOTS, N_ROW), 1)
    here = lax.shift_right_logical(slot, 3) & 1 == core_ref[0]
    spread = dot(ids_ref[...].astype(F32).astype(BF16), ones_where(line & here), 0, 1)
    spread = spread + dot(other_ref[...].astype(F32).astype(BF16), ones_where(line & ~here), 0, 1)
    mine = iota((D, SLOTS), 0) == (iota((D, SLOTS), 1) & (CAP - 1))
    line = jnp.sum(jnp.where(mine, spread, 0.0), axis=0, keepdims=True).astype(I32)
    place_ref[...] = ones_where(iota((SPAN, SLOTS), 0) == line)


def dense_kernel(dense_ref, w_ref, labels_ref, w_out_ref, pre_ref, labels_out_ref, w_out_out_ref):
    pre_ref[...] = dot(dense_ref[...], w_ref[D : 2 * D, :])
    a, b = iota((BAGS, BAGS), 0), iota((BAGS, BAGS), 1)
    labels = jnp.sum(
        jnp.where(a == b, jnp.broadcast_to(labels_ref[...], (BAGS, BAGS)), 0.0),
        axis=1,
        keepdims=True,
    )
    labels_out_ref[...] = jnp.broadcast_to(labels, (BAGS, D))
    w_out_out_ref[...] = w_out_ref[...]


def by_tile(ref, value):
    for i in range(8):
        for j in range(8):
            ref[i * 8 + j] = value[i * 16 : (i + 1) * 16, j * 128 : (j + 1) * 128]


def step_kernel(
    core_ref, rows_ref, use_ref, dense_ref, pre_ref, labels_ref, w_ref, w_out_ref,
    give_ref, keep_ref, dpre_ref,
):
    pooled = dot(use_ref[...], rows_ref[...]).astype(BF16)
    pre = pre_ref[...] + dot(pooled, w_ref[0:D, :])
    sig = jax.nn.sigmoid(pre)
    w_out = w_out_ref[...]
    logit = jnp.sum(pre * sig * w_out, axis=1, keepdims=True)
    dlogit = jax.nn.sigmoid(logit) - labels_ref[:, 0:1]
    dpre = (dlogit * w_out * (sig * (1.0 + pre * (1.0 - sig)))).astype(BF16)
    dpre_ref[...] = dpre
    first = core_ref[0] == 0
    dense = dense_ref[...]
    by_tile(give_ref, dot(jnp.where(first, dense, pooled), dpre, 0, 0).astype(BF16))
    keep_ref[...] = jnp.where(first, pooled, dense)


def rest_kernel(keep_ref, dpre_ref, w_ref, use_t_ref, kept_ref, out_ref):
    dpre = dpre_ref[...]
    pooled_grad = dot(dpre, w_ref[0:D, :], 1, 1)
    high = pooled_grad.astype(BF16)
    low = (pooled_grad - high.astype(F32)).astype(BF16)
    use_t = use_t_ref[...]
    out_ref[...] = (dot(use_t, high) + dot(use_t, low)).astype(BF16)
    by_tile(kept_ref, dot(keep_ref[...], dpre, 0, 0))


def parts_kernel(keep_ref, given_ref, row_grad_ref, out_ref):
    out_ref[:, 0:16, :] = (keep_ref[...] + given_ref[...].astype(F32)).astype(BF16)
    out_ref[:, 16:24, :] = row_grad_ref[...]


def owned_kernel(got_ref, place_ref, hot_ref, out_ref):
    grads = got_ref[:, :, 16:24, :].astype(F32).reshape(SLOTS, D).astype(BF16)
    out_ref[0:SPAN, :] = dot(place_ref[...], grads).astype(BF16)
    for half in range(2):
        at = SPAN + 16 * half
        out_ref[at : at + 16, :] = jnp.sum(
            got_ref[:, half, 0:16, :].astype(F32), axis=0
        ).astype(BF16)
    lane = iota((16, D), 1)
    hot = jnp.where(lane == 0, hot_ref[0, 0], jnp.where(lane == 1, hot_ref[0, 1], 0))
    out_ref[SPAN + 32 : SPAN + 48, :] = hot.astype(F32).astype(BF16)


def top_kernel(me_ref, x0_ref, x1_ref, x2_ref, x3_ref, top_ref, by_group):
    me = me_ref[0]
    for o, ref in enumerate((x0_ref, x1_ref, x2_ref, x3_ref)):
        by_group[me ^ o] = ref[SPAN : SPAN + 32, :]
    top = jnp.zeros((32, D), F32)
    for g in range(N_GRP):
        top = top + by_group[g].astype(F32)
    top_ref[...] = jnp.broadcast_to(top.astype(BF16)[None], (N_ROW // 2, 32, D))


def update_kernel(
    me_ref, x0_ref, x1_ref, x2_ref, x3_ref, master_ref, accum_ref,
    new_master_ref, new_accum_ref, coded_ref, by_group,
):
    me = me_ref[0]
    for o, ref in enumerate((x0_ref, x1_ref, x2_ref, x3_ref)):
        by_group[me ^ o] = ref[...]
    hot = [by_group[g, SPAN + 32 : SPAN + 48, :].astype(F32)[0:1, :] for g in range(N_GRP)]
    a, b = iota((BLOCK, BLOCK), 0), iota((BLOCK, BLOCK), 1)
    diagonal = a == b
    lane = iota((16, D), 1)
    scale_row = jnp.zeros((16, D), F32)
    for q in range(4):
        grad = jnp.zeros((BLOCK, D), F32)
        number = (me * 4 + q).astype(F32)
        for g in range(N_GRP):
            for j in range(2):
                block = by_group[g, j * BLOCK : (j + 1) * BLOCK, :].astype(F32)
                grad = grad + jnp.where(hot[g][:, j : j + 1] == number, block, 0.0)
        at = pl.ds(q * BLOCK, BLOCK)
        accum = jnp.broadcast_to(accum_ref[:, q * BLOCK : (q + 1) * BLOCK], (BLOCK, BLOCK))
        state = jnp.sum(jnp.where(diagonal, accum, 0.0), axis=1, keepdims=True) + jnp.mean(
            grad * grad, axis=1, keepdims=True
        )
        new_accum_ref[:, q * BLOCK : (q + 1) * BLOCK] = jnp.sum(
            jnp.where(diagonal, jnp.broadcast_to(state, (BLOCK, BLOCK)), 0.0), axis=0, keepdims=True
        )
        weights = master_ref[at, :] - grad * (LR / jnp.sqrt(state))
        new_master_ref[at, :] = weights
        largest = jnp.max(jnp.max(jnp.abs(weights), axis=0, keepdims=True), axis=1, keepdims=True)
        scale = (largest + 1e-06).astype(BF16).astype(F32)
        coded_ref[at, :] = (weights / scale).astype(BF16)
        scale_row = jnp.where(lane == me * 4 + q, scale, scale_row)
    coded_ref[pl.ds(QUARTER, 16), :] = scale_row.astype(BF16)


def fresh_kernel(me_ref, s0_ref, s1_ref, s2_ref, s3_ref, serving_ref, scale_ref):
    me = me_ref[0]
    scales = jnp.zeros((16, D), F32)
    for o, ref in enumerate((s0_ref, s1_ref, s2_ref, s3_ref)):
        start = pl.multiple_of((me ^ o) * QUARTER, QUARTER)
        serving_ref[pl.ds(start, QUARTER), :] = ref[0:QUARTER, :]
        scales = scales + ref[QUARTER : QUARTER + 16, :].astype(F32)
    scale_ref[...] = scales[0:1, 0:16].astype(BF16)


def last_kernel(core_ref, mine_ref, other_ref, top_ref):
    for ref, core in ((mine_ref, core_ref[0]), (other_ref, 1 - core_ref[0])):
        for s in range(N_ROW // 2):
            column = pl.multiple_of((s % 4 * 2 + core) * 128, 128)
            for half in range(2):
                line = half * 128 + s // 4 * 16
                top_ref[line : line + 16, pl.ds(column, 128)] = ref[
                    s, half * 16 : (half + 1) * 16, :
                ].astype(F32)


def like(shape, dtype):
    return jax.ShapeDtypeStruct(shape, dtype)


def over_groups(x):
    parts = [x]
    for o in (1, 2, 3):
        parts.append(lax.ppermute(x, "grp", [(g, g ^ o) for g in range(N_GRP)]))
    return parts


def other_core(x):
    return lax.ppermute(x, "row_2", [(0, 1), (1, 0)])


def exchange(x, axes=ROW):
    return lax.all_to_all(x, axes, 0, 0, tiled=True)


def on_device(
    serving, serving_scale, hot_blocks, bag_lengths, bag_indices, dense_act, labels, w_top, w_out, master, accum,
):
    me = lax.axis_index("grp").astype(I32).reshape(1)
    core = lax.axis_index("row_2").astype(I32).reshape(1)
    (ids,) = call(ids_kernel, [like((N_ROW, D), I32)], [VM], (bag_indices,), 1 << 26)
    wanted = exchange(ids.reshape(N_ROW // 2, 2, D), CHIPS).reshape(N_ROW, D)
    use, use_t = call(
        counts_kernel,
        [like((BAGS, SLOTS), BF16), like((SLOTS, BAGS), BF16)],
        [VM] * 2,
        (bag_indices, bag_lengths),
        1 << 29,
    )
    (table,) = call(
        table_kernel,
        [like((SPAN, D), BF16)],
        [SM, pl.BlockSpec(memory_space=pl.ANY), VM],
        (hot_blocks, serving, serving_scale.reshape(1, 16)),
        1 << 20,
        [pltpu.VMEM((2, BLOCK, D), BF16), pltpu.SemaphoreType.DMA((2,))],
    )
    pre, labels_column, w_out_line = call(
        dense_kernel,
        [like((BAGS, FF), F32), like((BAGS, D), F32), like((1, FF), F32)],
        [VM] * 4,
        (dense_act, w_top, labels.reshape(1, BAGS), w_out.reshape(1, FF)),
        1 << 27,
    )
    other_table = other_core(table)
    wanted, table, other_table, pre, labels_column, w_out_line = lax.optimization_barrier(
        (wanted, table, other_table, pre, labels_column, w_out_line)
    )
    (rows,) = call(
        pick_kernel,
        [like((SLOTS, D), BF16)],
        [SM] + [VM] * 3,
        (core, wanted, table, other_table),
        1 << 26,
    )
    fetched = exchange(rows.reshape(N_ROW // 2, 2 * CAP, D), CHIPS).reshape(SLOTS, D)
    other_wanted = other_core(wanted)
    (place,) = call(
        place_kernel,
        [like((SPAN, SLOTS), BF16)],
        [SM] + [VM] * 2,
        (core, wanted, other_wanted),
        1 << 26,
    )
    give, keep, dpre = call(
        step_kernel,
        [like((N_ROW, 16, D), BF16), like((BAGS, D), BF16), like((BAGS, FF), BF16)],
        [SM] + [VM] * 7,
        (core, fetched, use, dense_act, pre, labels_column, w_top, w_out_line),
        1 << 29,
    )
    given = other_core(give)
    kept, row_grad = call(
        rest_kernel,
        [like((N_ROW, 16, D), F32), like((SLOTS, D), BF16)],
        [VM] * 4,
        (keep, dpre, w_top, use_t),
        1 << 28,
    )
    (parts,) = call(
        parts_kernel,
        [like((N_ROW, 24, D), BF16)],
        [VM] * 3,
        (kept, given, row_grad.reshape(N_ROW, CAP, D)),
        1 << 20,
    )
    got = exchange(parts)
    (own,) = call(
        owned_kernel,
        [like((SPAN + 48, D), BF16)],
        [VM, VM, SM],
        (got.reshape(N_ROW // 2, 2, 24, D), place, hot_blocks),
        1 << 26,
    )
    owned = over_groups(own)
    (top_part,) = call(
        top_kernel,
        [like((N_ROW // 2, 32, D), BF16)],
        [SM] + [VM] * 4,
        (me, *owned),
        1 << 16,
        [pltpu.VMEM((N_GRP, 32, D), BF16)],
    )
    top_mine = exchange(top_part, CHIPS)
    new_master, new_accum, coded = call(
        update_kernel,
        [like((QUARTER, D), F32), like((1, QUARTER), F32), like((QUARTER + 16, D), BF16)],
        [SM] + [VM] * 6,
        (me, *owned, master[0], accum),
        1 << 22,
        [pltpu.VMEM((N_GRP, SPAN + 48, D), BF16)],
    )
    quarters = over_groups(coded)
    fresh, fresh_scale = call(
        fresh_kernel,
        [like((4 * QUARTER, D), BF16), like((1, 16), BF16)],
        [SM] + [VM] * 4,
        (me, *quarters),
        1 << 20,
    )
    top_other = other_core(top_mine)
    (top_grad,) = call(
        last_kernel, [like((2 * D, FF), F32)], [SM] + [VM] * 2, (core, top_mine, top_other), 1 << 20
    )
    return new_master[None], new_accum, fresh, fresh_scale.reshape(16), top_grad


def solution(mesh):
    finer = Mesh(
        mesh.devices.reshape(mesh.shape["grp"], 4, 8, 2), ("grp", "row_0", "row_1", "row_2")
    )
    in_specs = (
        P(ROW, None),
        P(ROW),
        P("grp", ROW),
        P(GRP_ROW, None),
        P(GRP_ROW, None),
        P(GRP_ROW, None),
        P(GRP_ROW),
        P(),
        P(),
        P("grp", ROW, None),
        P("grp", ROW),
    )
    out_specs = (P("grp", ROW, None), P("grp", ROW), P(ROW, None), P(ROW), P())
    return jax.shard_map(
        on_device, mesh=finer, in_specs=in_specs, out_specs=out_specs, check_vma=False
    )
```

```python
import jax
import jax.numpy as jnp
from jax import lax
from jax.experimental import pallas as pl
from jax.experimental.pallas import tpu as pltpu
from jax.sharding import Mesh
from jax.sharding import PartitionSpec as P


ROW = ("row_0", "row_1", "row_2")
CHIPS = ("row_0", "row_1")
GRP_ROW = ("grp", "row_0", "row_1", "row_2")
N_GRP = 4
N_ROW = 64
BLOCK = 128
SPAN = 256
CAP = 8
BAGS = 256
NNZ = 1024
SLOTS = N_ROW * CAP
D = 128
FF = 1024
QUARTER = 512
LR = 0.05
GRANT = 16 << 20
F32 = jnp.float32
BF16 = jnp.bfloat16
I32 = jnp.int32
VM = pl.BlockSpec(memory_space=pltpu.VMEM)
SM = pl.BlockSpec(memory_space=pltpu.SMEM)


def iota(shape, dim):
    return lax.broadcasted_iota(I32, shape, dim)


def dot(a, b, ca=1, cb=0):
    return lax.dot_general(a, b, (((ca,), (cb,)), ((), ())), preferred_element_type=F32)


def ones_where(mask):
    return jnp.where(mask, 1.0, 0.0).astype(BF16)


def call(kernel, outs, specs, args, flops, scratch=(), out_specs=None, grid=()):
    bytes_accessed = sum(a.size * a.dtype.itemsize for a in args) + sum(
        o.size * o.dtype.itemsize for o in outs
    )
    return pl.pallas_call(
        kernel,
        out_shape=outs,
        in_specs=specs,
        out_specs=out_specs or [VM] * len(outs),
        grid=grid,
        cost_estimate=pl.CostEstimate(
            flops=flops, bytes_accessed=bytes_accessed, transcendentals=0
        ),
        scratch_shapes=scratch,
        compiler_params=pltpu.CompilerParams(vmem_limit_bytes=GRANT),
    )(*args)


def shard_and_row(idx_ref):
    idx = idx_ref[...]
    shard = lax.shift_right_logical(idx, 8)
    return shard, idx & (SPAN - 1)


def ranks(shard, row):
    in_shard = ones_where(iota((N_ROW, NNZ), 0) == shard)
    at_row = ones_where(iota((SPAN, NNZ), 0) == row)
    used = dot(in_shard, at_row, 1, 1) > 0.5
    before = ones_where(iota((SPAN, SPAN), 0) < iota((SPAN, SPAN), 1))
    return in_shard, used, dot(ones_where(used), before)


def ids_kernel(idx_ref, ids_ref):
    _, used, rank = ranks(*shard_and_row(idx_ref))
    column = iota((N_ROW, SPAN), 1).astype(F32)
    lane = iota((N_ROW, D), 1)
    ids = jnp.zeros((N_ROW, D), F32)
    for k in range(CAP):
        mine = jnp.sum(
            jnp.where(used & (rank == float(k)), column, 0.0), axis=1, keepdims=True
        )
        ids = jnp.where(lane == k, mine, ids)
    ids_ref[...] = ids.astype(I32)


def counts_kernel(idx_ref, len_ref, use_ref, use_t_ref):
    shard, row = shard_and_row(idx_ref)
    in_shard, _, rank = ranks(shard, row)
    rank_at = dot(rank.astype(BF16), in_shard, 0, 0)
    rank = jnp.sum(jnp.where(iota((SPAN, NNZ), 0) == row, rank_at, 0.0), axis=0, keepdims=True)
    slot = shard * CAP + rank.astype(I32)
    at_slot = ones_where(iota((SLOTS, NNZ), 0) == slot)
    lengths = jnp.broadcast_to(len_ref[...].astype(F32), (BAGS, BAGS))
    a, b = iota((BAGS, BAGS), 0), iota((BAGS, BAGS), 1)
    starts = jnp.sum(jnp.where(b < a, lengths, 0.0), axis=1, keepdims=True).astype(I32)
    ends = jnp.sum(jnp.where(b <= a, lengths, 0.0), axis=1, keepdims=True).astype(I32)
    place = iota((BAGS, NNZ), 1)
    in_bag = ones_where((place >= starts) & (place < ends))
    use_ref[...] = dot(in_bag, at_slot, 1, 1).astype(BF16)
    use_t_ref[...] = dot(at_slot, in_bag, 1, 1).astype(BF16)


def table_kernel(hot_ref, serving_ref, scale_ref, table_ref, buf, sem):
    copies = [
        pltpu.make_async_copy(
            serving_ref.at[pl.ds(pl.multiple_of(hot_ref[0, j] * BLOCK, BLOCK), BLOCK)],
            buf.at[j],
            sem.at[j],
        )
        for j in range(2)
    ]
    for c in copies:
        c.start()
    scales = scale_ref[...].astype(F32)
    lane = iota(scales.shape, 1)
    for j, c in enumerate(copies):
        own = jnp.sum(jnp.where(lane == hot_ref[0, j], scales, 0.0), axis=1, keepdims=True)
        c.wait()
        table_ref[j * BLOCK : (j + 1) * BLOCK, :] = (buf[j].astype(F32) * own).astype(BF16)


def pick_kernel(core_ref, ids_ref, table_ref, other_ref, rows_ref):
    owner = ones_where(lax.shift_right_logical(iota((SLOTS, N_ROW), 0), 3) == iota((SLOTS, N_ROW), 1))
    spread = dot(owner, ids_ref[...].astype(F32).astype(BF16))
    mine = iota((SLOTS, D), 1) == (iota((SLOTS, D), 0) & (CAP - 1))
    column = dot(jnp.where(mine, spread, 0.0).astype(BF16), jnp.ones((D, SPAN), BF16))
    here = lax.shift_right_logical(iota((SLOTS, SPAN), 0), 3) & 1 == core_ref[0]
    match = iota((SLOTS, SPAN), 1) == column.astype(I32)
    rows = dot(ones_where(match & here), table_ref[...])
    rows_ref[...] = (rows + dot(ones_where(match & ~here), other_ref[...])).astype(BF16)


def place_kernel(core_ref, ids_ref, other_ref, place_ref):
    slot = iota((SLOTS, N_ROW), 0)
    line = lax.shift_right_logical(slot, 4) * 2 + core_ref[0] == iota((SLOTS, N_ROW), 1)
    here = lax.shift_right_logical(slot, 3) & 1 == core_ref[0]
    spread = dot(ids_ref[...].astype(F32).astype(BF16), ones_where(line & here), 0, 1)
    spread = spread + dot(other_ref[...].astype(F32).astype(BF16), ones_where(line & ~here), 0, 1)
    mine = iota((D, SLOTS), 0) == (iota((D, SLOTS), 1) & (CAP - 1))
    line = jnp.sum(jnp.where(mine, spread, 0.0), axis=0, keepdims=True).astype(I32)
    place_ref[...] = ones_where(iota((SPAN, SLOTS), 0) == line)


def dense_kernel(dense_ref, w_ref, labels_ref, w_out_ref, pre_ref, labels_out_ref, w_out_out_ref):
    pre_ref[...] = dot(dense_ref[...], w_ref[D : 2 * D, :])
    a, b = iota((BAGS, BAGS), 0), iota((BAGS, BAGS), 1)
    labels = jnp.sum(
        jnp.where(a == b, jnp.broadcast_to(labels_ref[...], (BAGS, BAGS)), 0.0),
        axis=1,
        keepdims=True,
    )
    labels_out_ref[...] = jnp.broadcast_to(labels, (BAGS, D))
    w_out_out_ref[...] = w_out_ref[...]


def by_tile(ref, value):
    for i in range(8):
        for j in range(8):
            ref[i * 8 + j] = value[i * 16 : (i + 1) * 16, j * 128 : (j + 1) * 128]


def step_kernel(
    core_ref, rows_ref, use_ref, dense_ref, pre_ref, labels_ref, w_ref, w_out_ref,
    give_ref, keep_ref, dpre_ref,
):
    pooled = dot(use_ref[...], rows_ref[...]).astype(BF16)
    pre = pre_ref[...] + dot(pooled, w_ref[0:D, :])
    sig = jax.nn.sigmoid(pre)
    w_out = w_out_ref[...]
    logit = jnp.sum(pre * sig * w_out, axis=1, keepdims=True)
    dlogit = jax.nn.sigmoid(logit) - labels_ref[:, 0:1]
    dpre = (dlogit * w_out * (sig * (1.0 + pre * (1.0 - sig)))).astype(BF16)
    dpre_ref[...] = dpre
    first = core_ref[0] == 0
    dense = dense_ref[...]
    by_tile(give_ref, dot(jnp.where(first, dense, pooled), dpre, 0, 0).astype(BF16))
    keep_ref[...] = jnp.where(first, pooled, dense)


def rest_kernel(keep_ref, dpre_ref, w_ref, use_t_ref, kept_ref, out_ref):
    dpre = dpre_ref[...]
    pooled_grad = dot(dpre, w_ref[0:D, :], 1, 1)
    high = pooled_grad.astype(BF16)
    low = (pooled_grad - high.astype(F32)).astype(BF16)
    use_t = use_t_ref[...]
    out_ref[...] = (dot(use_t, high) + dot(use_t, low)).astype(BF16)
    by_tile(kept_ref, dot(keep_ref[...], dpre, 0, 0))


def parts_kernel(keep_ref, given_ref, row_grad_ref, out_ref):
    at = pl.ds(pl.program_id(0) * 16, 16)
    out_ref[:, 0:16, :] = (keep_ref[at] + given_ref[at].astype(F32)).astype(BF16)
    out_ref[:, 16:24, :] = row_grad_ref[at]


def owned_kernel(got_ref, place_ref, hot_ref, out_ref):
    grads = got_ref[:, :, 16:24, :].astype(F32).reshape(SLOTS, D).astype(BF16)
    out_ref[0:SPAN, :] = dot(place_ref[...], grads).astype(BF16)
    for half in range(2):
        at = SPAN + 16 * half
        out_ref[at : at + 16, :] = jnp.sum(
            got_ref[:, half, 0:16, :].astype(F32), axis=0
        ).astype(BF16)
    lane = iota((16, D), 1)
    hot = jnp.where(lane == 0, hot_ref[0, 0], jnp.where(lane == 1, hot_ref[0, 1], 0))
    out_ref[SPAN + 32 : SPAN + 48, :] = hot.astype(F32).astype(BF16)


def top_kernel(me_ref, x0_ref, x1_ref, x2_ref, x3_ref, top_ref, by_group):
    me = me_ref[0]
    for o, ref in enumerate((x0_ref, x1_ref, x2_ref, x3_ref)):
        by_group[me ^ o] = ref[SPAN : SPAN + 32, :]
    top = jnp.zeros((32, D), F32)
    for g in range(N_GRP):
        top = top + by_group[g].astype(F32)
    top_ref[...] = jnp.broadcast_to(top.astype(BF16)[None], (N_ROW // 2, 32, D))


def update_kernel(
    me_ref, x0_ref, x1_ref, x2_ref, x3_ref, master_ref, accum_ref,
    new_master_ref, new_accum_ref, coded_ref, by_group,
):
    me = me_ref[0]
    for o, ref in enumerate((x0_ref, x1_ref, x2_ref, x3_ref)):
        by_group[me ^ o] = ref[...]
    hot = [by_group[g, SPAN + 32 : SPAN + 48, :].astype(F32)[0:1, :] for g in range(N_GRP)]
    a, b = iota((BLOCK, BLOCK), 0), iota((BLOCK, BLOCK), 1)
    diagonal = a == b
    lane = iota((16, D), 1)
    scale_row = jnp.zeros((16, D), F32)
    for q in range(4):
        grad = jnp.zeros((BLOCK, D), F32)
        number = (me * 4 + q).astype(F32)
        for g in range(N_GRP):
            for j in range(2):
                block = by_group[g, j * BLOCK : (j + 1) * BLOCK, :].astype(F32)
                grad = grad + jnp.where(hot[g][:, j : j + 1] == number, block, 0.0)
        at = pl.ds(q * BLOCK, BLOCK)
        accum = jnp.broadcast_to(accum_ref[:, q * BLOCK : (q + 1) * BLOCK], (BLOCK, BLOCK))
        state = jnp.sum(jnp.where(diagonal, accum, 0.0), axis=1, keepdims=True) + jnp.mean(
            grad * grad, axis=1, keepdims=True
        )
        new_accum_ref[:, q * BLOCK : (q + 1) * BLOCK] = jnp.sum(
            jnp.where(diagonal, jnp.broadcast_to(state, (BLOCK, BLOCK)), 0.0), axis=0, keepdims=True
        )
        weights = master_ref[at, :] - grad * (LR / jnp.sqrt(state))
        new_master_ref[at, :] = weights
        largest = jnp.max(jnp.max(jnp.abs(weights), axis=0, keepdims=True), axis=1, keepdims=True)
        scale = (largest + 1e-06).astype(BF16).astype(F32)
        coded_ref[at, :] = (weights / scale).astype(BF16)
        scale_row = jnp.where(lane == me * 4 + q, scale, scale_row)
    coded_ref[pl.ds(QUARTER, 16), :] = scale_row.astype(BF16)


def fresh_kernel(me_ref, s0_ref, s1_ref, s2_ref, s3_ref, serving_ref, scale_ref):
    me = me_ref[0]
    scales = jnp.zeros((16, D), F32)
    for o, ref in enumerate((s0_ref, s1_ref, s2_ref, s3_ref)):
        start = pl.multiple_of((me ^ o) * QUARTER, QUARTER)
        serving_ref[pl.ds(start, QUARTER), :] = ref[0:QUARTER, :]
        scales = scales + ref[QUARTER : QUARTER + 16, :].astype(F32)
    scale_ref[...] = scales[0:1, 0:16].astype(BF16)


def last_kernel(core_ref, mine_ref, other_ref, top_ref):
    step = pl.program_id(0)
    half = pl.ds(pl.multiple_of(step // 2 * 16, 16), 16)
    for ref, core in ((mine_ref, core_ref[0]), (other_ref, 1 - core_ref[0])):
        for s in range(16):
            column = pl.multiple_of((s % 4 * 2 + core) * 128, 128)
            line = s // 4 * 16
            top_ref[line : line + 16, pl.ds(column, 128)] = ref[
                step % 2 * 16 + s, half, :
            ].astype(F32)


def like(shape, dtype):
    return jax.ShapeDtypeStruct(shape, dtype)


def over_groups(x):
    parts = [x]
    for o in (1, 2, 3):
        parts.append(lax.ppermute(x, "grp", [(g, g ^ o) for g in range(N_GRP)]))
    return parts


def other_core(x):
    return lax.ppermute(x, "row_2", [(0, 1), (1, 0)])


def exchange(x, axes=ROW):
    return lax.all_to_all(x, axes, 0, 0, tiled=True)


def on_device(
    serving, serving_scale, hot_blocks, bag_lengths, bag_indices, dense_act, labels, w_top, w_out, master, accum,
):
    me = lax.axis_index("grp").astype(I32).reshape(1)
    core = lax.axis_index("row_2").astype(I32).reshape(1)
    (ids,) = call(ids_kernel, [like((N_ROW, D), I32)], [VM], (bag_indices,), 1 << 26)
    wanted = exchange(ids.reshape(N_ROW // 2, 2, D), CHIPS).reshape(N_ROW, D)
    use, use_t = call(
        counts_kernel,
        [like((BAGS, SLOTS), BF16), like((SLOTS, BAGS), BF16)],
        [VM] * 2,
        (bag_indices, bag_lengths),
        1 << 29,
    )
    (table,) = call(
        table_kernel,
        [like((SPAN, D), BF16)],
        [SM, pl.BlockSpec(memory_space=pl.ANY), VM],
        (hot_blocks, serving, serving_scale.reshape(1, 16)),
        1 << 20,
        [pltpu.VMEM((2, BLOCK, D), BF16), pltpu.SemaphoreType.DMA((2,))],
    )
    pre, labels_column, w_out_line = call(
        dense_kernel,
        [like((BAGS, FF), F32), like((BAGS, D), F32), like((1, FF), F32)],
        [VM] * 4,
        (dense_act, w_top, labels.reshape(1, BAGS), w_out.reshape(1, FF)),
        1 << 27,
    )
    other_table = other_core(table)
    wanted, table, other_table, pre, labels_column, w_out_line = lax.optimization_barrier(
        (wanted, table, other_table, pre, labels_column, w_out_line)
    )
    (rows,) = call(
        pick_kernel,
        [like((SLOTS, D), BF16)],
        [SM] + [VM] * 3,
        (core, wanted, table, other_table),
        1 << 26,
    )
    fetched = exchange(rows.reshape(N_ROW // 2, 2 * CAP, D), CHIPS).reshape(SLOTS, D)
    other_wanted = other_core(wanted)
    (place,) = call(
        place_kernel,
        [like((SPAN, SLOTS), BF16)],
        [SM] + [VM] * 2,
        (core, wanted, other_wanted),
        1 << 26,
    )
    give, keep, dpre = call(
        step_kernel,
        [like((N_ROW, 16, D), BF16), like((BAGS, D), BF16), like((BAGS, FF), BF16)],
        [SM] + [VM] * 7,
        (core, fetched, use, dense_act, pre, labels_column, w_top, w_out_line),
        1 << 29,
    )
    given = other_core(give)
    kept, row_grad = call(
        rest_kernel,
        [like((N_ROW, 16, D), F32), like((SLOTS, D), BF16)],
        [VM] * 4,
        (keep, dpre, w_top, use_t),
        1 << 28,
    )
    (parts,) = call(
        parts_kernel,
        [like((N_ROW, 24, D), BF16)],
        [VM] * 3,
        (kept, given, row_grad.reshape(N_ROW, CAP, D)),
        1 << 20,
        out_specs=[pl.BlockSpec((16, 24, D), lambda i: (i, 0, 0))],
        grid=(4,),
    )
    got = exchange(parts)
    (own,) = call(
        owned_kernel,
        [like((SPAN + 48, D), BF16)],
        [VM, VM, SM],
        (got.reshape(N_ROW // 2, 2, 24, D), place, hot_blocks),
        1 << 26,
    )
    owned = over_groups(own)
    (top_part,) = call(
        top_kernel,
        [like((N_ROW // 2, 32, D), BF16)],
        [SM] + [VM] * 4,
        (me, *owned),
        1 << 16,
        [pltpu.VMEM((N_GRP, 32, D), BF16)],
    )
    top_mine = exchange(top_part, CHIPS)
    new_master, new_accum, coded = call(
        update_kernel,
        [like((QUARTER, D), F32), like((1, QUARTER), F32), like((QUARTER + 16, D), BF16)],
        [SM] + [VM] * 6,
        (me, *owned, master[0], accum),
        1 << 22,
        [pltpu.VMEM((N_GRP, SPAN + 48, D), BF16)],
    )
    quarters = over_groups(coded)
    fresh, fresh_scale = call(
        fresh_kernel,
        [like((4 * QUARTER, D), BF16), like((1, 16), BF16)],
        [SM] + [VM] * 4,
        (me, *quarters),
        1 << 20,
    )
    top_other = other_core(top_mine)
    (top_grad,) = call(
        last_kernel,
        [like((2 * D, FF), F32)],
        [SM] + [VM] * 2,
        (core, top_mine, top_other),
        1 << 20,
        out_specs=[pl.BlockSpec((64, FF), lambda i: (i, 0))],
        grid=(4,),
    )
    return new_master[None], new_accum, fresh, fresh_scale.reshape(16), top_grad


def solution(mesh):
    finer = Mesh(
        mesh.devices.reshape(mesh.shape["grp"], 4, 8, 2), ("grp", "row_0", "row_1", "row_2")
    )
    in_specs = (
        P(ROW, None),
        P(ROW),
        P("grp", ROW),
        P(GRP_ROW, None),
        P(GRP_ROW, None),
        P(GRP_ROW, None),
        P(GRP_ROW),
        P(),
        P(),
        P("grp", ROW, None),
        P("grp", ROW),
    )
    out_specs = (P("grp", ROW, None), P("grp", ROW), P(ROW, None), P(ROW), P())
    return jax.shard_map(
        on_device, mesh=finer, in_specs=in_specs, out_specs=out_specs, check_vma=False
    )
```

```python
import jax
import jax.numpy as jnp
from jax import lax
from jax.experimental import pallas as pl
from jax.experimental.pallas import tpu as pltpu
from jax.sharding import Mesh
from jax.sharding import PartitionSpec as P


ROW = ("row_0", "row_1", "row_2")
CHIPS = ("row_0", "row_1")
GRP_ROW = ("grp", "row_0", "row_1", "row_2")
N_GRP = 4
N_ROW = 64
BLOCK = 128
SPAN = 256
CAP = 8
BAGS = 256
NNZ = 1024
SLOTS = N_ROW * CAP
D = 128
FF = 1024
QUARTER = 512
LR = 0.05
GRANT = 16 << 20
F32 = jnp.float32
BF16 = jnp.bfloat16
I32 = jnp.int32
VM = pl.BlockSpec(memory_space=pltpu.VMEM)
SM = pl.BlockSpec(memory_space=pltpu.SMEM)
ANY = pl.BlockSpec(memory_space=pl.ANY)


def iota(shape, dim):
    return lax.broadcasted_iota(I32, shape, dim)


def dot(a, b, ca=1, cb=0):
    return lax.dot_general(a, b, (((ca,), (cb,)), ((), ())), preferred_element_type=F32)


def ones_where(mask):
    return jnp.where(mask, 1.0, 0.0).astype(BF16)


def call(kernel, outs, specs, args, flops, scratch=(), out_specs=None):
    bytes_accessed = sum(a.size * a.dtype.itemsize for a in args) + sum(
        o.size * o.dtype.itemsize for o in outs
    )
    return pl.pallas_call(
        kernel,
        out_shape=outs,
        in_specs=specs,
        out_specs=out_specs or [VM] * len(outs),
        cost_estimate=pl.CostEstimate(
            flops=flops, bytes_accessed=bytes_accessed, transcendentals=0
        ),
        scratch_shapes=scratch,
        compiler_params=pltpu.CompilerParams(vmem_limit_bytes=GRANT),
    )(*args)


def shard_and_row(idx_ref):
    idx = idx_ref[...]
    shard = lax.shift_right_logical(idx, 8)
    return shard, idx & (SPAN - 1)


def ranks(shard, row):
    in_shard = ones_where(iota((N_ROW, NNZ), 0) == shard)
    at_row = ones_where(iota((SPAN, NNZ), 0) == row)
    used = dot(in_shard, at_row, 1, 1) > 0.5
    before = ones_where(iota((SPAN, SPAN), 0) < iota((SPAN, SPAN), 1))
    return in_shard, used, dot(ones_where(used), before)


def ids_kernel(idx_ref, ids_ref):
    _, used, rank = ranks(*shard_and_row(idx_ref))
    column = iota((N_ROW, SPAN), 1).astype(F32)
    lane = iota((N_ROW, D), 1)
    ids = jnp.zeros((N_ROW, D), F32)
    for k in range(CAP):
        mine = jnp.sum(
            jnp.where(used & (rank == float(k)), column, 0.0), axis=1, keepdims=True
        )
        ids = jnp.where(lane == k, mine, ids)
    ids_ref[...] = ids.astype(I32)


def counts_kernel(idx_ref, len_ref, use_ref, use_t_ref):
    shard, row = shard_and_row(idx_ref)
    in_shard, _, rank = ranks(shard, row)
    rank_at = dot(rank.astype(BF16), in_shard, 0, 0)
    rank = jnp.sum(jnp.where(iota((SPAN, NNZ), 0) == row, rank_at, 0.0), axis=0, keepdims=True)
    slot = shard * CAP + rank.astype(I32)
    at_slot = ones_where(iota((SLOTS, NNZ), 0) == slot)
    lengths = jnp.broadcast_to(len_ref[...].astype(F32), (BAGS, BAGS))
    a, b = iota((BAGS, BAGS), 0), iota((BAGS, BAGS), 1)
    starts = jnp.sum(jnp.where(b < a, lengths, 0.0), axis=1, keepdims=True).astype(I32)
    ends = jnp.sum(jnp.where(b <= a, lengths, 0.0), axis=1, keepdims=True).astype(I32)
    place = iota((BAGS, NNZ), 1)
    in_bag = ones_where((place >= starts) & (place < ends))
    use_ref[...] = dot(in_bag, at_slot, 1, 1).astype(BF16)
    use_t_ref[...] = dot(at_slot, in_bag, 1, 1).astype(BF16)


def table_kernel(hot_ref, serving_ref, scale_ref, table_ref, buf, sem):
    copies = [
        pltpu.make_async_copy(
            serving_ref.at[pl.ds(pl.multiple_of(hot_ref[0, j] * BLOCK, BLOCK), BLOCK)],
            buf.at[j],
            sem.at[j],
        )
        for j in range(2)
    ]
    for c in copies:
        c.start()
    scales = scale_ref[...].astype(F32)
    lane = iota(scales.shape, 1)
    for j, c in enumerate(copies):
        own = jnp.sum(jnp.where(lane == hot_ref[0, j], scales, 0.0), axis=1, keepdims=True)
        c.wait()
        table_ref[j * BLOCK : (j + 1) * BLOCK, :] = (buf[j].astype(F32) * own).astype(BF16)


def pick_kernel(core_ref, ids_ref, table_ref, other_ref, rows_ref):
    owner = ones_where(lax.shift_right_logical(iota((SLOTS, N_ROW), 0), 3) == iota((SLOTS, N_ROW), 1))
    spread = dot(owner, ids_ref[...].astype(F32).astype(BF16))
    mine = iota((SLOTS, D), 1) == (iota((SLOTS, D), 0) & (CAP - 1))
    column = jnp.sum(jnp.where(mine, spread, 0.0), axis=1, keepdims=True).astype(I32)
    here = lax.shift_right_logical(iota((SLOTS, SPAN), 0), 3) & 1 == core_ref[0]
    match = iota((SLOTS, SPAN), 1) == column
    rows = dot(ones_where(match & here), table_ref[...])
    rows_ref[...] = (rows + dot(ones_where(match & ~here), other_ref[...])).astype(BF16)


def place_kernel(core_ref, ids_ref, other_ref, place_ref):
    slot = iota((SLOTS, N_ROW), 0)
    line = lax.shift_right_logical(slot, 4) * 2 + core_ref[0] == iota((SLOTS, N_ROW), 1)
    here = lax.shift_right_logical(slot, 3) & 1 == core_ref[0]
    spread = dot(ids_ref[...].astype(F32).astype(BF16), ones_where(line & here), 0, 1)
    spread = spread + dot(other_ref[...].astype(F32).astype(BF16), ones_where(line & ~here), 0, 1)
    mine = iota((D, SLOTS), 0) == (iota((D, SLOTS), 1) & (CAP - 1))
    line = jnp.sum(jnp.where(mine, spread, 0.0), axis=0, keepdims=True).astype(I32)
    place_ref[...] = ones_where(iota((SPAN, SLOTS), 0) == line)


def dense_kernel(dense_ref, w_ref, labels_ref, w_out_ref, pre_ref, labels_out_ref, w_out_out_ref):
    pre_ref[...] = dot(dense_ref[...], w_ref[D : 2 * D, :])
    a, b = iota((BAGS, BAGS), 0), iota((BAGS, BAGS), 1)
    labels = jnp.sum(
        jnp.where(a == b, jnp.broadcast_to(labels_ref[...], (BAGS, BAGS)), 0.0),
        axis=1,
        keepdims=True,
    )
    labels_out_ref[...] = jnp.broadcast_to(labels, (BAGS, D))
    w_out_out_ref[...] = w_out_ref[...]


def by_tile(ref, value):
    for i in range(8):
        for j in range(8):
            ref[i * 8 + j] = value[i * 16 : (i + 1) * 16, j * 128 : (j + 1) * 128]


def step_kernel(
    core_ref, rows_ref, use_ref, dense_ref, pre_ref, labels_ref, w_ref, w_out_ref,
    give_ref, keep_ref, dpre_ref,
):
    pooled = dot(use_ref[...], rows_ref[...]).astype(BF16)
    pre = pre_ref[...] + dot(pooled, w_ref[0:D, :])
    sig = jax.nn.sigmoid(pre)
    w_out = w_out_ref[...]
    logit = jnp.sum(pre * sig * w_out, axis=1, keepdims=True)
    dlogit = jax.nn.sigmoid(logit) - labels_ref[:, 0:1]
    dpre = (dlogit * w_out * (sig * (1.0 + pre * (1.0 - sig)))).astype(BF16)
    dpre_ref[...] = dpre
    first = core_ref[0] == 0
    dense = dense_ref[...]
    by_tile(give_ref, dot(jnp.where(first, dense, pooled), dpre, 0, 0).astype(BF16))
    keep_ref[...] = jnp.where(first, pooled, dense)


def rest_kernel(keep_ref, dpre_ref, w_ref, use_t_ref, kept_ref, out_ref):
    dpre = dpre_ref[...]
    pooled_grad = dot(dpre, w_ref[0:D, :], 1, 1)
    high = pooled_grad.astype(BF16)
    low = (pooled_grad - high.astype(F32)).astype(BF16)
    use_t = use_t_ref[...]
    out_ref[...] = (dot(use_t, high) + dot(use_t, low)).astype(BF16)
    by_tile(kept_ref, dot(keep_ref[...], dpre, 0, 0))


def store_quarters(fill, out_ref, buf, sem):
    size = out_ref.shape[0] // 4
    copies = []
    for i in range(4):
        fill(i)
        copies.append(
            pltpu.make_async_copy(buf.at[i], out_ref.at[pl.ds(i * size, size)], sem.at[i])
        )
        copies[i].start()
    for copy in copies:
        copy.wait()


def quarters_of(shape, dtype):
    return [pltpu.VMEM((4, shape[0] // 4, *shape[1:]), dtype), pltpu.SemaphoreType.DMA((4,))]


def parts_kernel(keep_ref, given_ref, row_grad_ref, out_ref, buf, sem):
    def fill(i):
        at = slice(i * 16, (i + 1) * 16)
        buf[i, :, 0:16, :] = (keep_ref[at] + given_ref[at].astype(F32)).astype(BF16)
        buf[i, :, 16:24, :] = row_grad_ref[at]

    store_quarters(fill, out_ref, buf, sem)


def owned_kernel(got_ref, place_ref, hot_ref, out_ref):
    grads = got_ref[:, :, 16:24, :].astype(F32).reshape(SLOTS, D).astype(BF16)
    out_ref[0:SPAN, :] = dot(place_ref[...], grads).astype(BF16)
    for half in range(2):
        at = SPAN + 16 * half
        out_ref[at : at + 16, :] = jnp.sum(
            got_ref[:, half, 0:16, :].astype(F32), axis=0
        ).astype(BF16)
    lane = iota((16, D), 1)
    hot = jnp.where(lane == 0, hot_ref[0, 0], jnp.where(lane == 1, hot_ref[0, 1], 0))
    out_ref[SPAN + 32 : SPAN + 48, :] = hot.astype(F32).astype(BF16)


def top_kernel(me_ref, x0_ref, x1_ref, x2_ref, x3_ref, top_ref, by_group):
    me = me_ref[0]
    for o, ref in enumerate((x0_ref, x1_ref, x2_ref, x3_ref)):
        by_group[me ^ o] = ref[SPAN : SPAN + 32, :]
    top = jnp.zeros((32, D), F32)
    for g in range(N_GRP):
        top = top + by_group[g].astype(F32)
    top_ref[...] = jnp.broadcast_to(top.astype(BF16)[None], (N_ROW // 2, 32, D))


def update_kernel(
    me_ref, x0_ref, x1_ref, x2_ref, x3_ref, master_ref, accum_ref,
    new_master_ref, new_accum_ref, coded_ref, by_group,
):
    me = me_ref[0]
    for o, ref in enumerate((x0_ref, x1_ref, x2_ref, x3_ref)):
        by_group[me ^ o] = ref[...]
    hot = [by_group[g, SPAN + 32 : SPAN + 48, :].astype(F32)[0:1, :] for g in range(N_GRP)]
    a, b = iota((BLOCK, BLOCK), 0), iota((BLOCK, BLOCK), 1)
    diagonal = a == b
    lane = iota((16, D), 1)
    scale_row = jnp.zeros((16, D), F32)
    for q in range(4):
        grad = jnp.zeros((BLOCK, D), F32)
        number = (me * 4 + q).astype(F32)
        for g in range(N_GRP):
            for j in range(2):
                block = by_group[g, j * BLOCK : (j + 1) * BLOCK, :].astype(F32)
                grad = grad + jnp.where(hot[g][:, j : j + 1] == number, block, 0.0)
        at = pl.ds(q * BLOCK, BLOCK)
        accum = jnp.broadcast_to(accum_ref[:, q * BLOCK : (q + 1) * BLOCK], (BLOCK, BLOCK))
        state = jnp.sum(jnp.where(diagonal, accum, 0.0), axis=1, keepdims=True) + jnp.mean(
            grad * grad, axis=1, keepdims=True
        )
        new_accum_ref[:, q * BLOCK : (q + 1) * BLOCK] = jnp.sum(
            jnp.where(diagonal, jnp.broadcast_to(state, (BLOCK, BLOCK)), 0.0), axis=0, keepdims=True
        )
        weights = master_ref[at, :] - grad * (LR / jnp.sqrt(state))
        new_master_ref[at, :] = weights
        largest = jnp.max(jnp.max(jnp.abs(weights), axis=0, keepdims=True), axis=1, keepdims=True)
        scale = (largest + 1e-06).astype(BF16).astype(F32)
        coded_ref[at, :] = (weights / scale).astype(BF16)
        scale_row = jnp.where(lane == me * 4 + q, scale, scale_row)
    coded_ref[pl.ds(QUARTER, 16), :] = scale_row.astype(BF16)


def fresh_kernel(me_ref, s0_ref, s1_ref, s2_ref, s3_ref, serving_ref, scale_ref):
    me = me_ref[0]
    scales = jnp.zeros((16, D), F32)
    for o, ref in enumerate((s0_ref, s1_ref, s2_ref, s3_ref)):
        start = pl.multiple_of((me ^ o) * QUARTER, QUARTER)
        serving_ref[pl.ds(start, QUARTER), :] = ref[0:QUARTER, :]
        scales = scales + ref[QUARTER : QUARTER + 16, :].astype(F32)
    scale_ref[...] = scales[0:1, 0:16].astype(BF16)


def last_kernel(core_ref, mine_ref, other_ref, top_ref, buf, sem):
    def fill(i):
        half = slice(i // 2 * 16, i // 2 * 16 + 16)
        for ref, core in ((mine_ref, core_ref[0]), (other_ref, 1 - core_ref[0])):
            for s in range(16):
                column = pl.multiple_of((s % 4 * 2 + core) * 128, 128)
                line = s // 4 * 16
                buf[i, line : line + 16, pl.ds(column, 128)] = ref[
                    i % 2 * 16 + s, half, :
                ].astype(F32)

    store_quarters(fill, top_ref, buf, sem)


def like(shape, dtype):
    return jax.ShapeDtypeStruct(shape, dtype)


def over_groups(x):
    parts = [x]
    for o in (1, 2, 3):
        parts.append(lax.ppermute(x, "grp", [(g, g ^ o) for g in range(N_GRP)]))
    return parts


def other_core(x):
    return lax.ppermute(x, "row_2", [(0, 1), (1, 0)])


def exchange(x, axes=ROW):
    return lax.all_to_all(x, axes, 0, 0, tiled=True)


def on_device(
    serving, serving_scale, hot_blocks, bag_lengths, bag_indices, dense_act, labels, w_top, w_out, master, accum,
):
    me = lax.axis_index("grp").astype(I32).reshape(1)
    core = lax.axis_index("row_2").astype(I32).reshape(1)
    (ids,) = call(ids_kernel, [like((N_ROW, D), I32)], [VM], (bag_indices,), 1 << 26)
    wanted = exchange(ids.reshape(N_ROW // 2, 2, D), CHIPS).reshape(N_ROW, D)
    use, use_t = call(
        counts_kernel,
        [like((BAGS, SLOTS), BF16), like((SLOTS, BAGS), BF16)],
        [VM] * 2,
        (bag_indices, bag_lengths),
        1 << 29,
    )
    (table,) = call(
        table_kernel,
        [like((SPAN, D), BF16)],
        [SM, pl.BlockSpec(memory_space=pl.ANY), VM],
        (hot_blocks, serving, serving_scale.reshape(1, 16)),
        1 << 20,
        [pltpu.VMEM((2, BLOCK, D), BF16), pltpu.SemaphoreType.DMA((2,))],
    )
    pre, labels_column, w_out_line = call(
        dense_kernel,
        [like((BAGS, FF), F32), like((BAGS, D), F32), like((1, FF), F32)],
        [VM] * 4,
        (dense_act, w_top, labels.reshape(1, BAGS), w_out.reshape(1, FF)),
        1 << 27,
    )
    other_table = other_core(table)
    wanted, table, other_table, pre, labels_column, w_out_line = lax.optimization_barrier(
        (wanted, table, other_table, pre, labels_column, w_out_line)
    )
    (rows,) = call(
        pick_kernel,
        [like((SLOTS, D), BF16)],
        [SM] + [VM] * 3,
        (core, wanted, table, other_table),
        1 << 26,
    )
    fetched = exchange(rows.reshape(N_ROW // 2, 2 * CAP, D), CHIPS).reshape(SLOTS, D)
    other_wanted = other_core(wanted)
    (place,) = call(
        place_kernel,
        [like((SPAN, SLOTS), BF16)],
        [SM] + [VM] * 2,
        (core, wanted, other_wanted),
        1 << 26,
    )
    give, keep, dpre = call(
        step_kernel,
        [like((N_ROW, 16, D), BF16), like((BAGS, D), BF16), like((BAGS, FF), BF16)],
        [SM] + [VM] * 7,
        (core, fetched, use, dense_act, pre, labels_column, w_top, w_out_line),
        1 << 29,
    )
    given = other_core(give)
    kept, row_grad = call(
        rest_kernel,
        [like((N_ROW, 16, D), F32), like((SLOTS, D), BF16)],
        [VM] * 4,
        (keep, dpre, w_top, use_t),
        1 << 28,
    )
    (parts,) = call(
        parts_kernel,
        [like((N_ROW, 24, D), BF16)],
        [VM] * 3,
        (kept, given, row_grad.reshape(N_ROW, CAP, D)),
        1 << 20,
        quarters_of((N_ROW, 24, D), BF16),
        [ANY],
    )
    got = exchange(parts)
    (own,) = call(
        owned_kernel,
        [like((SPAN + 48, D), BF16)],
        [VM, VM, SM],
        (got.reshape(N_ROW // 2, 2, 24, D), place, hot_blocks),
        1 << 26,
    )
    owned = over_groups(own)
    (top_part,) = call(
        top_kernel,
        [like((N_ROW // 2, 32, D), BF16)],
        [SM] + [VM] * 4,
        (me, *owned),
        1 << 16,
        [pltpu.VMEM((N_GRP, 32, D), BF16)],
    )
    top_mine = exchange(top_part, CHIPS)
    new_master, new_accum, coded = call(
        update_kernel,
        [like((QUARTER, D), F32), like((1, QUARTER), F32), like((QUARTER + 16, D), BF16)],
        [SM] + [VM] * 6,
        (me, *owned, master[0], accum),
        1 << 22,
        [pltpu.VMEM((N_GRP, SPAN + 48, D), BF16)],
    )
    quarters = over_groups(coded)
    fresh, fresh_scale = call(
        fresh_kernel,
        [like((4 * QUARTER, D), BF16), like((1, 16), BF16)],
        [SM] + [VM] * 4,
        (me, *quarters),
        1 << 20,
    )
    top_other = other_core(top_mine)
    (top_grad,) = call(
        last_kernel,
        [like((2 * D, FF), F32)],
        [SM] + [VM] * 2,
        (core, top_mine, top_other),
        1 << 20,
        quarters_of((2 * D, FF), F32),
        [ANY],
    )
    return new_master[None], new_accum, fresh, fresh_scale.reshape(16), top_grad


def solution(mesh):
    finer = Mesh(
        mesh.devices.reshape(mesh.shape["grp"], 4, 8, 2), ("grp", "row_0", "row_1", "row_2")
    )
    in_specs = (
        P(ROW, None),
        P(ROW),
        P("grp", ROW),
        P(GRP_ROW, None),
        P(GRP_ROW, None),
        P(GRP_ROW, None),
        P(GRP_ROW),
        P(),
        P(),
        P("grp", ROW, None),
        P("grp", ROW),
    )
    out_specs = (P("grp", ROW, None), P("grp", ROW), P(ROW, None), P(ROW), P())
    return jax.shard_map(
        on_device, mesh=finer, in_specs=in_specs, out_specs=out_specs, check_vma=False
    )
```

```python
import jax
import jax.numpy as jnp
from jax import lax
from jax.experimental import pallas as pl
from jax.experimental.pallas import tpu as pltpu
from jax.sharding import Mesh
from jax.sharding import PartitionSpec as P


ROW = ("row_0", "row_1", "row_2")
CHIPS = ("row_0", "row_1")
GRP_ROW = ("grp", "row_0", "row_1", "row_2")
N_GRP = 4
N_ROW = 64
BLOCK = 128
SPAN = 256
CAP = 8
BAGS = 256
NNZ = 1024
SLOTS = N_ROW * CAP
D = 128
FF = 1024
QUARTER = 512
LR = 0.05
GRANT = 16 << 20
F32 = jnp.float32
BF16 = jnp.bfloat16
I32 = jnp.int32
VM = pl.BlockSpec(memory_space=pltpu.VMEM)
SM = pl.BlockSpec(memory_space=pltpu.SMEM)
ANY = pl.BlockSpec(memory_space=pl.ANY)


def group():
    return lax.axis_index("grp").astype(I32)


def own_core():
    return lax.axis_index("row_2").astype(I32)


def iota(shape, dim):
    return lax.broadcasted_iota(I32, shape, dim)


def dot(a, b, ca=1, cb=0):
    return lax.dot_general(a, b, (((ca,), (cb,)), ((), ())), preferred_element_type=F32)


def ones_where(mask):
    return jnp.where(mask, 1.0, 0.0).astype(BF16)


def call(kernel, outs, specs, args, flops, scratch=(), out_specs=None):
    bytes_accessed = sum(a.size * a.dtype.itemsize for a in args) + sum(
        o.size * o.dtype.itemsize for o in outs
    )
    return pl.pallas_call(
        kernel,
        out_shape=outs,
        in_specs=specs,
        out_specs=out_specs or [VM] * len(outs),
        cost_estimate=pl.CostEstimate(
            flops=flops, bytes_accessed=bytes_accessed, transcendentals=0
        ),
        scratch_shapes=scratch,
        compiler_params=pltpu.CompilerParams(vmem_limit_bytes=GRANT),
    )(*args)


def shard_and_row(idx_ref):
    idx = idx_ref[...]
    shard = lax.shift_right_logical(idx, 8)
    return shard, idx & (SPAN - 1)


def ranks(shard, row):
    in_shard = ones_where(iota((N_ROW, NNZ), 0) == shard)
    at_row = ones_where(iota((SPAN, NNZ), 0) == row)
    used = dot(in_shard, at_row, 1, 1) > 0.5
    before = ones_where(iota((SPAN, SPAN), 0) < iota((SPAN, SPAN), 1))
    return in_shard, used, dot(ones_where(used), before)


def ids_kernel(idx_ref, ids_ref):
    _, used, rank = ranks(*shard_and_row(idx_ref))
    column = iota((N_ROW, SPAN), 1).astype(F32)
    lane = iota((N_ROW, D), 1)
    ids = jnp.zeros((N_ROW, D), F32)
    for k in range(CAP):
        mine = jnp.sum(
            jnp.where(used & (rank == float(k)), column, 0.0), axis=1, keepdims=True
        )
        ids = jnp.where(lane == k, mine, ids)
    ids_ref[...] = ids.astype(I32)


def counts_kernel(idx_ref, len_ref, use_ref, use_t_ref):
    shard, row = shard_and_row(idx_ref)
    in_shard, _, rank = ranks(shard, row)
    rank_at = dot(rank.astype(BF16), in_shard, 0, 0)
    rank = jnp.sum(jnp.where(iota((SPAN, NNZ), 0) == row, rank_at, 0.0), axis=0, keepdims=True)
    slot = shard * CAP + rank.astype(I32)
    at_slot = ones_where(iota((SLOTS, NNZ), 0) == slot)
    lengths = jnp.broadcast_to(len_ref[...].astype(F32), (BAGS, BAGS))
    a, b = iota((BAGS, BAGS), 0), iota((BAGS, BAGS), 1)
    starts = jnp.sum(jnp.where(b < a, lengths, 0.0), axis=1, keepdims=True).astype(I32)
    ends = jnp.sum(jnp.where(b <= a, lengths, 0.0), axis=1, keepdims=True).astype(I32)
    place = iota((BAGS, NNZ), 1)
    in_bag = ones_where((place >= starts) & (place < ends))
    use_ref[...] = dot(in_bag, at_slot, 1, 1).astype(BF16)
    use_t_ref[...] = dot(at_slot, in_bag, 1, 1).astype(BF16)


def table_kernel(hot_ref, serving_ref, scale_ref, table_ref, buf, sem):
    copies = [
        pltpu.make_async_copy(
            serving_ref.at[pl.ds(pl.multiple_of(hot_ref[0, j] * BLOCK, BLOCK), BLOCK)],
            buf.at[j],
            sem.at[j],
        )
        for j in range(2)
    ]
    for c in copies:
        c.start()
    scales = scale_ref[...].astype(F32)
    lane = iota(scales.shape, 1)
    for j, c in enumerate(copies):
        own = jnp.sum(jnp.where(lane == hot_ref[0, j], scales, 0.0), axis=1, keepdims=True)
        c.wait()
        table_ref[j * BLOCK : (j + 1) * BLOCK, :] = (buf[j].astype(F32) * own).astype(BF16)


def pick_kernel(ids_ref, table_ref, other_ref, rows_ref):
    owner = ones_where(lax.shift_right_logical(iota((SLOTS, N_ROW), 0), 3) == iota((SLOTS, N_ROW), 1))
    spread = dot(owner, ids_ref[...].astype(F32).astype(BF16))
    mine = iota((SLOTS, D), 1) == (iota((SLOTS, D), 0) & (CAP - 1))
    column = jnp.sum(jnp.where(mine, spread, 0.0), axis=1, keepdims=True).astype(I32)
    here = lax.shift_right_logical(iota((SLOTS, SPAN), 0), 3) & 1 == own_core()
    match = iota((SLOTS, SPAN), 1) == column
    rows = dot(ones_where(match & here), table_ref[...])
    rows_ref[...] = (rows + dot(ones_where(match & ~here), other_ref[...])).astype(BF16)


def place_kernel(hot_ref, ids_ref, other_ref, place_ref, hot_lines_ref):
    slot = iota((SLOTS, N_ROW), 0)
    line = lax.shift_right_logical(slot, 4) * 2 + own_core() == iota((SLOTS, N_ROW), 1)
    here = lax.shift_right_logical(slot, 3) & 1 == own_core()
    spread = dot(ids_ref[...].astype(F32).astype(BF16), ones_where(line & here), 0, 1)
    spread = spread + dot(other_ref[...].astype(F32).astype(BF16), ones_where(line & ~here), 0, 1)
    mine = iota((D, SLOTS), 0) == (iota((D, SLOTS), 1) & (CAP - 1))
    line = jnp.sum(jnp.where(mine, spread, 0.0), axis=0, keepdims=True).astype(I32)
    place_ref[...] = ones_where(iota((SPAN, SLOTS), 0) == line)
    lane = iota((16, D), 1)
    hot = jnp.where(lane == 0, hot_ref[0, 0], jnp.where(lane == 1, hot_ref[0, 1], 0))
    hot_lines_ref[...] = hot.astype(F32).astype(BF16)


def dense_kernel(dense_ref, w_ref, labels_ref, w_out_ref, pre_ref, labels_out_ref, w_out_out_ref):
    pre_ref[...] = dot(dense_ref[...], w_ref[D : 2 * D, :])
    a, b = iota((BAGS, BAGS), 0), iota((BAGS, BAGS), 1)
    labels = jnp.sum(
        jnp.where(a == b, jnp.broadcast_to(labels_ref[...], (BAGS, BAGS)), 0.0),
        axis=1,
        keepdims=True,
    )
    labels_out_ref[...] = jnp.broadcast_to(labels, (BAGS, D))
    w_out_out_ref[...] = w_out_ref[...]


def by_tile(ref, value):
    for i in range(8):
        for j in range(8):
            ref[i * 8 + j] = value[i * 16 : (i + 1) * 16, j * 128 : (j + 1) * 128]


def step_kernel(
    rows_ref, use_ref, dense_ref, pre_ref, labels_ref, w_ref, w_out_ref,
    give_ref, keep_ref, dpre_ref,
):
    pooled = dot(use_ref[...], rows_ref[...]).astype(BF16)
    pre = pre_ref[...] + dot(pooled, w_ref[0:D, :])
    sig = jax.nn.sigmoid(pre)
    w_out = w_out_ref[...]
    logit = jnp.sum(pre * sig * w_out, axis=1, keepdims=True)
    dlogit = jax.nn.sigmoid(logit) - labels_ref[:, 0:1]
    dpre = (dlogit * w_out * (sig * (1.0 + pre * (1.0 - sig)))).astype(BF16)
    dpre_ref[...] = dpre
    first = own_core() == 0
    dense = dense_ref[...]
    by_tile(give_ref, dot(jnp.where(first, dense, pooled), dpre, 0, 0).astype(BF16))
    keep_ref[...] = jnp.where(first, pooled, dense)


def rest_kernel(keep_ref, dpre_ref, w_ref, use_t_ref, kept_ref, out_ref):
    dpre = dpre_ref[...]
    pooled_grad = dot(dpre, w_ref[0:D, :], 1, 1)
    high = pooled_grad.astype(BF16)
    low = (pooled_grad - high.astype(F32)).astype(BF16)
    use_t = use_t_ref[...]
    out_ref[...] = (dot(use_t, high) + dot(use_t, low)).astype(BF16)
    by_tile(kept_ref, dot(keep_ref[...], dpre, 0, 0))


def store_quarters(fill, out_ref, buf, sem):
    size = out_ref.shape[0] // 4
    copies = []
    for i in range(4):
        fill(i)
        copies.append(
            pltpu.make_async_copy(buf.at[i], out_ref.at[pl.ds(i * size, size)], sem.at[i])
        )
        copies[i].start()
    for copy in copies:
        copy.wait()


def quarters_of(shape, dtype):
    return [pltpu.VMEM((4, shape[0] // 4, *shape[1:]), dtype), pltpu.SemaphoreType.DMA((4,))]


def parts_kernel(keep_ref, given_ref, row_grad_ref, out_ref, buf, sem):
    def fill(i):
        at = slice(i * 16, (i + 1) * 16)
        buf[i, :, 0:16, :] = (keep_ref[at] + given_ref[at].astype(F32)).astype(BF16)
        buf[i, :, 16:24, :] = row_grad_ref[at]

    store_quarters(fill, out_ref, buf, sem)


def owned_kernel(got_ref, place_ref, hot_lines_ref, out_ref):
    grads = got_ref[:, :, 16:24, :].astype(F32).reshape(SLOTS, D).astype(BF16)
    out_ref[0:SPAN, :] = dot(place_ref[...], grads).astype(BF16)
    for half in range(2):
        at = SPAN + 16 * half
        out_ref[at : at + 16, :] = jnp.sum(
            got_ref[:, half, 0:16, :].astype(F32), axis=0
        ).astype(BF16)
    out_ref[SPAN + 32 : SPAN + 48, :] = hot_lines_ref[...]


def top_kernel(x0_ref, x1_ref, x2_ref, x3_ref, top_ref, by_group):
    me = group()
    for o, ref in enumerate((x0_ref, x1_ref, x2_ref, x3_ref)):
        by_group[me ^ o] = ref[SPAN : SPAN + 32, :]
    top = jnp.zeros((32, D), F32)
    for g in range(N_GRP):
        top = top + by_group[g].astype(F32)
    top_ref[...] = jnp.broadcast_to(top.astype(BF16)[None], (N_ROW // 2, 32, D))


def update_kernel(
    x0_ref, x1_ref, x2_ref, x3_ref, master_ref, accum_ref,
    new_master_ref, new_accum_ref, coded_ref, by_group,
):
    me = group()
    for o, ref in enumerate((x0_ref, x1_ref, x2_ref, x3_ref)):
        by_group[me ^ o] = ref[...]
    hot = [by_group[g, SPAN + 32 : SPAN + 48, :].astype(F32)[0:1, :] for g in range(N_GRP)]
    a, b = iota((BLOCK, BLOCK), 0), iota((BLOCK, BLOCK), 1)
    diagonal = a == b
    lane = iota((16, D), 1)
    scale_row = jnp.zeros((16, D), F32)
    for q in range(4):
        grad = jnp.zeros((BLOCK, D), F32)
        number = (me * 4 + q).astype(F32)
        for g in range(N_GRP):
            for j in range(2):
                block = by_group[g, j * BLOCK : (j + 1) * BLOCK, :].astype(F32)
                grad = grad + jnp.where(hot[g][:, j : j + 1] == number, block, 0.0)
        at = pl.ds(q * BLOCK, BLOCK)
        accum = jnp.broadcast_to(accum_ref[:, q * BLOCK : (q + 1) * BLOCK], (BLOCK, BLOCK))
        state = jnp.sum(jnp.where(diagonal, accum, 0.0), axis=1, keepdims=True) + jnp.mean(
            grad * grad, axis=1, keepdims=True
        )
        new_accum_ref[:, q * BLOCK : (q + 1) * BLOCK] = jnp.sum(
            jnp.where(diagonal, jnp.broadcast_to(state, (BLOCK, BLOCK)), 0.0), axis=0, keepdims=True
        )
        weights = master_ref[at, :] - grad * (LR / jnp.sqrt(state))
        new_master_ref[at, :] = weights
        largest = jnp.max(jnp.max(jnp.abs(weights), axis=0, keepdims=True), axis=1, keepdims=True)
        scale = (largest + 1e-06).astype(BF16).astype(F32)
        coded_ref[at, :] = (weights / scale).astype(BF16)
        scale_row = jnp.where(lane == me * 4 + q, scale, scale_row)
    coded_ref[pl.ds(QUARTER, 16), :] = scale_row.astype(BF16)


def fresh_kernel(s0_ref, s1_ref, s2_ref, s3_ref, serving_ref, scale_ref):
    me = group()
    scales = jnp.zeros((16, D), F32)
    for o, ref in enumerate((s0_ref, s1_ref, s2_ref, s3_ref)):
        start = pl.multiple_of((me ^ o) * QUARTER, QUARTER)
        serving_ref[pl.ds(start, QUARTER), :] = ref[0:QUARTER, :]
        scales = scales + ref[QUARTER : QUARTER + 16, :].astype(F32)
    scale_ref[...] = scales[0:1, 0:16].astype(BF16)


def last_kernel(mine_ref, other_ref, top_ref, buf, sem):
    def fill(i):
        half = slice(i // 2 * 16, i // 2 * 16 + 16)
        for ref, core in ((mine_ref, own_core()), (other_ref, 1 - own_core())):
            for s in range(16):
                column = pl.multiple_of((s % 4 * 2 + core) * 128, 128)
                line = s // 4 * 16
                buf[i, line : line + 16, pl.ds(column, 128)] = ref[
                    i % 2 * 16 + s, half, :
                ].astype(F32)

    store_quarters(fill, top_ref, buf, sem)


def like(shape, dtype):
    return jax.ShapeDtypeStruct(shape, dtype)


def over_groups(x):
    parts = [x]
    for o in (1, 2, 3):
        parts.append(lax.ppermute(x, "grp", [(g, g ^ o) for g in range(N_GRP)]))
    return parts


def other_core(x):
    return lax.ppermute(x, "row_2", [(0, 1), (1, 0)])


def exchange(x, axes=ROW):
    return lax.all_to_all(x, axes, 0, 0, tiled=True)


def on_device(
    serving, serving_scale, hot_blocks, bag_lengths, bag_indices, dense_act, labels, w_top, w_out, master, accum,
):
    (ids,) = call(ids_kernel, [like((N_ROW, D), I32)], [VM], (bag_indices,), 1 << 26)
    wanted = exchange(ids.reshape(N_ROW // 2, 2, D), CHIPS).reshape(N_ROW, D)
    use, use_t = call(
        counts_kernel,
        [like((BAGS, SLOTS), BF16), like((SLOTS, BAGS), BF16)],
        [VM] * 2,
        (bag_indices, bag_lengths),
        1 << 29,
    )
    (table,) = call(
        table_kernel,
        [like((SPAN, D), BF16)],
        [SM, pl.BlockSpec(memory_space=pl.ANY), VM],
        (hot_blocks, serving, serving_scale.reshape(1, 16)),
        1 << 20,
        [pltpu.VMEM((2, BLOCK, D), BF16), pltpu.SemaphoreType.DMA((2,))],
    )
    pre, labels_column, w_out_line = call(
        dense_kernel,
        [like((BAGS, FF), F32), like((BAGS, D), F32), like((1, FF), F32)],
        [VM] * 4,
        (dense_act, w_top, labels.reshape(1, BAGS), w_out.reshape(1, FF)),
        1 << 27,
    )
    other_table = other_core(table)
    wanted, table, other_table, pre, labels_column, w_out_line = lax.optimization_barrier(
        (wanted, table, other_table, pre, labels_column, w_out_line)
    )
    (rows,) = call(
        pick_kernel, [like((SLOTS, D), BF16)], [VM] * 3, (wanted, table, other_table), 1 << 26
    )
    fetched = exchange(rows.reshape(N_ROW // 2, 2 * CAP, D), CHIPS).reshape(SLOTS, D)
    other_wanted = other_core(wanted)
    place, hot_lines = call(
        place_kernel,
        [like((SPAN, SLOTS), BF16), like((16, D), BF16)],
        [SM] + [VM] * 2,
        (hot_blocks, wanted, other_wanted),
        1 << 26,
    )
    give, keep, dpre = call(
        step_kernel,
        [like((N_ROW, 16, D), BF16), like((BAGS, D), BF16), like((BAGS, FF), BF16)],
        [VM] * 7,
        (fetched, use, dense_act, pre, labels_column, w_top, w_out_line),
        1 << 29,
    )
    given = other_core(give)
    kept, row_grad = call(
        rest_kernel,
        [like((N_ROW, 16, D), F32), like((SLOTS, D), BF16)],
        [VM] * 4,
        (keep, dpre, w_top, use_t),
        1 << 28,
    )
    (parts,) = call(
        parts_kernel,
        [like((N_ROW, 24, D), BF16)],
        [VM] * 3,
        (kept, given, row_grad.reshape(N_ROW, CAP, D)),
        1 << 20,
        quarters_of((N_ROW, 24, D), BF16),
        [ANY],
    )
    got = exchange(parts)
    (own,) = call(
        owned_kernel,
        [like((SPAN + 48, D), BF16)],
        [VM] * 3,
        (got.reshape(N_ROW // 2, 2, 24, D), place, hot_lines),
        1 << 26,
    )
    owned = over_groups(own)
    (top_part,) = call(
        top_kernel,
        [like((N_ROW // 2, 32, D), BF16)],
        [VM] * 4,
        tuple(owned),
        1 << 16,
        [pltpu.VMEM((N_GRP, 32, D), BF16)],
    )
    top_mine = exchange(top_part, CHIPS)
    new_master, new_accum, coded = call(
        update_kernel,
        [like((QUARTER, D), F32), like((1, QUARTER), F32), like((QUARTER + 16, D), BF16)],
        [VM] * 6,
        (*owned, master[0], accum),
        1 << 22,
        [pltpu.VMEM((N_GRP, SPAN + 48, D), BF16)],
    )
    quarters = over_groups(coded)
    fresh, fresh_scale = call(
        fresh_kernel,
        [like((4 * QUARTER, D), BF16), like((1, 16), BF16)],
        [VM] * 4,
        tuple(quarters),
        1 << 20,
    )
    top_other = other_core(top_mine)
    (top_grad,) = call(
        last_kernel,
        [like((2 * D, FF), F32)],
        [VM] * 2,
        (top_mine, top_other),
        1 << 20,
        quarters_of((2 * D, FF), F32),
        [ANY],
    )
    return new_master[None], new_accum, fresh, fresh_scale.reshape(16), top_grad


def solution(mesh):
    finer = Mesh(
        mesh.devices.reshape(mesh.shape["grp"], 4, 8, 2), ("grp", "row_0", "row_1", "row_2")
    )
    in_specs = (
        P(ROW, None),
        P(ROW),
        P("grp", ROW),
        P(GRP_ROW, None),
        P(GRP_ROW, None),
        P(GRP_ROW, None),
        P(GRP_ROW),
        P(),
        P(),
        P("grp", ROW, None),
        P("grp", ROW),
    )
    out_specs = (P("grp", ROW, None), P("grp", ROW), P(ROW, None), P(ROW), P())
    return jax.shard_map(
        on_device, mesh=finer, in_specs=in_specs, out_specs=out_specs, check_vma=False
    )
```
